32 devices in a mesh: rows: 16 (over z, y, core), heads: 2 (over x).
Axes of the slice: x: 2, y: 2, z: 4, core: 2. Of those that a mesh axis runs over, the one named last changes fastest.
Arguments:
- features: bfloat16 [8192, 1664], P(('rows', 'heads')), may hold values from -6 to 6
- segment_ids: int32 [8192], P(('rows', 'heads')), may hold values from 0 to 1, as said below
- padding_mask: int32 [8192], P(('rows', 'heads')), may hold values from 0 to 1, as said below
- w_proj: bfloat16 [1664, 1024], replicated, may hold values from -0.15625 to 0.15625
- proj_bias: float32 [1024], replicated, may hold values from -3 to 3
- gain_attn: float32 [1024], replicated, may hold values from 0.1 to 1.9
- w_qkv: bfloat16 [1024, 3, 1024], P(None, None, 'heads'), may hold values from -0.09375 to 0.09375
- w_out: bfloat16 [1024, 1024], P('heads'), may hold values from -3 to 3
- gain_ffn: float32 [1024], replicated, may hold values from 0.1 to 1.9
- w_gate_up: bfloat16 [1024, 2, 2816], P(None, None, 'heads'), may hold values from -0.1875 to 0.1875
- w_down: bfloat16 [2816, 1024], P('heads'), may hold values from -0.109375 to 0.109375
- cotangent: bfloat16 [8192, 1024], P(('rows', 'heads')), may hold values from -6 to 6
Outputs:
- layer_out: bfloat16 [8192, 1024], P(('rows', 'heads'))
- grad_features: float32 [8192, 1664], P(('rows', 'heads'))
- grad_proj: float32 [1664, 1024], replicated
- grad_bias: float32 [1024], replicated
- grad_gain_attn: float32 [1024], replicated
- grad_qkv: float32 [1024, 3, 1024], P(None, None, 'heads')
- grad_out: float32 [1024, 1024], P('heads')
- grad_gain_ffn: float32 [1024], replicated
- grad_gate_up: float32 [1024, 2, 2816], P(None, None, 'heads')
- grad_down: float32 [2816, 1024], P('heads')
The draws below stay inside these ranges and needn't reach their ends.
Inputs may be any that keep to these rules, and one draw needn't show every extreme that they name: `segment_ids`: within each aligned block of 512 tokens (one packed row) the ids start at 0 and never fall; each pair holds 256 patches followed by its text, and the padding at a row's end has one id of its own. `padding_mask`: in each packed row the ones form a leading run that ends where the row's last whole pair ends; the rest is 0.
All inputs are finite; a program needn't handle non-finite values.
Results may differ from the reference program's by a relative error of at most 0.024.
Values may be sent and summed in bfloat16 or wider, within the bound.
No kernel may reach another device: no remote copies, remote signals or barrier semaphores. Data moves between devices by JAX's collectives and lax.ppermute only.
A program may use at most 128 MiB of HBM per device.

```python
from functools import partial
import jax
import jax.numpy as jnp
from jax import lax

D = 1024
HEADS = 16
HEAD_DIM = 64
FF = 2816
FEAT = 1664
PATCHES = 256
TEXT_MIN = 16
TEXT_MAX = 128
SEQ_LEN = 512
TOKENS = 8192


def packed_rows(key):
    inner = jax.random.fold_in(key, 11)
    row_count = TOKENS // SEQ_LEN
    pair_count = SEQ_LEN // PATCHES + 1
    text_lengths = jax.random.randint(inner, (row_count, pair_count), TEXT_MIN, TEXT_MAX + 1)
    first_row = (jnp.arange(row_count) == 0)[:, None]
    text_lengths = jnp.where(first_row, TEXT_MIN, text_lengths).astype(jnp.int32)
    pair_ends = jnp.cumsum(PATCHES + text_lengths, axis=1)
    places = jnp.arange(SEQ_LEN)
    segment = jnp.sum((pair_ends[:, None, :] <= places[None, :, None]).astype(jnp.int32), axis=2)
    used_end = jnp.max(jnp.where(pair_ends <= SEQ_LEN, pair_ends, 0), axis=1)
    real_tokens = (places[None, :] < used_end[:, None]).astype(jnp.int32)
    return (segment.reshape(TOKENS).astype(jnp.int32), real_tokens.reshape(TOKENS))


def draw_segment_ids(key, part):
    return packed_rows(key)[0]


def draw_padding_mask(key, part):
    return packed_rows(key)[1]


def block_levels(own_key, dims, cuts, low, largest):
    def one(dim, parts):
        heights = jax.random.uniform(jax.random.fold_in(jax.random.fold_in(own_key, 6), dim), (parts,), jnp.float32, low / len(cuts), largest / len(cuts))
        return jnp.repeat(jnp.exp(heights), dims[dim] // parts).reshape((-1,) + (1,) * (len(dims) - dim - 1))

    level = one(*cuts[0])
    for cut in cuts[1:]:
        level = level * one(*cut)
    return level


def centred(rng, shape, spread, limit, shards=(), dtype=jnp.bfloat16):
    values = jax.random.normal(rng, shape, jnp.float32) * spread
    if len(shards) > 0:
        values = block_levels(rng, shape, shards, -0.22, 0.18) * values
    return jnp.clip(values, min=-limit, max=limit).astype(dtype)


def setup_inputs(seed: int = 0) -> dict:
    key_list = jax.random.split(jax.random.key(seed), 13)
    return {
        "features": centred(key_list[0], (TOKENS, FEAT), 1.0, 6.0, ((0, 32),)),
        "segment_ids": draw_segment_ids(jax.random.fold_in(key_list[12], 71), 0),
        "padding_mask": draw_padding_mask(jax.random.fold_in(key_list[12], 71), 0),
        "w_proj": centred(key_list[3], (FEAT, D), FEAT ** -0.5, 0.15625),
        "proj_bias": centred(key_list[4], (D,), 0.5, 3.0, (), jnp.float32),
        "gain_attn": jnp.clip(1.0 + 0.18 * jax.random.normal(key_list[5], (D,), jnp.float32), 0.1, 1.9),
        "w_qkv": centred(key_list[6], (D, 3, D), (4 * D) ** -0.5, 0.09375, ((2, 2),)),
        "w_out": centred(key_list[7], (D, D), (max(4, D // 256)) ** -0.5, 3.0, ((0, 2),)),
        "gain_ffn": jnp.clip(1.0 + 0.18 * jax.random.normal(key_list[8], (D,), jnp.float32), 0.1, 1.9),
        "w_gate_up": centred(key_list[9], (D, 2, FF), D ** -0.5, 0.1875, ((2, 2),)),
        "w_down": centred(key_list[10], (FF, D), FF ** -0.5, 0.109375, ((0, 2),)),
        "cotangent": centred(key_list[11], (TOKENS, D), 1.0, 6.0, ((0, 32),)),
    }


@jax.custom_vjp
def low(v):
    return lax.optimization_barrier(v.astype(jnp.bfloat16)).astype(jnp.float32)

@jax.custom_vjp
def low_back(v):
    return v

def low_keep(v):
    return (low(v), None)

def low_pass(kept, grad):
    return (grad,)

def back_keep(v):
    return (v, None)

def back_low(kept, grad):
    return (low(grad),)
low.defvjp(low_keep, low_pass)
low_back.defvjp(back_keep, back_low)
EPSILON = 1e-06
MASKED = -1000000000.0
HIGHEST = lax.Precision.HIGHEST

def product(left, right):
    return jnp.dot(left, right, precision=HIGHEST, preferred_element_type=jnp.float32)

def rms_norm(values, gain):
    return values * lax.rsqrt(lax.optimization_barrier(jnp.mean(values * values, axis=-1, keepdims=True)) + EPSILON) * gain

def attend_row(queries, key_rows, value_rows, segment_row, padding_row):
    scores = low_back(jnp.einsum('qhd,khd->hqk', queries, key_rows, precision=HIGHEST))
    places = jnp.arange(SEQ_LEN)
    allowed = (segment_row[:, None] == segment_row[None, :]) & ((padding_row[None, :] == 1) | (places[:, None] == places[None, :]))
    scores = jnp.where(allowed[None], scores, MASKED)
    top = lax.optimization_barrier(jnp.max(scores, axis=-1, keepdims=True))
    expo = jnp.exp(scores - top)
    probs = low(expo / lax.optimization_barrier(jnp.sum(expo, axis=-1, keepdims=True)))
    return jnp.einsum('hqk,khd->qhd', probs, value_rows, precision=HIGHEST)

def layer_forward(segment_ids, padding_mask, features, w_proj, proj_bias, gain_attn, w_qkv, w_out, gain_ffn, w_gate_up, w_down):
    lifted = low_back(product(features, w_proj)) + proj_bias
    normed = low(rms_norm(lifted, gain_attn))
    projected = low(low_back(product(normed, w_qkv.reshape(D, 3 * D))))
    projected = projected.reshape(TOKENS // SEQ_LEN, SEQ_LEN, 3, HEADS, HEAD_DIM)
    segment_rows = segment_ids.reshape(TOKENS // SEQ_LEN, SEQ_LEN)
    padding_rows = padding_mask.reshape(TOKENS // SEQ_LEN, SEQ_LEN)
    checked = jax.checkpoint(attend_row)

    def per_row(carry, item):
        return (carry, checked(item[0], item[1], item[2], item[3], item[4]))
    _, mixed = lax.scan(per_row, jnp.zeros((), jnp.float32), (projected[:, :, 0], projected[:, :, 1], projected[:, :, 2], segment_rows, padding_rows))
    mixed = low(low_back(mixed.reshape(TOKENS, D)))
    middle = lifted + low_back(product(mixed, w_out))
    normed_ffn = low(rms_norm(middle, gain_ffn))
    gate_up = low_back(product(normed_ffn, w_gate_up.reshape(D, 2 * FF)))
    hidden = low(jax.nn.gelu(gate_up[:, :FF], approximate=True) * gate_up[:, FF:])
    return middle + low_back(product(hidden, w_down))

def reference(features, segment_ids, padding_mask, w_proj, proj_bias, gain_attn, w_qkv, w_out, gain_ffn, w_gate_up, w_down, cotangent):
    floats = tuple((array_in.astype(jnp.float32) for array_in in (features, w_proj, proj_bias, gain_attn, w_qkv, w_out, gain_ffn, w_gate_up, w_down)))
    output, pull = jax.vjp(partial(layer_forward, segment_ids, padding_mask), *floats)
    grads = pull(cotangent.astype(jnp.float32))
    return (output.astype(jnp.bfloat16), grads[0], grads[1], grads[2], grads[3], grads[4], grads[5], grads[6], grads[7], grads[8])
```

```python
import jax
import jax.numpy as jnp
from jax import lax
from jax.sharding import PartitionSpec as P

HEAD_DIM = 64
LEN_MAX = 2048


EPSILON = 1e-06
MASKED = -1000000000.0


def gelu_tanh(values):
    return jax.nn.gelu(values, approximate=True)


def contract(left, right, left_dim, right_dim):
    return lax.dot_general(
        left, right, (((left_dim,), (right_dim,)), ((), ())), preferred_element_type=jnp.float32
    )


def swap_rows(value, masks):
    count = lax.axis_size("rows")
    return lax.ppermute(value, "rows", [(r, r ^ masks[r % 2]) for r in range(count)])


def core_swap(value):
    return swap_rows(value, (1, 1))


def peer_swap(value):
    return lax.ppermute(value, "heads", [(0, 1), (1, 0)])


def gather_group(value):
    if lax.axis_size("heads") == 2:
        return jnp.concatenate([value, peer_swap(value)], axis=0)
    return lax.all_gather(value, "heads", axis=0, tiled=True)


def scatter_group(value):
    if lax.axis_size("heads") == 2:
        mine = value.shape[0] // 2
        return value[:mine].astype(jnp.float32) + peer_swap(value[mine:]).astype(jnp.float32)
    return lax.psum_scatter(value, "heads", scatter_dimension=0, tiled=True).astype(jnp.float32)


def columns_to_group(value):
    size = lax.axis_size("heads")
    if size == 2:
        width = value.shape[1] // 2
        place = lax.axis_index("heads")
        mine = lax.dynamic_slice_in_dim(value, place * width, width, 1)
        theirs = lax.dynamic_slice_in_dim(value, (1 - place) * width, width, 1)
        return jnp.concatenate([mine, peer_swap(theirs)], axis=0)
    return lax.all_to_all(value, "heads", 1, 0, tiled=True)


def columns_to_pair(value, axis=1):
    width = value.shape[axis] // 2
    core = lax.axis_index("rows") % 2
    mine = lax.dynamic_slice_in_dim(value, core * width, width, axis)
    theirs = lax.dynamic_slice_in_dim(value, (1 - core) * width, width, axis)
    return jnp.concatenate([mine, core_swap(theirs)], axis=0)


def with_pair(value):
    return jnp.concatenate([value, core_swap(value)], axis=0)


def plane_steps():
    bits = (lax.axis_size("rows") // 2).bit_length() - 1
    low = bits // 2

    def line(first, count):
        return [
            ((1 << first, (first,) if count == 1 else (first, first + 1)))
        ] if count == 1 else [
            (1 << first, (first, first + 1)),
            (3 << first, (first + 1,)),
        ]

    near = line(1, low)
    far = line(1 + low, bits - low)

    def weave(one, two):
        one, two, order = list(one), list(two), []
        while one or two:
            if one:
                order.append(one.pop(0))
            if two:
                order.append(two.pop(0))
        return order

    return list(zip(weave(near, far), weave(far, near)))


def side(step):
    index = lax.axis_index("rows")

    def parity(places):
        total = jnp.zeros((), jnp.int32)
        for place in places:
            total = total ^ ((index >> place) & 1)
        return total

    return jnp.where(index % 2 == 0, parity(step[0][1]), parity(step[1][1]))


def plane_sum(value):
    steps = plane_steps()
    for step in steps:
        half = value.shape[0] // 2
        place = side(step)
        keep = lax.dynamic_slice_in_dim(value, place * half, half, 0)
        send = lax.dynamic_slice_in_dim(value, (1 - place) * half, half, 0)
        got = swap_rows(send, (step[0][0], step[1][0]))
        value = (keep.astype(jnp.float32) + got.astype(jnp.float32)).astype(jnp.bfloat16)
    for step in reversed(steps):
        got = swap_rows(value, (step[0][0], step[1][0]))
        value = jnp.where(
            side(step) == 0,
            jnp.concatenate([value, got], axis=0),
            jnp.concatenate([got, value], axis=0),
        )
    return value


def pair_columns(value, axis):
    other = core_swap(value)
    core = lax.axis_index("rows") % 2
    return jnp.where(
        core == 0,
        jnp.concatenate([value, other], axis=axis),
        jnp.concatenate([other, value], axis=axis),
    )


def small_sum(value):
    count = lax.axis_size("rows")
    mask = 1
    while mask < count:
        value = value + swap_rows(value, (mask, mask))
        mask *= 2
    if lax.axis_size("heads") == 2:
        return value + peer_swap(value)
    return lax.psum(value, "heads")


def rms_forward(values, gain):
    scale = lax.rsqrt(jnp.mean(values * values, axis=-1, keepdims=True) + EPSILON)
    return (values * scale * gain, scale)


def rms_backward(values, scale, gain, grad_normed):
    unit = values * scale
    grad_unit = grad_normed * gain
    grad_values = scale * (grad_unit - unit * jnp.mean(grad_unit * unit, axis=-1, keepdims=True))
    return (grad_values, jnp.sum(grad_normed * unit, axis=0))


def block_scores(
    queries, key_rows, segments, padding, query_start, row_start, query_count, seq_len
):
    query_block = lax.dynamic_slice_in_dim(queries, query_start, query_count, 0)
    scores = jnp.einsum("qhd,khd->hqk", query_block, key_rows, preferred_element_type=jnp.float32)
    query_segment = lax.dynamic_slice_in_dim(segments, query_start, query_count, 0)
    query_place = query_start + jnp.arange(query_count)
    key_place = row_start + jnp.arange(seq_len)
    allowed = (query_segment[:, None] == segments[None, :]) & (
        (padding[None, :] == 1) | (query_place[:, None] == key_place[None, :])
    )
    return (jnp.where(allowed[None], scores, MASKED), query_block, key_rows)


def attention_forward(queries, key_rows, value_rows, segments, padding, seq_len, query_count):
    group_tokens = queries.shape[0]
    per_seq = seq_len // query_count

    def one_block(number):
        query_start = number * query_count
        row_start = number // per_seq * seq_len
        scores, _, _ = block_scores(
            queries, key_rows, segments, padding, query_start, row_start, query_count, seq_len
        )
        top = jnp.max(scores, axis=-1, keepdims=True)
        expo = jnp.exp(scores - top)
        weight_sum = jnp.sum(expo, axis=-1, keepdims=True)
        probs = (expo / weight_sum).astype(jnp.bfloat16)
        mixed = jnp.einsum("hqk,khd->qhd", probs, value_rows, preferred_element_type=jnp.float32)
        return (mixed.astype(jnp.bfloat16), (top + jnp.log(weight_sum))[:, :, 0])

    mixed, log_sums = lax.map(one_block, jnp.arange(group_tokens // query_count))
    return (mixed.reshape(group_tokens, -1), log_sums)


def attention_backward(
    queries, key_rows, value_rows, segments, padding, log_sums, grad_mixed, seq_len, query_count
):
    group_tokens, heads_here, head_size = queries.shape
    per_seq = seq_len // query_count

    def one_block(carry, item):
        grad_keys, grad_values = carry
        number, log_sum = item
        query_start = number * query_count
        row_start = number // per_seq * seq_len
        scores, query_block, key_block = block_scores(
            queries, key_rows, segments, padding, query_start, row_start, query_count, seq_len
        )
        grad_block = lax.dynamic_slice_in_dim(grad_mixed, query_start, query_count, 0)
        probs = jnp.exp(scores - log_sum[:, :, None])
        grad_probs = jnp.einsum(
            "qhd,khd->hqk", grad_block, value_rows, preferred_element_type=jnp.float32
        )
        grad_scores = probs * (grad_probs - jnp.sum(grad_probs * probs, axis=-1, keepdims=True))
        grad_scores = grad_scores.astype(jnp.bfloat16)
        grad_query = jnp.einsum(
            "hqk,khd->qhd", grad_scores, key_block, preferred_element_type=jnp.float32
        )
        key_part = jnp.einsum(
            "hqk,qhd->khd", grad_scores, query_block, preferred_element_type=jnp.float32
        )
        value_part = jnp.einsum(
            "hqk,qhd->khd",
            probs.astype(jnp.bfloat16),
            grad_block,
            preferred_element_type=jnp.float32,
        )
        grad_keys = grad_keys + key_part
        grad_values = grad_values + value_part
        return ((grad_keys, grad_values), grad_query)

    zero_grads = jnp.zeros((group_tokens, heads_here, head_size), jnp.float32)
    (grad_keys, grad_values), grad_queries = lax.scan(
        one_block, (zero_grads, zero_grads), (jnp.arange(group_tokens // query_count), log_sums)
    )
    return (grad_queries.reshape(group_tokens, heads_here, head_size), grad_keys, grad_values)


def local(
    features,
    segment_ids,
    padding_mask,
    w_proj,
    proj_bias,
    gain_attn,
    w_qkv,
    w_out,
    gain_ffn,
    w_gate_up,
    w_down,
    cotangent,
):
    local_tokens = features.shape[0]
    model_width = w_proj.shape[1]
    attn_cols = w_qkv.shape[2]
    heads_here = attn_cols // HEAD_DIM
    group_tokens = local_tokens * lax.axis_size("heads")
    seq_len = min(LEN_MAX, group_tokens)
    query_count = min(512, seq_len)
    ff_here = w_gate_up.shape[2]
    core = lax.axis_index("rows") % 2
    qkv_flat = w_qkv.reshape(model_width, 3 * attn_cols)
    lifted = jnp.dot(features, w_proj, preferred_element_type=jnp.float32) + proj_bias
    normed, scale_attn = rms_forward(lifted, gain_attn)
    gathered = gather_group(normed.astype(jnp.bfloat16))
    segments = gather_group(segment_ids)
    padding = gather_group(padding_mask)
    projected = jnp.dot(gathered, qkv_flat, preferred_element_type=jnp.float32).astype(jnp.bfloat16)
    projected = projected.reshape(group_tokens, 3, heads_here, HEAD_DIM)
    queries, key_rows, value_rows = (projected[:, 0], projected[:, 1], projected[:, 2])
    mixed, log_sums = attention_forward(
        queries, key_rows, value_rows, segments, padding, seq_len, query_count
    )
    middle = lifted + scatter_group(
        jnp.dot(mixed, w_out, preferred_element_type=jnp.float32).astype(jnp.bfloat16)
    )
    normed_ffn, scale_ffn = rms_forward(middle, gain_ffn)
    gathered_ffn = gather_group(normed_ffn.astype(jnp.bfloat16))
    gate_flat = w_gate_up.reshape(model_width, 2 * ff_here)
    gate_up = jnp.dot(gathered_ffn, gate_flat, preferred_element_type=jnp.float32)
    activ, gelu_pull = jax.vjp(gelu_tanh, gate_up[:, :ff_here])
    up_part = gate_up[:, ff_here:]
    hidden = (activ * up_part).astype(jnp.bfloat16)
    layer_out = middle + scatter_group(
        jnp.dot(hidden, w_down, preferred_element_type=jnp.float32).astype(jnp.bfloat16)
    )
    grad_gathered = gather_group(cotangent)
    grad_hidden = contract(grad_gathered, w_down, 1, 1)
    grad_gate = gelu_pull(grad_hidden * up_part)[0].astype(jnp.bfloat16)
    grad_up = (grad_hidden * activ).astype(jnp.bfloat16)
    pair_hidden = with_pair(hidden)
    pair_cot = columns_to_pair(grad_gathered)
    down_part = contract(pair_hidden, pair_cot, 0, 0).astype(jnp.bfloat16)
    pair_ffn = with_pair(gathered_ffn)
    pre_own = jnp.where(core == 0, grad_gate, grad_up)
    pre_other = core_swap(jnp.where(core == 0, grad_up, grad_gate))
    gate_part = contract(pair_ffn, jnp.concatenate([pre_own, pre_other], axis=0), 0, 0).astype(
        jnp.bfloat16
    )
    grad_down = pair_columns(plane_sum(down_part), 1).astype(jnp.float32)
    gate_sum = plane_sum(gate_part)
    grad_gate_up = pair_columns(gate_sum[:, None, :], 1).astype(jnp.float32)
    grad_pre = jnp.concatenate([grad_gate, grad_up], axis=1)
    grad_normed_ffn = scatter_group(contract(grad_pre, gate_flat, 1, 1).astype(jnp.bfloat16))
    grad_ffn_norm, grad_gain_ffn = rms_backward(middle, scale_ffn, gain_ffn, grad_normed_ffn)
    grad_middle = cotangent.astype(jnp.float32) + grad_ffn_norm
    grad_mid_b = grad_middle.astype(jnp.bfloat16)
    grad_attn_in = gather_group(grad_mid_b)
    grad_mixed = contract(grad_attn_in, w_out, 1, 1).astype(jnp.bfloat16)
    out_part = contract(with_pair(mixed), columns_to_pair(grad_attn_in), 0, 0).astype(jnp.bfloat16)
    grad_out = pair_columns(plane_sum(out_part), 1).astype(jnp.float32)
    grad_queries, grad_keys, grad_values = attention_backward(
        queries,
        key_rows,
        value_rows,
        segments,
        padding,
        log_sums,
        grad_mixed.reshape(group_tokens, heads_here, HEAD_DIM),
        seq_len,
        query_count,
    )
    grad_heads = jnp.stack([grad_queries, grad_keys, grad_values], axis=1).astype(jnp.bfloat16)
    grad_flat = grad_heads.reshape(group_tokens, 3 * attn_cols)
    pair_heads = columns_to_pair(grad_heads.reshape(group_tokens, 3, attn_cols), 2)
    qkv_part = contract(
        with_pair(gathered), pair_heads.reshape(2 * group_tokens, -1), 0, 0
    ).astype(jnp.bfloat16)
    qkv_sum = plane_sum(qkv_part).reshape(model_width, 3, attn_cols // 2)
    grad_qkv = pair_columns(qkv_sum, 2).astype(jnp.float32)
    grad_normed = scatter_group(contract(grad_flat, qkv_flat, 1, 1).astype(jnp.bfloat16))
    grad_attn_norm, grad_gain_attn = rms_backward(lifted, scale_attn, gain_attn, grad_normed)
    grad_lifted = grad_middle + grad_attn_norm
    grad_lift_b = grad_lifted.astype(jnp.bfloat16)
    grad_features = contract(grad_lift_b, w_proj, 1, 1)
    pair_lift = columns_to_pair(columns_to_group(grad_lift_b))
    proj_part = contract(with_pair(gather_group(features)), pair_lift, 0, 0).astype(jnp.bfloat16)
    proj_half = pair_columns(plane_sum(proj_part), 1)
    if lax.axis_size("heads") == 2:
        other = peer_swap(proj_half)
        grad_proj = jnp.where(
            lax.axis_index("heads") == 0,
            jnp.concatenate([proj_half, other], axis=1),
            jnp.concatenate([other, proj_half], axis=1),
        ).astype(jnp.float32)
    else:
        grad_proj = lax.all_gather(proj_half, "heads", axis=1, tiled=True).astype(jnp.float32)
    sums = small_sum(jnp.stack([jnp.sum(grad_lifted, axis=0), grad_gain_attn, grad_gain_ffn]))
    return (
        layer_out.astype(jnp.bfloat16),
        grad_features,
        grad_proj,
        sums[0],
        sums[1],
        grad_qkv,
        grad_out,
        sums[2],
        grad_gate_up,
        grad_down,
    )


def solution(mesh):
    in_specs = (
        P(("rows", "heads"), None),
        P(("rows", "heads")),
        P(("rows", "heads")),
        P(),
        P(),
        P(),
        P(None, None, "heads"),
        P("heads", None),
        P(),
        P(None, None, "heads"),
        P("heads", None),
        P(("rows", "heads"), None),
    )
    out_specs = (
        P(("rows", "heads"), None),
        P(("rows", "heads"), None),
        P(),
        P(),
        P(),
        P(None, None, "heads"),
        P("heads", None),
        P(),
        P(None, None, "heads"),
        P("heads", None),
    )
    return jax.shard_map(local, mesh=mesh, in_specs=in_specs, out_specs=out_specs, check_vma=False)
```

```python
import jax
import jax.numpy as jnp
from jax import lax
from jax.experimental import pallas as pl
from jax.experimental.pallas import tpu as pltpu
from jax.sharding import PartitionSpec as P

HEAD_DIM = 64


EPSILON = 1e-06
MASKED = -1000000000.0


def gelu_tanh(values):
    return jax.nn.gelu(values, approximate=True)


def contract(left, right, left_dim, right_dim):
    return lax.dot_general(
        left, right, (((left_dim,), (right_dim,)), ((), ())), preferred_element_type=jnp.float32
    )


def swap_rows(value, masks):
    count = lax.axis_size("rows")
    return lax.ppermute(value, "rows", [(r, r ^ masks[r % 2]) for r in range(count)])


def core_swap(value):
    return swap_rows(value, (1, 1))


def peer_swap(value):
    return lax.ppermute(value, "heads", [(0, 1), (1, 0)])


def gather_group(value):
    if lax.axis_size("heads") == 2:
        return jnp.concatenate([value, peer_swap(value)], axis=0)
    return lax.all_gather(value, "heads", axis=0, tiled=True)


def scatter_group(value):
    if lax.axis_size("heads") == 2:
        mine = value.shape[0] // 2
        return value[:mine].astype(jnp.float32) + peer_swap(value[mine:]).astype(jnp.float32)
    return lax.psum_scatter(value, "heads", scatter_dimension=0, tiled=True).astype(jnp.float32)


def to_owners(product, left):
    if lax.axis_size("heads") == 2:
        mine = left.shape[0] // 2
        given = peer_swap(product(left[mine:]).astype(jnp.bfloat16))
        return (given, product(left[:mine]))
    given = lax.psum_scatter(
        product(left).astype(jnp.bfloat16), "heads", scatter_dimension=0, tiled=True
    )
    return (given, jnp.zeros((), jnp.float32))


def columns_to_group(value):
    size = lax.axis_size("heads")
    if size == 2:
        width = value.shape[1] // 2
        place = lax.axis_index("heads")
        mine = lax.dynamic_slice_in_dim(value, place * width, width, 1)
        theirs = lax.dynamic_slice_in_dim(value, (1 - place) * width, width, 1)
        return jnp.concatenate([mine, peer_swap(theirs)], axis=0)
    return lax.all_to_all(value, "heads", 1, 0, tiled=True)


def columns_to_pair(value, axis=1):
    width = value.shape[axis] // 2
    core = lax.axis_index("rows") % 2
    mine = lax.dynamic_slice_in_dim(value, core * width, width, axis)
    theirs = lax.dynamic_slice_in_dim(value, (1 - core) * width, width, axis)
    return jnp.concatenate([mine, core_swap(theirs)], axis=0)


def mixed_columns_to_pair(value, pieces):
    width = value.shape[1] // (2 * pieces)
    core = lax.axis_index("rows") % 2
    mine, theirs = (
        jnp.concatenate(
            [
                lax.dynamic_slice_in_dim(value, (2 * k + which) * width, width, 1)
                for k in range(pieces)
            ],
            axis=1,
        )
        for which in (core, 1 - core)
    )
    return jnp.concatenate([mine, core_swap(theirs)], axis=0)


def with_pair(value):
    return jnp.concatenate([value, core_swap(value)], axis=0)


def plane_steps(same=False):
    bits = (lax.axis_size("rows") // 2).bit_length() - 1
    low = bits // 2

    def line(first, count):
        return [
            ((1 << first, (first,) if count == 1 else (first, first + 1)))
        ] if count == 1 else [
            (1 << first, (first, first + 1)),
            (3 << first, (first + 1,)),
        ]

    near = line(1, low)
    far = line(1 + low, bits - low)

    def weave(one, two):
        one, two, order = list(one), list(two), []
        while one or two:
            if one:
                order.append(one.pop(0))
            if two:
                order.append(two.pop(0))
        return order

    first = weave(near, far)
    return list(zip(first, first if same else weave(far, near)))


def side(step, index=None):
    index = lax.axis_index("rows") if index is None else index

    def parity(places):
        total = jnp.zeros((), jnp.int32)
        for place in places:
            total = total ^ ((index >> place) & 1)
        return total

    return jnp.where(index % 2 == 0, parity(step[0][1]), parity(step[1][1]))


def block_place(steps, index):
    place = jnp.zeros((), jnp.int32)
    for step in steps:
        place = place * 2 + side(step, index)
    return place


class Summing:
    def __init__(self, steps, value, send=None):
        self.steps, self.done = steps, 0
        self.sides = [side(step) for step in steps]
        self.size = value.shape[0] if send is None else 2 * value.shape[0]
        self.terms, self.send = [(value, jnp.zeros((), jnp.int32))], send
        self.pieces, self.others = [], []

    def last(self):
        return self.pieces[-1] if self.pieces else self.terms[-1][0]

    def update(self, value):
        if self.pieces:
            self.pieces = self.pieces[:-1] + [value]
        else:
            self.terms = self.terms[:-1] + [(value, self.terms[-1][1])]

    def masks(self, number):
        step = self.steps[number]
        return (step[0][0], step[1][0])

    def part(self, offset, size):
        total = sum(
            lax.dynamic_slice_in_dim(term, base + offset, size, 0).astype(jnp.float32)
            for term, base in self.terms
        )
        return total.astype(jnp.bfloat16)

    def step(self):
        count = len(self.steps)
        if self.done < count:
            place, half = self.sides[self.done], self.size // 2
            if self.send is None:
                send = self.part((1 - place) * half, half)
                self.terms = [(term, base + place * half) for term, base in self.terms]
            else:
                send, self.send = self.send, None
            got = swap_rows(send, self.masks(self.done))
            self.terms = self.terms + [(got, jnp.zeros((), jnp.int32))]
            self.size = half
        else:
            number = 2 * count - 1 - self.done
            if self.done == count:
                self.pieces, self.terms = [self.part(0, self.size)], []
            elif number > 0:
                self.pieces = [jnp.concatenate(self.pieces, axis=0)]
            if number > 0:
                self.pieces = self.pieces + [swap_rows(self.pieces[0], self.masks(number))]
                if number == 1:
                    self.others = [swap_rows(self.pieces[0], self.masks(0))]
            else:
                self.pieces = self.pieces + [
                    self.others[0],
                    swap_rows(self.pieces[1], self.masks(0)),
                ]
                self.others = []
        self.done += 1

    def peers(self):
        own = self.part(0, self.size)
        if lax.axis_size("heads") == 2:
            total = own.astype(jnp.float32) + peer_swap(own).astype(jnp.float32)
        else:
            total = lax.psum(own.astype(jnp.float32), "heads")
        self.terms = [(total.astype(jnp.bfloat16), jnp.zeros((), jnp.int32))]

    def cores(self):
        self.others = [core_swap(piece) for piece in self.pieces]


class Gathering(Summing):
    def __init__(self, steps, own):
        super().__init__(steps, own)
        self.done, self.size = len(steps), 1


def tie_sums(*sums_and_others):
    sums = [item for item in sums_and_others if isinstance(item, Summing)]
    others = [item for item in sums_and_others if not isinstance(item, Summing)]
    values, others = lax.optimization_barrier(([item.last() for item in sums], others))
    for item, value in zip(sums, values):
        item.update(value)
    return others


def ordered(pieces, place):
    value = jnp.concatenate(pieces, axis=0)
    return jnp.concatenate(
        [
            lax.dynamic_slice_in_dim(value, place ^ block, 1, 0)
            for block in range(value.shape[0])
        ],
        axis=0,
    ).reshape(-1, value.shape[2])


def two_cores(sums, places, axis, reshape=None):
    mine, theirs = ordered(sums.pieces, places[0]), ordered(sums.others, places[1])
    if reshape is not None:
        mine, theirs = (value.reshape(reshape) for value in (mine, theirs))
    return jnp.where(
        lax.axis_index("rows") % 2 == 0,
        jnp.concatenate([mine, theirs], axis=axis),
        jnp.concatenate([theirs, mine], axis=axis),
    )


def place_blocks(kernel, index, pieces, out_specs, out_shape, name):
    height, rows, width = pieces[0].shape

    def body(index, *refs):
        sources, results = refs[:8], refs[8:]
        quarter = pl.program_id(0)
        for number, source in enumerate(sources):
            own = index[number // 4]
            slot = index[2] if number < 4 else 1 - index[2]
            for core in range(2):

                @pl.when(((quarter ^ (own // height)) == number % 4) & (slot == core))
                def _(source=source, core=core, own=own):
                    kernel(index, source, own % height, core, *results)

    whole = pl.BlockSpec((height, rows, width), lambda b, i: (0, 0, 0))
    return pl.pallas_call(
        body,
        grid_spec=pltpu.PrefetchScalarGridSpec(
            num_scalar_prefetch=1, grid=(4,), in_specs=[whole] * 8, out_specs=out_specs
        ),
        out_shape=out_shape,
        cost_estimate=pl.CostEstimate(
            flops=0, bytes_accessed=48 * height * rows * width, transcendentals=0
        ),
        compiler_params=pltpu.CompilerParams(vmem_limit_bytes=26 << 20),
        name=name,
    )(index, *pieces)


def place_ffn(index, sums, split):
    height, rows, width = sums.pieces[0].shape
    columns = height * (rows - split)

    def kernel(index, source, low, core, gate_up, down):
        parts = [source[k ^ low] for k in range(height)]
        for k, part in enumerate(parts):
            gate_up[k * split : (k + 1) * split, core, :] = part[:split].astype(jnp.float32)
        value = jnp.concatenate([part[split:] for part in parts], axis=0)
        down[:, core * columns : (core + 1) * columns] = value.astype(jnp.float32).T

    return place_blocks(
        kernel,
        index,
        sums.pieces + sums.others,
        [
            pl.BlockSpec((height * split, 2, width), lambda b, i: (b, 0, 0)),
            pl.BlockSpec((width, 2 * columns), lambda b, i: (0, b)),
        ],
        [
            jax.ShapeDtypeStruct((4 * height * split, 2, width), jnp.float32),
            jax.ShapeDtypeStruct((width, 8 * columns), jnp.float32),
        ],
        "place_ffn",
    )


def place_attn(index, sums, attn_cols):
    height, rows, width = sums.pieces[0].shape
    part = attn_cols // 2

    def kernel(index, source, low, core, result, out):
        value = jnp.concatenate([source[k ^ low] for k in range(height)], axis=0)
        value = value.astype(jnp.float32)
        place = slice(core * part, (core + 1) * part)

        @pl.when(pl.program_id(0) < 3)
        def _():
            result[0, :, place] = value.T

        @pl.when(pl.program_id(0) == 3)
        def _():
            out[place, :] = value

    return place_blocks(
        kernel,
        index,
        sums.pieces + sums.others,
        [
            pl.BlockSpec((1, width, attn_cols), lambda b, i: (jnp.minimum(b, 2), 0, 0)),
            pl.BlockSpec((attn_cols, width), lambda b, i: (0, 0)),
        ],
        [
            jax.ShapeDtypeStruct((3, width, attn_cols), jnp.float32),
            jax.ShapeDtypeStruct((attn_cols, width), jnp.float32),
        ],
        "place_attn",
    )


def place_proj(index, sums, total, extra):
    height, rows, width = sums.pieces[0].shape
    last = total - (4 * height - 1) * rows

    def kernel(index, source, low, core, result, others):
        columns = slice(core * width, (core + 1) * width)
        for k in range(height):
            value = source[k ^ low].astype(jnp.float32)
            result[k * rows : (k + 1) * rows, columns] = value

            @pl.when((pl.program_id(0) == 3) & (k == height - 1))
            def _(value=value):
                others[:, columns] = value[last : last + extra]

    return place_blocks(
        kernel,
        index,
        sums.pieces + sums.others,
        [
            pl.BlockSpec((height * rows, 2 * width), lambda b, i: (b, 0)),
            pl.BlockSpec((extra, 2 * width), lambda b, i: (0, 0)),
        ],
        [
            jax.ShapeDtypeStruct((total, 2 * width), jnp.float32),
            jax.ShapeDtypeStruct((extra, 2 * width), jnp.float32),
        ],
        "place_proj",
    )


def rms_forward(values, gain):
    scale = lax.rsqrt(jnp.mean(values * values, axis=-1, keepdims=True) + EPSILON)
    return (values * scale * gain, scale)


def rms_backward(values, scale, gain, grad_normed):
    unit = values * scale
    grad_unit = grad_normed * gain
    grad_values = scale * (grad_unit - unit * jnp.mean(grad_unit * unit, axis=-1, keepdims=True))
    return (grad_values, jnp.sum(grad_normed * unit, axis=0))


def block_scores(
    queries, key_rows, segments, padding, query_start, row_start, query_count, seq_len
):
    query_block = lax.dynamic_slice_in_dim(queries, query_start, query_count, 0)
    scores = jnp.einsum("qhd,khd->hqk", query_block, key_rows, preferred_element_type=jnp.float32)
    query_segment = lax.dynamic_slice_in_dim(segments, query_start, query_count, 0)
    query_place = query_start + jnp.arange(query_count)
    key_place = row_start + jnp.arange(seq_len)
    allowed = (query_segment[:, None] == segments[None, :]) & (
        (padding[None, :] == 1) | (query_place[:, None] == key_place[None, :])
    )
    return (jnp.where(allowed[None], scores, MASKED), query_block, key_rows)


def attention_forward(queries, key_rows, value_rows, segments, padding, seq_len, query_count):
    group_tokens = queries.shape[0]
    per_seq = seq_len // query_count

    def one_block(number):
        query_start = number * query_count
        row_start = number // per_seq * seq_len
        scores, _, _ = block_scores(
            queries, key_rows, segments, padding, query_start, row_start, query_count, seq_len
        )
        top = jnp.max(scores, axis=-1, keepdims=True)
        expo = jnp.exp(scores - top)
        weight_sum = jnp.sum(expo, axis=-1, keepdims=True)
        probs = (expo / weight_sum).astype(jnp.bfloat16)
        mixed = jnp.einsum("hqk,khd->qhd", probs, value_rows, preferred_element_type=jnp.float32)
        return (mixed.astype(jnp.bfloat16), (top + jnp.log(weight_sum))[:, :, 0])

    mixed, log_sums = lax.map(one_block, jnp.arange(group_tokens // query_count))
    return (mixed.reshape(group_tokens, -1), log_sums)


def attention_backward(
    queries, key_rows, value_rows, segments, padding, log_sums, grad_mixed, seq_len, query_count
):
    group_tokens, heads_here, head_size = queries.shape
    per_seq = seq_len // query_count

    def one_block(carry, item):
        grad_keys, grad_values = carry
        number, log_sum = item
        query_start = number * query_count
        row_start = number // per_seq * seq_len
        scores, query_block, key_block = block_scores(
            queries, key_rows, segments, padding, query_start, row_start, query_count, seq_len
        )
        grad_block = lax.dynamic_slice_in_dim(grad_mixed, query_start, query_count, 0)
        probs = jnp.exp(scores - log_sum[:, :, None])
        grad_probs = jnp.einsum(
            "qhd,khd->hqk", grad_block, value_rows, preferred_element_type=jnp.float32
        )
        grad_scores = probs * (grad_probs - jnp.sum(grad_probs * probs, axis=-1, keepdims=True))
        grad_scores = grad_scores.astype(jnp.bfloat16)
        grad_query = jnp.einsum(
            "hqk,khd->qhd", grad_scores, key_block, preferred_element_type=jnp.float32
        )
        key_part = jnp.einsum(
            "hqk,qhd->khd", grad_scores, query_block, preferred_element_type=jnp.float32
        )
        value_part = jnp.einsum(
            "hqk,qhd->khd",
            probs.astype(jnp.bfloat16),
            grad_block,
            preferred_element_type=jnp.float32,
        )
        grad_keys = grad_keys + key_part
        grad_values = grad_values + value_part
        return ((grad_keys, grad_values), grad_query)

    zero_grads = jnp.zeros((group_tokens, heads_here, head_size), jnp.float32)
    (grad_keys, grad_values), grad_queries = lax.scan(
        one_block, (zero_grads, zero_grads), (jnp.arange(group_tokens // query_count), log_sums)
    )
    return (grad_queries.reshape(group_tokens, heads_here, head_size), grad_keys, grad_values)


def local(
    features,
    segment_ids,
    padding_mask,
    w_proj,
    proj_bias,
    gain_attn,
    w_qkv,
    w_out,
    gain_ffn,
    w_gate_up,
    w_down,
    cotangent,
):
    local_tokens = features.shape[0]
    model_width = w_proj.shape[1]
    attn_cols = w_qkv.shape[2]
    heads_here = attn_cols // HEAD_DIM
    group_tokens = local_tokens * lax.axis_size("heads")
    query_count = min(512, group_tokens)
    ff_here = w_gate_up.shape[2]
    core = lax.axis_index("rows") % 2
    steps = plane_steps()
    count = len(steps)
    blocks = 1 << count
    rows_index = lax.axis_index("rows")
    places = [block_place(steps, rows_index ^ other) for other in range(2)]
    index = jnp.stack(places + [core, lax.axis_index("heads")]).astype(jnp.int32)
    fast = lax.axis_size("heads") == 2 and blocks == 8 and attn_cols % 256 == 0
    w_heads = jnp.transpose(w_qkv, (1, 0, 2))
    gate_flat = w_gate_up.reshape(model_width, 2 * ff_here)
    lifted = jnp.dot(features, w_proj, preferred_element_type=jnp.float32) + proj_bias
    normed, scale_attn = rms_forward(lifted, gain_attn)
    gathered = gather_group(normed.astype(jnp.bfloat16))
    segments = gather_group(segment_ids)
    padding = gather_group(padding_mask)
    gathered, cot_here = tie_sums(gathered, cotangent)
    grad_gathered = gather_group(cot_here)
    queries, key_rows, value_rows = (
        jnp.dot(gathered, w_heads[i], preferred_element_type=jnp.float32)
        .astype(jnp.bfloat16)
        .reshape(group_tokens, heads_here, HEAD_DIM)
        for i in range(3)
    )
    mixed, log_sums = attention_forward(
        queries, key_rows, value_rows, segments, padding, group_tokens, query_count
    )
    mixed, grad_gathered = tie_sums(mixed, grad_gathered)
    middle = lifted + scatter_group(
        jnp.dot(mixed, w_out, preferred_element_type=jnp.float32).astype(jnp.bfloat16)
    )
    normed_ffn, scale_ffn = rms_forward(middle, gain_ffn)
    gathered_ffn = gather_group(normed_ffn.astype(jnp.bfloat16))
    pair_normed = with_pair(gathered)
    pair_mixed = columns_to_pair(mixed)
    pair_cot = mixed_columns_to_pair(grad_gathered, blocks // 2)
    pair_features = with_pair(features)
    gathered_ffn, gate_flat, pair_normed, pair_mixed, pair_cot, pair_features = tie_sums(
        gathered_ffn, gate_flat, pair_normed, pair_mixed, pair_cot, pair_features
    )
    gate_up = jnp.dot(gathered_ffn, gate_flat, preferred_element_type=jnp.float32)
    activ, gelu_pull = jax.vjp(gelu_tanh, gate_up[:, :ff_here])
    up_part = gate_up[:, ff_here:]
    hidden = (activ * up_part).astype(jnp.bfloat16)
    pair_hidden = with_pair(hidden)
    grad_hidden = contract(grad_gathered, w_down, 1, 1)
    grad_gate = gelu_pull(grad_hidden * up_part)[0].astype(jnp.bfloat16)
    grad_up = (grad_hidden * activ).astype(jnp.bfloat16)
    pair_ffn = with_pair(gathered_ffn)
    pre_own = jnp.where(core == 0, grad_gate, grad_up)
    pre_other = jnp.where(core == 0, grad_up, grad_gate)
    pair_hidden, pre_own, pre_other, pair_ffn = tie_sums(pair_hidden, pre_own, pre_other, pair_ffn)
    pre_other = core_swap(pre_other)
    down_part = contract(pair_cot, pair_hidden, 0, 0)
    down = Summing(steps, down_part.astype(jnp.bfloat16).reshape(blocks, -1, ff_here))
    down.step()
    pair_pre = jnp.concatenate([pre_own, pre_other], axis=0)
    width = model_width // 2
    place = side(steps[0])
    grad_pre = jnp.concatenate([grad_gate, grad_up], axis=1)
    grad_pre, pair_pre = tie_sums(grad_pre, pair_pre)
    given, own = to_owners(lambda part: contract(part, gate_flat, 1, 1), grad_pre)
    gate_send, gate_keep = (
        contract(lax.dynamic_slice_in_dim(pair_ffn, which * width, width, 1), pair_pre, 0, 0)
        .astype(jnp.bfloat16)
        .reshape(blocks // 2, -1, ff_here)
        for which in (1 - place, place)
    )
    gate = Summing(steps, gate_keep, gate_send)
    gate.step()
    given, own, gate_send = tie_sums(down, given, own, gate_send)
    down.step()
    grad_normed_ffn = own + given.astype(jnp.float32)
    grad_ffn_norm, grad_gain_ffn = rms_backward(middle, scale_ffn, gain_ffn, grad_normed_ffn)
    grad_middle = cotangent.astype(jnp.float32) + grad_ffn_norm
    grad_mid_b = grad_middle.astype(jnp.bfloat16)
    grad_attn_in = gather_group(grad_mid_b)
    (grad_attn_in,) = tie_sums(gate, down, grad_attn_in)
    gate.step()
    down.step()
    grad_mixed = contract(grad_attn_in, w_out, 1, 1).astype(jnp.bfloat16)
    pair_mid = with_pair(grad_attn_in)
    grad_mixed, pair_mid = tie_sums(grad_mixed, pair_mid)
    grad_queries, grad_keys, grad_values = attention_backward(
        queries,
        key_rows,
        value_rows,
        segments,
        padding,
        log_sums,
        grad_mixed.reshape(group_tokens, heads_here, HEAD_DIM),
        group_tokens,
        query_count,
    )
    grad_flat = jnp.concatenate(
        [
            part.astype(jnp.bfloat16).reshape(group_tokens, attn_cols)
            for part in (grad_queries, grad_keys, grad_values)
        ],
        axis=1,
    )
    w_flat = jnp.concatenate([w_heads[i] for i in range(3)], axis=1)
    grad_flat, pair_mid = tie_sums(grad_flat, pair_mid)
    given, own = to_owners(lambda part: contract(part, w_flat, 1, 1), grad_flat)
    grad_flat, own, pair_mid = tie_sums(gate, down, grad_flat, own, pair_mid)
    gate.step()
    while down.done < count:
        down.step()
    pair_heads = jnp.concatenate(
        [columns_to_pair(grad_flat[:, i * attn_cols : (i + 1) * attn_cols]) for i in range(3)],
        axis=1,
    )
    attn_part = jnp.concatenate(
        [
            contract(pair_heads, pair_normed, 0, 0).astype(jnp.bfloat16),
            contract(pair_mixed, pair_mid, 0, 0).astype(jnp.bfloat16),
        ],
        axis=0,
    )
    attn = Summing(steps, attn_part.reshape(blocks, -1, attn_part.shape[1]))
    attn.step()
    given, own, attn_part = tie_sums(given, own, attn_part)
    grad_normed = own + given.astype(jnp.float32)
    grad_attn_norm, grad_gain_attn = rms_backward(lifted, scale_attn, gain_attn, grad_normed)
    grad_lifted = grad_middle + grad_attn_norm
    grad_lift_b = grad_lifted.astype(jnp.bfloat16)
    sums = jnp.stack([jnp.sum(grad_lifted, axis=0), grad_gain_attn, grad_gain_ffn])
    sums = jnp.pad(sums, ((0, 16 - sums.shape[0]), (0, 0)))
    half = model_width // 2
    mine, theirs = (
        lax.dynamic_slice_in_dim(sums, which * half, half, 1) for which in (core, 1 - core)
    )
    sums = (mine + core_swap(theirs)).astype(jnp.bfloat16)
    sums = jnp.pad(sums, ((0, 16 * blocks - sums.shape[0]), (0, 0)))
    proj_part = contract(pair_features, columns_to_pair(grad_lift_b), 0, 0).astype(jnp.bfloat16)
    proj_part = jnp.concatenate([proj_part, sums], axis=0)
    proj = Summing(steps, proj_part.reshape(blocks, -1, proj_part.shape[1]))
    proj.step()
    while gate.done < count:
        gate.step()
    ffn_rows = model_width // blocks
    ffn = Gathering(steps, jnp.concatenate([gate.part(0, 1), down.part(0, 1)], axis=1))
    ffn.step()
    hidden, grad_lift_b = tie_sums(proj, ffn, attn, hidden, grad_lift_b)
    proj.step()
    attn.step()
    while ffn.done < 2 * count - 1:
        ffn.step()
    tie_sums(proj)
    while proj.done < count:
        proj.step()
    layer_out = scatter_group(
        jnp.dot(hidden, w_down, preferred_element_type=jnp.float32).astype(jnp.bfloat16)
    )
    grad_features = contract(grad_lift_b, w_proj, 1, 1)
    tie_sums(proj, attn, ffn)
    proj.peers()
    while attn.done < count:
        attn.step()
    ffn.step()
    layer_out, grad_features = tie_sums(attn, ffn, proj, layer_out, grad_features)
    layer_out = middle + layer_out
    proj.step()
    attn.step()
    ffn.cores()
    if fast:
        grad_gate_up, grad_down = place_ffn(index, ffn, ffn_rows)
        tie_sums(proj, attn, grad_gate_up, grad_down)
    while proj.done < 2 * count:
        proj.step()
    while attn.done < 2 * count:
        attn.step()
    proj.cores()
    attn.cores()
    if fast:
        grad_proj, sums = place_proj(index, proj, w_proj.shape[0], 16)
        grad_qkv, grad_out = place_attn(index, attn, attn_cols)
        grad_qkv = jnp.transpose(grad_qkv, (1, 0, 2))
    else:
        half = attn_cols // 2
        mine, theirs = ordered(ffn.pieces, places[0]), ordered(ffn.others, places[1])
        pair = jnp.stack([jnp.where(core == 0, mine, theirs), jnp.where(core == 0, theirs, mine)])
        pair = pair.reshape(2, blocks, -1, ff_here).astype(jnp.float32)
        grad_gate_up = jnp.moveaxis(pair[:, :, :ffn_rows], 0, 2).reshape(model_width, 2, ff_here)
        grad_down = pair[:, :, ffn_rows:].reshape(2, blocks // 2, -1, ff_here)
        grad_down = jnp.moveaxis(grad_down, 0, 1).reshape(model_width, ff_here).T
        pair = two_cores(proj, places, 1).astype(jnp.float32)
        grad_proj, sums = pair[: w_proj.shape[0]], pair[w_proj.shape[0] :]
        pair = two_cores(attn, places, 0).reshape(2, 4, half, model_width)
        pair = jnp.moveaxis(pair, 0, 1).reshape(4, attn_cols, model_width).astype(jnp.float32)
        grad_qkv, grad_out = jnp.transpose(pair[:3], (2, 0, 1)), pair[3]
    return (
        layer_out.astype(jnp.bfloat16),
        grad_features,
        grad_proj,
        sums[0],
        sums[1],
        grad_qkv,
        grad_out,
        sums[2],
        grad_gate_up,
        grad_down,
    )


def solution(mesh):
    in_specs = (
        P(("rows", "heads"), None),
        P(("rows", "heads")),
        P(("rows", "heads")),
        P(),
        P(),
        P(),
        P(None, None, "heads"),
        P("heads", None),
        P(),
        P(None, None, "heads"),
        P("heads", None),
        P(("rows", "heads"), None),
    )
    out_specs = (
        P(("rows", "heads"), None),
        P(("rows", "heads"), None),
        P(),
        P(),
        P(),
        P(None, None, "heads"),
        P("heads", None),
        P(),
        P(None, None, "heads"),
        P("heads", None),
    )
    return jax.shard_map(local, mesh=mesh, in_specs=in_specs, out_specs=out_specs, check_vma=False)
```

```python
import jax
import jax.numpy as jnp
from jax import lax
from jax.experimental import pallas as pl
from jax.experimental.pallas import tpu as pltpu
from jax.sharding import PartitionSpec as P

HEAD_DIM = 64


EPSILON = 1e-06
MASKED = -1000000000.0


def gelu_tanh(values):
    return jax.nn.gelu(values, approximate=True)


def contract(left, right, left_dim, right_dim):
    return lax.dot_general(
        left, right, (((left_dim,), (right_dim,)), ((), ())), preferred_element_type=jnp.float32
    )


def swap_rows(value, masks):
    count = lax.axis_size("rows")
    return lax.ppermute(value, "rows", [(r, r ^ masks[r % 2]) for r in range(count)])


def core_swap(value):
    return swap_rows(value, (1, 1))


def peer_swap(value):
    return lax.ppermute(value, "heads", [(0, 1), (1, 0)])


def gather_group(value):
    if lax.axis_size("heads") == 2:
        return jnp.concatenate([value, peer_swap(value)], axis=0)
    return lax.all_gather(value, "heads", axis=0, tiled=True)


def scatter_group(value):
    if lax.axis_size("heads") == 2:
        mine = value.shape[0] // 2
        return value[:mine].astype(jnp.float32) + peer_swap(value[mine:]).astype(jnp.float32)
    return lax.psum_scatter(value, "heads", scatter_dimension=0, tiled=True).astype(jnp.float32)


def to_owners(product, left):
    if lax.axis_size("heads") == 2:
        mine = left.shape[0] // 2
        given = peer_swap(product(left[mine:]).astype(jnp.bfloat16))
        return (given, product(left[:mine]))
    given = lax.psum_scatter(
        product(left).astype(jnp.bfloat16), "heads", scatter_dimension=0, tiled=True
    )
    return (given, jnp.zeros((), jnp.float32))


def columns_to_group(value):
    size = lax.axis_size("heads")
    if size == 2:
        width = value.shape[1] // 2
        place = lax.axis_index("heads")
        mine = lax.dynamic_slice_in_dim(value, place * width, width, 1)
        theirs = lax.dynamic_slice_in_dim(value, (1 - place) * width, width, 1)
        return jnp.concatenate([mine, peer_swap(theirs)], axis=0)
    return lax.all_to_all(value, "heads", 1, 0, tiled=True)


def columns_to_pair(value, axis=1):
    width = value.shape[axis] // 2
    core = lax.axis_index("rows") % 2
    mine = lax.dynamic_slice_in_dim(value, core * width, width, axis)
    theirs = lax.dynamic_slice_in_dim(value, (1 - core) * width, width, axis)
    return jnp.concatenate([mine, core_swap(theirs)], axis=0)


def mixed_columns_to_pair(value, pieces):
    width = value.shape[1] // (2 * pieces)
    core = lax.axis_index("rows") % 2
    mine, theirs = (
        jnp.concatenate(
            [
                lax.dynamic_slice_in_dim(value, (2 * k + which) * width, width, 1)
                for k in range(pieces)
            ],
            axis=1,
        )
        for which in (core, 1 - core)
    )
    return jnp.concatenate([mine, core_swap(theirs)], axis=0)


def with_pair(value):
    return jnp.concatenate([value, core_swap(value)], axis=0)


def plane_steps(same=False):
    bits = (lax.axis_size("rows") // 2).bit_length() - 1
    low = bits // 2

    def line(first, count):
        return [
            ((1 << first, (first,) if count == 1 else (first, first + 1)))
        ] if count == 1 else [
            (1 << first, (first, first + 1)),
            (3 << first, (first + 1,)),
        ]

    near = line(1, low)
    far = line(1 + low, bits - low)

    def weave(one, two):
        one, two, order = list(one), list(two), []
        while one or two:
            if one:
                order.append(one.pop(0))
            if two:
                order.append(two.pop(0))
        return order

    first = weave(near, far)
    return list(zip(first, first if same else weave(far, near)))


def side(step, index=None):
    index = lax.axis_index("rows") if index is None else index

    def parity(places):
        total = jnp.zeros((), jnp.int32)
        for place in places:
            total = total ^ ((index >> place) & 1)
        return total

    return jnp.where(index % 2 == 0, parity(step[0][1]), parity(step[1][1]))


def block_place(steps, index):
    place = jnp.zeros((), jnp.int32)
    for step in steps:
        place = place * 2 + side(step, index)
    return place


class Summing:
    def __init__(self, steps, value, send=None):
        self.steps, self.done = steps, 0
        self.sides = [side(step) for step in steps]
        self.size = value.shape[0] if send is None else 2 * value.shape[0]
        self.terms, self.send = [(value, jnp.zeros((), jnp.int32))], send
        self.pieces, self.others, self.sent = [], [], None

    def last(self):
        return self.pieces[-1] if self.pieces else self.terms[-1][0]

    def update(self, value):
        if self.pieces:
            self.pieces = self.pieces[:-1] + [value]
        else:
            self.terms = self.terms[:-1] + [(value, self.terms[-1][1])]

    def masks(self, number):
        step = self.steps[number]
        return (step[0][0], step[1][0])

    def part(self, offset, size):
        total = sum(
            lax.dynamic_slice_in_dim(term, base + offset, size, 0).astype(jnp.float32)
            for term, base in self.terms
        )
        return total.astype(jnp.bfloat16)

    def step(self):
        count = len(self.steps)
        if self.done < count:
            place, half = self.sides[self.done], self.size // 2
            if self.send is None:
                send = self.part((1 - place) * half, half)
                self.terms = [(term, base + place * half) for term, base in self.terms]
            else:
                send, self.send = self.send, None
            got = swap_rows(send, self.masks(self.done))
            self.sent = send
            self.terms = self.terms + [(got, jnp.zeros((), jnp.int32))]
            self.size = half
        else:
            number = 2 * count - 1 - self.done
            if self.done == count:
                self.pieces, self.terms = [self.part(0, self.size)], []
            else:
                self.pieces = [jnp.concatenate(self.pieces, axis=0)]
            self.sent = self.pieces[0]
            self.pieces = self.pieces + [swap_rows(self.sent, self.masks(number))]
        self.done += 1

    def peers(self):
        own = self.part(0, self.size)
        if lax.axis_size("heads") == 2:
            total = own.astype(jnp.float32) + peer_swap(own).astype(jnp.float32)
        else:
            total = lax.psum(own.astype(jnp.float32), "heads")
        self.terms, self.sent = [(total.astype(jnp.bfloat16), jnp.zeros((), jnp.int32))], own

    def cores(self):
        self.others = [core_swap(piece) for piece in self.pieces]


def tie_sums(*sums_and_others):
    sums = [item for item in sums_and_others if isinstance(item, Summing)]
    others = [item for item in sums_and_others if not isinstance(item, Summing)]
    values, others = lax.optimization_barrier(([item.last() for item in sums], others))
    for item, value in zip(sums, values):
        item.update(value)
    return others


def advance(item, *earlier):
    item.update(lax.optimization_barrier((item.last(), earlier))[0])
    item.step()
    return item.sent


def behind(sums, *values):
    return lax.optimization_barrier(([item.sent for item in sums], values))[1]


def ordered(pieces, place):
    value = jnp.concatenate(pieces, axis=0)
    return jnp.concatenate(
        [
            lax.dynamic_slice_in_dim(value, place ^ block, 1, 0)
            for block in range(value.shape[0])
        ],
        axis=0,
    ).reshape(-1, value.shape[2])


def two_cores(sums, places, axis, reshape=None):
    mine, theirs = ordered(sums.pieces, places[0]), ordered(sums.others, places[1])
    if reshape is not None:
        mine, theirs = (value.reshape(reshape) for value in (mine, theirs))
    return jnp.where(
        lax.axis_index("rows") % 2 == 0,
        jnp.concatenate([mine, theirs], axis=axis),
        jnp.concatenate([theirs, mine], axis=axis),
    )


def place_blocks(kernel, index, sums, out_specs, out_shape, name):
    pieces = sums.pieces + sums.others
    blocks, rows, width = pieces[0].shape
    here = blocks // 2

    def body(index, *refs):
        sources, results = refs[:4], refs[4:]
        for number, source in enumerate(sources):
            own = index[number // 2]
            slot = index[2] if number < 2 else 1 - index[2]
            quarter = pl.program_id(0) ^ (own // here)
            inside = quarter // 2 == number % 2
            first = quarter % 2 * here
            for core in range(2):

                @pl.when(inside & (slot == core))
                def _(source=source, core=core, own=own, first=first):
                    parts = [source[first + (k ^ (own % here))] for k in range(here)]
                    kernel(parts, core, *results)

    whole = pl.BlockSpec((blocks, rows, width), lambda b, i: (0, 0, 0))
    return pl.pallas_call(
        body,
        grid_spec=pltpu.PrefetchScalarGridSpec(
            num_scalar_prefetch=1, grid=(4,), in_specs=[whole] * 4, out_specs=out_specs
        ),
        out_shape=out_shape,
        cost_estimate=pl.CostEstimate(
            flops=0, bytes_accessed=24 * blocks * rows * width, transcendentals=0
        ),
        compiler_params=pltpu.CompilerParams(vmem_limit_bytes=26 << 20),
        name=name,
    )(index, *pieces)


def place_gate_up(index, sums):
    blocks, rows, width = sums.pieces[0].shape

    def kernel(parts, core, result):
        for k, part in enumerate(parts):
            result[k * rows : (k + 1) * rows, core, :] = part.astype(jnp.float32)

    return place_blocks(
        kernel,
        index,
        sums,
        pl.BlockSpec((blocks // 2 * rows, 2, width), lambda b, i: (b, 0, 0)),
        jax.ShapeDtypeStruct((2 * blocks * rows, 2, width), jnp.float32),
        "place_gate_up",
    )


def place_down(index, sums):
    blocks, rows, width = sums.pieces[0].shape
    columns = blocks // 2 * rows

    def kernel(parts, core, result):
        value = jnp.concatenate(parts, axis=0).astype(jnp.float32)
        result[:, core * columns : (core + 1) * columns] = value.T

    return place_blocks(
        kernel,
        index,
        sums,
        pl.BlockSpec((width, 2 * columns), lambda b, i: (0, b)),
        jax.ShapeDtypeStruct((width, 8 * columns), jnp.float32),
        "place_down",
    )


def place_attn(index, sums, attn_cols):
    blocks, rows, width = sums.pieces[0].shape
    part = attn_cols // 2

    def kernel(parts, core, result, out):
        value = jnp.concatenate(parts, axis=0).astype(jnp.float32)
        place = slice(core * part, (core + 1) * part)

        @pl.when(pl.program_id(0) < 3)
        def _():
            result[0, :, place] = value.T

        @pl.when(pl.program_id(0) == 3)
        def _():
            out[place, :] = value

    return place_blocks(
        kernel,
        index,
        sums,
        [
            pl.BlockSpec((1, width, attn_cols), lambda b, i: (jnp.minimum(b, 2), 0, 0)),
            pl.BlockSpec((attn_cols, width), lambda b, i: (0, 0)),
        ],
        [
            jax.ShapeDtypeStruct((3, width, attn_cols), jnp.float32),
            jax.ShapeDtypeStruct((attn_cols, width), jnp.float32),
        ],
        "place_attn",
    )


def place_proj(index, sums, total, extra):
    blocks, rows, width = sums.pieces[0].shape
    last = total - (2 * blocks - 1) * rows

    def kernel(parts, core, result, others):
        columns = slice(core * width, (core + 1) * width)
        for k, part in enumerate(parts):
            value = part.astype(jnp.float32)
            result[k * rows : (k + 1) * rows, columns] = value

        @pl.when(pl.program_id(0) == 3)
        def _():
            others[:, columns] = value[last : last + extra]

    return place_blocks(
        kernel,
        index,
        sums,
        [
            pl.BlockSpec((blocks // 2 * rows, 2 * width), lambda b, i: (b, 0)),
            pl.BlockSpec((extra, 2 * width), lambda b, i: (0, 0)),
        ],
        [
            jax.ShapeDtypeStruct((total, 2 * width), jnp.float32),
            jax.ShapeDtypeStruct((extra, 2 * width), jnp.float32),
        ],
        "place_proj",
    )


def rms_forward(values, gain):
    scale = lax.rsqrt(jnp.mean(values * values, axis=-1, keepdims=True) + EPSILON)
    return (values * scale * gain, scale)


def rms_backward(values, scale, gain, grad_normed):
    unit = values * scale
    grad_unit = grad_normed * gain
    grad_values = scale * (grad_unit - unit * jnp.mean(grad_unit * unit, axis=-1, keepdims=True))
    return (grad_values, jnp.sum(grad_normed * unit, axis=0))


def block_scores(
    queries, key_rows, segments, padding, query_start, row_start, query_count, seq_len
):
    query_block = lax.dynamic_slice_in_dim(queries, query_start, query_count, 0)
    scores = jnp.einsum("qhd,khd->hqk", query_block, key_rows, preferred_element_type=jnp.float32)
    query_segment = lax.dynamic_slice_in_dim(segments, query_start, query_count, 0)
    query_place = query_start + jnp.arange(query_count)
    key_place = row_start + jnp.arange(seq_len)
    allowed = (query_segment[:, None] == segments[None, :]) & (
        (padding[None, :] == 1) | (query_place[:, None] == key_place[None, :])
    )
    return (jnp.where(allowed[None], scores, MASKED), query_block, key_rows)


def attention_forward(queries, key_rows, value_rows, segments, padding, seq_len, query_count):
    group_tokens = queries.shape[0]
    per_seq = seq_len // query_count

    def one_block(number):
        query_start = number * query_count
        row_start = number // per_seq * seq_len
        scores, _, _ = block_scores(
            queries, key_rows, segments, padding, query_start, row_start, query_count, seq_len
        )
        top = jnp.max(scores, axis=-1, keepdims=True)
        expo = jnp.exp(scores - top)
        weight_sum = jnp.sum(expo, axis=-1, keepdims=True)
        probs = (expo / weight_sum).astype(jnp.bfloat16)
        mixed = jnp.einsum("hqk,khd->qhd", probs, value_rows, preferred_element_type=jnp.float32)
        return (mixed.astype(jnp.bfloat16), (top + jnp.log(weight_sum))[:, :, 0])

    mixed, log_sums = lax.map(one_block, jnp.arange(group_tokens // query_count))
    return (mixed.reshape(group_tokens, -1), log_sums)


def attention_backward(
    queries, key_rows, value_rows, segments, padding, log_sums, grad_mixed, query_count, between
):
    tokens, heads_here, head_size = queries.shape

    def one_block(carry, item, between=lambda value: value):
        grad_keys, grad_values = carry
        start, log_sum = item
        scores, query_block, key_block = block_scores(
            queries, key_rows, segments, padding, start, 0, query_count, tokens
        )
        grad_block = lax.dynamic_slice_in_dim(grad_mixed, start, query_count, 0)
        probs = jnp.exp(scores - log_sum[:, :, None])
        grad_probs = jnp.einsum(
            "qhd,khd->hqk", grad_block, value_rows, preferred_element_type=jnp.float32
        )
        mean = between(jnp.sum(grad_probs * probs, axis=-1, keepdims=True))
        grad_scores = (probs * (grad_probs - mean)).astype(jnp.bfloat16)
        grad_query = jnp.einsum(
            "hqk,khd->qhd", grad_scores, key_block, preferred_element_type=jnp.float32
        )
        key_part = jnp.einsum(
            "hqk,qhd->khd", grad_scores, query_block, preferred_element_type=jnp.float32
        )
        value_part = jnp.einsum(
            "hqk,qhd->khd",
            probs.astype(jnp.bfloat16),
            grad_block,
            preferred_element_type=jnp.float32,
        )
        return ((grad_keys + key_part, grad_values + value_part), grad_query)

    zero_grads = jnp.zeros((tokens, heads_here, head_size), jnp.float32)
    starts = query_count * jnp.arange(tokens // query_count)
    if tokens == query_count:
        (grad_keys, grad_values), grad_queries = one_block(
            (zero_grads, zero_grads), (0, log_sums[0]), between
        )
    else:
        (grad_keys, grad_values), grad_queries = lax.scan(
            one_block, (zero_grads, zero_grads), (starts, log_sums)
        )
    return (grad_queries.reshape(tokens, heads_here, head_size), grad_keys, grad_values)


def local(
    features,
    segment_ids,
    padding_mask,
    w_proj,
    proj_bias,
    gain_attn,
    w_qkv,
    w_out,
    gain_ffn,
    w_gate_up,
    w_down,
    cotangent,
):
    local_tokens = features.shape[0]
    model_width = w_proj.shape[1]
    attn_cols = w_qkv.shape[2]
    heads_here = attn_cols // HEAD_DIM
    group_tokens = local_tokens * lax.axis_size("heads")
    query_count = min(512, group_tokens)
    ff_here = w_gate_up.shape[2]
    core = lax.axis_index("rows") % 2
    steps = plane_steps()
    count = len(steps)
    blocks = 1 << count
    rows_index = lax.axis_index("rows")
    places = [block_place(steps, rows_index ^ other) for other in range(2)]
    index = jnp.stack(places + [core, lax.axis_index("heads")]).astype(jnp.int32)
    fast = blocks == 8 and attn_cols % 256 == 0 and ff_here % 128 == 0
    w_heads = jnp.transpose(w_qkv, (1, 0, 2))
    gate_flat = w_gate_up.reshape(model_width, 2 * ff_here)
    lifted = jnp.dot(features, w_proj, preferred_element_type=jnp.float32) + proj_bias
    normed, scale_attn = rms_forward(lifted, gain_attn)
    gathered = gather_group(normed.astype(jnp.bfloat16))
    segments = gather_group(segment_ids)
    padding = gather_group(padding_mask)
    gathered, cot_here = tie_sums(gathered, cotangent)
    grad_gathered = gather_group(cot_here)
    queries, key_rows, value_rows = (
        jnp.dot(gathered, w_heads[i], preferred_element_type=jnp.float32)
        .astype(jnp.bfloat16)
        .reshape(group_tokens, heads_here, HEAD_DIM)
        for i in range(3)
    )
    mixed, log_sums = attention_forward(
        queries, key_rows, value_rows, segments, padding, group_tokens, query_count
    )
    mixed, grad_gathered = tie_sums(mixed, grad_gathered)
    middle = lifted + scatter_group(
        jnp.dot(mixed, w_out, preferred_element_type=jnp.float32).astype(jnp.bfloat16)
    )
    normed_ffn, scale_ffn = rms_forward(middle, gain_ffn)
    gathered_ffn = gather_group(normed_ffn.astype(jnp.bfloat16))
    pair_normed = with_pair(gathered)
    pair_mixed = columns_to_pair(mixed)
    pair_cot = mixed_columns_to_pair(grad_gathered, blocks // 2)
    pair_features = with_pair(features)
    gathered_ffn, gate_flat, pair_normed, pair_mixed, pair_cot, pair_features = tie_sums(
        gathered_ffn, gate_flat, pair_normed, pair_mixed, pair_cot, pair_features
    )
    gate_up = jnp.dot(gathered_ffn, gate_flat, preferred_element_type=jnp.float32)
    activ, gelu_pull = jax.vjp(gelu_tanh, gate_up[:, :ff_here])
    up_part = gate_up[:, ff_here:]
    hidden = (activ * up_part).astype(jnp.bfloat16)
    grad_hidden = contract(grad_gathered, w_down, 1, 1)
    grad_gate = gelu_pull(grad_hidden * up_part)[0].astype(jnp.bfloat16)
    grad_up = (grad_hidden * activ).astype(jnp.bfloat16)
    grad_pre = jnp.concatenate([grad_gate, grad_up], axis=1)
    given, own = to_owners(lambda part: contract(part, gate_flat, 1, 1), grad_pre)
    pre_other = core_swap(jnp.where(core == 0, grad_up, grad_gate))
    pair_hidden = with_pair(hidden)
    pair_ffn = with_pair(gathered_ffn)
    pair_pre = jnp.concatenate([jnp.where(core == 0, grad_gate, grad_up), pre_other], axis=0)
    down_part = contract(pair_cot, pair_hidden, 0, 0)
    down = Summing(steps, down_part.astype(jnp.bfloat16).reshape(blocks, -1, ff_here))
    down.step()
    width = model_width // 2
    place = side(steps[0])
    gate_send, gate_keep = (
        contract(lax.dynamic_slice_in_dim(pair_ffn, which * width, width, 1), pair_pre, 0, 0)
        .astype(jnp.bfloat16)
        .reshape(blocks // 2, -1, ff_here)
        for which in (1 - place, place)
    )
    gate = Summing(steps, gate_keep, gate_send)
    gate.step()
    given, own, gate_send, gate_keep = tie_sums(down, given, own, gate_send, gate_keep)
    down.step()
    grad_normed_ffn = own + given.astype(jnp.float32)
    grad_ffn_norm, grad_gain_ffn = rms_backward(middle, scale_ffn, gain_ffn, grad_normed_ffn)
    grad_middle = cotangent.astype(jnp.float32) + grad_ffn_norm
    grad_mid_b = grad_middle.astype(jnp.bfloat16)
    grad_attn_in = gather_group(grad_mid_b)
    (grad_attn_in,) = tie_sums(gate, down, grad_attn_in)
    gate.step()
    down.step()
    (grad_attn_in,) = behind((gate, down), grad_attn_in)
    grad_mixed = contract(grad_attn_in, w_out, 1, 1).astype(jnp.bfloat16)
    pair_mid = []

    def between(value):
        (value,) = tie_sums(gate, down, value)
        gate.step()
        down.step()
        value, group_mid = behind((gate, down), value, grad_attn_in)
        pair_mid.append(with_pair(group_mid))
        return value

    grad_queries, grad_keys, grad_values = attention_backward(
        queries,
        key_rows,
        value_rows,
        segments,
        padding,
        log_sums,
        grad_mixed.reshape(group_tokens, heads_here, HEAD_DIM),
        query_count,
        between,
    )
    pair_mid = pair_mid[0] if pair_mid else with_pair(grad_attn_in)
    grad_heads = [
        part.astype(jnp.bfloat16).reshape(group_tokens, attn_cols)
        for part in (grad_queries, grad_keys, grad_values)
    ]
    grad_heads = tie_sums(*grad_heads)
    grad_all = jnp.stack(grad_heads, axis=1)

    def to_normed(part):
        return sum(contract(part[:, i], w_heads[i], 1, 1) for i in range(3))

    given, own = to_owners(to_normed, grad_all)
    width = attn_cols // 2
    mine, theirs = (
        jnp.concatenate(
            [lax.dynamic_slice_in_dim(part, which * width, width, 1) for part in grad_heads],
            axis=1,
        )
        for which in (core, 1 - core)
    )
    pair_heads = jnp.concatenate([mine, core_swap(theirs)], axis=0)
    attn_part = jnp.concatenate(
        [
            contract(pair_heads, pair_normed, 0, 0).astype(jnp.bfloat16),
            contract(pair_mixed, pair_mid, 0, 0).astype(jnp.bfloat16),
        ],
        axis=0,
    )
    attn = Summing(steps, attn_part.reshape(blocks, -1, attn_part.shape[1]))
    attn.step()
    given, own = tie_sums(gate, given, own)
    gate.step()
    grad_normed = own + given.astype(jnp.float32)
    grad_attn_norm, grad_gain_attn = rms_backward(lifted, scale_attn, gain_attn, grad_normed)
    grad_lifted = grad_middle + grad_attn_norm
    grad_lift_b = grad_lifted.astype(jnp.bfloat16)
    sums = jnp.stack([jnp.sum(grad_lifted, axis=0), grad_gain_attn, grad_gain_ffn])
    sums = jnp.pad(sums, ((0, 16 - sums.shape[0]), (0, 0)))
    half = model_width // 2
    mine, theirs = (
        lax.dynamic_slice_in_dim(sums, which * half, half, 1) for which in (core, 1 - core)
    )
    sums = (mine + core_swap(theirs)).astype(jnp.bfloat16)
    sums = jnp.pad(sums, ((0, 16 * blocks - sums.shape[0]), (0, 0)))
    proj_part = contract(pair_features, columns_to_pair(grad_lift_b), 0, 0).astype(jnp.bfloat16)
    proj_part = jnp.concatenate([proj_part, sums], axis=0)
    proj = Summing(steps, proj_part.reshape(blocks, -1, proj_part.shape[1]))
    proj.step()
    sent = advance(down, proj.sent)
    sent = advance(attn, sent)
    sent = advance(gate, sent)
    hidden, grad_lift_b = lax.optimization_barrier((sent, hidden, grad_lift_b))[1:]
    layer_out = jnp.dot(hidden, w_down, preferred_element_type=jnp.float32).astype(jnp.bfloat16)
    layer_out = scatter_group(layer_out)
    grad_features = contract(grad_lift_b, w_proj, 1, 1)
    sent = advance(proj, grad_features)
    while down.done < 2 * count:
        sent = advance(down, sent)
    while attn.done < count:
        sent = advance(attn, sent)
    sent = advance(gate, sent)
    while proj.done < count:
        sent = advance(proj, sent)
    sent = advance(attn, sent)
    layer_out, sent = lax.optimization_barrier((layer_out, sent))
    layer_out = middle + layer_out
    down.update(lax.optimization_barrier((down.last(), sent, layer_out))[0])
    while down.done < 2 * count:
        down.step()
    down.cores()
    if fast:
        grad_down = place_down(index, down)
        sent = grad_down
    proj.update(lax.optimization_barrier((proj.last(), sent))[0])
    proj.peers()
    sent = advance(attn, proj.sent)
    sent = advance(proj, sent)
    gate.update(lax.optimization_barrier((gate.last(), sent))[0])
    while gate.done < 2 * count:
        gate.step()
    gate.cores()
    if fast:
        grad_gate_up = place_gate_up(index, gate)
        sent = grad_gate_up
    sent = advance(proj, sent)
    while attn.done < 2 * count:
        sent = advance(attn, sent)
    while proj.done < 2 * count:
        sent = advance(proj, sent)
    attn.update(lax.optimization_barrier((attn.last(), sent))[0])
    attn.cores()
    if fast:
        grad_qkv, grad_out = place_attn(index, attn, attn_cols)
        grad_qkv = jnp.transpose(grad_qkv, (1, 0, 2))
        sent = grad_qkv
    proj.update(lax.optimization_barrier((proj.last(), sent))[0])
    proj.cores()
    if fast:
        grad_proj, sums = place_proj(index, proj, w_proj.shape[0], 16)
    else:
        half = attn_cols // 2
        pair = two_cores(gate, places, 1, (model_width, 1, ff_here))
        grad_gate_up = pair.astype(jnp.float32)
        pair = two_cores(down, places, 0).reshape(2, blocks // 2, -1, ff_here)
        grad_down = jnp.moveaxis(pair, 0, 1).reshape(model_width, ff_here).T.astype(jnp.float32)
        pair = two_cores(proj, places, 1).astype(jnp.float32)
        grad_proj, sums = pair[: w_proj.shape[0]], pair[w_proj.shape[0] :]
        pair = two_cores(attn, places, 0).reshape(2, 4, half, model_width)
        pair = jnp.moveaxis(pair, 0, 1).reshape(4, attn_cols, model_width).astype(jnp.float32)
        grad_qkv, grad_out = jnp.transpose(pair[:3], (2, 0, 1)), pair[3]
    return (
        layer_out.astype(jnp.bfloat16),
        grad_features,
        grad_proj,
        sums[0],
        sums[1],
        grad_qkv,
        grad_out,
        sums[2],
        grad_gate_up,
        grad_down,
    )


def solution(mesh):
    in_specs = (
        P(("rows", "heads"), None),
        P(("rows", "heads")),
        P(("rows", "heads")),
        P(),
        P(),
        P(),
        P(None, None, "heads"),
        P("heads", None),
        P(),
        P(None, None, "heads"),
        P("heads", None),
        P(("rows", "heads"), None),
    )
    out_specs = (
        P(("rows", "heads"), None),
        P(("rows", "heads"), None),
        P(),
        P(),
        P(),
        P(None, None, "heads"),
        P("heads", None),
        P(),
        P(None, None, "heads"),
        P("heads", None),
    )
    return jax.shard_map(local, mesh=mesh, in_specs=in_specs, out_specs=out_specs, check_vma=False)
```

```python
import jax
import jax.numpy as jnp
from jax import lax
from jax.experimental import pallas as pl
from jax.experimental.pallas import tpu as pltpu
from jax.sharding import PartitionSpec as P

HEAD_DIM = 64


EPSILON = 1e-06
MASKED = -1000000000.0


def gelu_tanh(values):
    return jax.nn.gelu(values, approximate=True)


def contract(left, right, left_dim, right_dim):
    return lax.dot_general(
        left, right, (((left_dim,), (right_dim,)), ((), ())), preferred_element_type=jnp.float32
    )


def swap_rows(value, masks):
    count = lax.axis_size("rows")
    return lax.ppermute(value, "rows", [(r, r ^ masks[r % 2]) for r in range(count)])


def core_swap(value):
    return swap_rows(value, (1, 1))


def peer_swap(value):
    return lax.ppermute(value, "heads", [(0, 1), (1, 0)])


def gather_group(value):
    if lax.axis_size("heads") == 2:
        return jnp.concatenate([value, peer_swap(value)], axis=0)
    return lax.all_gather(value, "heads", axis=0, tiled=True)


def scatter_group(value):
    if lax.axis_size("heads") == 2:
        mine = value.shape[0] // 2
        return value[:mine].astype(jnp.float32) + peer_swap(value[mine:]).astype(jnp.float32)
    return lax.psum_scatter(value, "heads", scatter_dimension=0, tiled=True).astype(jnp.float32)


def to_owners(product, left):
    if lax.axis_size("heads") == 2:
        mine = left.shape[0] // 2
        given = peer_swap(product(left[mine:]).astype(jnp.bfloat16))
        return (given, product(left[:mine]))
    given = lax.psum_scatter(
        product(left).astype(jnp.bfloat16), "heads", scatter_dimension=0, tiled=True
    )
    return (given, jnp.zeros((), jnp.float32))


def columns_to_group(value):
    size = lax.axis_size("heads")
    if size == 2:
        width = value.shape[1] // 2
        place = lax.axis_index("heads")
        mine = lax.dynamic_slice_in_dim(value, place * width, width, 1)
        theirs = lax.dynamic_slice_in_dim(value, (1 - place) * width, width, 1)
        return jnp.concatenate([mine, peer_swap(theirs)], axis=0)
    return lax.all_to_all(value, "heads", 1, 0, tiled=True)


def columns_to_pair(value, axis=1):
    width = value.shape[axis] // 2
    core = lax.axis_index("rows") % 2
    mine = lax.dynamic_slice_in_dim(value, core * width, width, axis)
    theirs = lax.dynamic_slice_in_dim(value, (1 - core) * width, width, axis)
    return jnp.concatenate([mine, core_swap(theirs)], axis=0)


def mixed_columns_to_pair(value, pieces):
    width = value.shape[1] // (2 * pieces)
    core = lax.axis_index("rows") % 2
    mine, theirs = (
        jnp.concatenate(
            [
                lax.dynamic_slice_in_dim(value, (2 * k + which) * width, width, 1)
                for k in range(pieces)
            ],
            axis=1,
        )
        for which in (core, 1 - core)
    )
    return jnp.concatenate([mine, core_swap(theirs)], axis=0)


def with_pair(value):
    return jnp.concatenate([value, core_swap(value)], axis=0)


def plane_steps(same=False):
    bits = (lax.axis_size("rows") // 2).bit_length() - 1
    low = bits // 2

    def line(first, count):
        return [
            ((1 << first, (first,) if count == 1 else (first, first + 1)))
        ] if count == 1 else [
            (1 << first, (first, first + 1)),
            (3 << first, (first + 1,)),
        ]

    near = line(1, low)
    far = line(1 + low, bits - low)

    def weave(one, two):
        one, two, order = list(one), list(two), []
        while one or two:
            if one:
                order.append(one.pop(0))
            if two:
                order.append(two.pop(0))
        return order

    first = weave(near, far)
    return list(zip(first, first if same else weave(far, near)))


def side(step, index=None):
    index = lax.axis_index("rows") if index is None else index

    def parity(places):
        total = jnp.zeros((), jnp.int32)
        for place in places:
            total = total ^ ((index >> place) & 1)
        return total

    return jnp.where(index % 2 == 0, parity(step[0][1]), parity(step[1][1]))


def block_place(steps, index):
    place = jnp.zeros((), jnp.int32)
    for step in steps:
        place = place * 2 + side(step, index)
    return place


class Summing:
    def __init__(self, steps, value, send=None):
        self.steps, self.done = steps, 0
        self.sides = [side(step) for step in steps]
        self.size = value.shape[0] if send is None else 2 * value.shape[0]
        self.terms, self.send = [(value, jnp.zeros((), jnp.int32))], send
        self.pieces, self.others, self.sent = [], [], None

    def last(self):
        return self.pieces[-1] if self.pieces else self.terms[-1][0]

    def update(self, value):
        if self.pieces:
            self.pieces = self.pieces[:-1] + [value]
        else:
            self.terms = self.terms[:-1] + [(value, self.terms[-1][1])]

    def masks(self, number):
        step = self.steps[number]
        return (step[0][0], step[1][0])

    def part(self, offset, size):
        total = sum(
            lax.dynamic_slice_in_dim(term, base + offset, size, 0).astype(jnp.float32)
            for term, base in self.terms
        )
        return total.astype(jnp.bfloat16)

    def prepare(self):
        count = len(self.steps)
        if self.done < count:
            place, half = self.sides[self.done], self.size // 2
            if self.send is None:
                self.sent = self.part((1 - place) * half, half)
                self.terms = [(term, base + place * half) for term, base in self.terms]
            else:
                self.sent, self.send = self.send, None
            self.size = half
        else:
            if self.done == count:
                self.pieces, self.terms = [self.part(0, self.size)], []
            else:
                self.pieces = [jnp.concatenate(self.pieces, axis=0)]
            self.sent = self.pieces[0]

    def issue(self):
        count = len(self.steps)
        if self.done < count:
            got = swap_rows(self.sent, self.masks(self.done))
            self.terms = self.terms + [(got, jnp.zeros((), jnp.int32))]
        else:
            self.pieces = [self.sent, swap_rows(self.sent, self.masks(2 * count - 1 - self.done))]
        self.done += 1

    def step(self, *values):
        self.prepare()
        if values:
            self.sent, values = lax.optimization_barrier((self.sent, values))
        self.issue()
        return values if len(values) != 1 else values[0]

    def cores(self):
        self.others = [core_swap(piece) for piece in self.pieces]


def over_peers(steps, value):
    size = lax.axis_size("heads")
    width = value.shape[2] // size
    if size != 2:
        value = lax.psum_scatter(value, "heads", scatter_dimension=2, tiled=True)
        return Summing(steps, value)
    mine, theirs = (
        lax.dynamic_slice_in_dim(value, which * width, width, 2)
        for which in (lax.axis_index("heads"), 1 - lax.axis_index("heads"))
    )
    half = value.shape[0] // 2
    place = side(steps[0])

    def cut(part, which):
        return lax.dynamic_slice_in_dim(part, which * half, half, 0)

    got_send = peer_swap(cut(theirs, 1 - place))
    send = cut(mine, 1 - place).astype(jnp.float32) + got_send.astype(jnp.float32)
    got_keep = peer_swap(cut(theirs, place))
    total = Summing(steps, cut(mine, place), send.astype(jnp.bfloat16))
    total.terms.append((got_keep, jnp.zeros((), jnp.int32)))
    return total


def tie_sums(*sums_and_others):
    sums = [item for item in sums_and_others if isinstance(item, Summing)]
    others = [item for item in sums_and_others if not isinstance(item, Summing)]
    values, others = lax.optimization_barrier(([item.last() for item in sums], others))
    for item, value in zip(sums, values):
        item.update(value)
    return others


def advance(item, *earlier):
    item.update(lax.optimization_barrier((item.last(), earlier))[0])
    item.step()
    return item.sent


def behind(sums, *values):
    return lax.optimization_barrier(([item.sent for item in sums], values))[1]


def ordered(pieces, place):
    value = jnp.concatenate(pieces, axis=0)
    return jnp.concatenate(
        [
            lax.dynamic_slice_in_dim(value, place ^ block, 1, 0)
            for block in range(value.shape[0])
        ],
        axis=0,
    ).reshape(-1, value.shape[2])


def two_cores(sums, places, axis, reshape=None):
    mine, theirs = ordered(sums.pieces, places[0]), ordered(sums.others, places[1])
    if reshape is not None:
        mine, theirs = (value.reshape(reshape) for value in (mine, theirs))
    return jnp.where(
        lax.axis_index("rows") % 2 == 0,
        jnp.concatenate([mine, theirs], axis=axis),
        jnp.concatenate([theirs, mine], axis=axis),
    )


def place_blocks(kernel, index, sums, out_specs, out_shape, name):
    pieces = sums.pieces + sums.others
    blocks, rows, width = pieces[0].shape
    here = blocks // 2

    def body(index, *refs):
        sources, results = refs[:4], refs[4:]
        for number, source in enumerate(sources):
            own = index[number // 2]
            slot = index[2] if number < 2 else 1 - index[2]
            quarter = pl.program_id(0) ^ (own // here)
            inside = quarter // 2 == number % 2
            first = quarter % 2 * here
            for core in range(2):

                @pl.when(inside & (slot == core))
                def _(source=source, core=core, own=own, first=first):
                    parts = [source[first + (k ^ (own % here))] for k in range(here)]
                    kernel(parts, core, *results)

    whole = pl.BlockSpec((blocks, rows, width), lambda b, i: (0, 0, 0))
    return pl.pallas_call(
        body,
        grid_spec=pltpu.PrefetchScalarGridSpec(
            num_scalar_prefetch=1, grid=(4,), in_specs=[whole] * 4, out_specs=out_specs
        ),
        out_shape=out_shape,
        cost_estimate=pl.CostEstimate(
            flops=0, bytes_accessed=24 * blocks * rows * width, transcendentals=0
        ),
        compiler_params=pltpu.CompilerParams(vmem_limit_bytes=26 << 20),
        name=name,
    )(index, *pieces)


def place_gate_up(index, sums):
    blocks, rows, width = sums.pieces[0].shape

    def kernel(parts, core, result):
        for k, part in enumerate(parts):
            result[k * rows : (k + 1) * rows, core, :] = part.astype(jnp.float32)

    return place_blocks(
        kernel,
        index,
        sums,
        pl.BlockSpec((blocks // 2 * rows, 2, width), lambda b, i: (b, 0, 0)),
        jax.ShapeDtypeStruct((2 * blocks * rows, 2, width), jnp.float32),
        "place_gate_up",
    )


def place_down(index, sums):
    blocks, rows, width = sums.pieces[0].shape
    columns = blocks // 2 * rows

    def kernel(parts, core, result):
        value = jnp.concatenate(parts, axis=0).astype(jnp.float32)
        result[:, core * columns : (core + 1) * columns] = value.T

    return place_blocks(
        kernel,
        index,
        sums,
        pl.BlockSpec((width, 2 * columns), lambda b, i: (0, b)),
        jax.ShapeDtypeStruct((width, 8 * columns), jnp.float32),
        "place_down",
    )


def place_attn(index, sums, attn_cols):
    blocks, rows, width = sums.pieces[0].shape
    part = attn_cols // 2

    def kernel(parts, core, result, out):
        value = jnp.concatenate(parts, axis=0).astype(jnp.float32)
        place = slice(core * part, (core + 1) * part)

        @pl.when(pl.program_id(0) < 3)
        def _():
            result[0, :, place] = value.T

        @pl.when(pl.program_id(0) == 3)
        def _():
            out[place, :] = value

    return place_blocks(
        kernel,
        index,
        sums,
        [
            pl.BlockSpec((1, width, attn_cols), lambda b, i: (jnp.minimum(b, 2), 0, 0)),
            pl.BlockSpec((attn_cols, width), lambda b, i: (0, 0)),
        ],
        [
            jax.ShapeDtypeStruct((3, width, attn_cols), jnp.float32),
            jax.ShapeDtypeStruct((attn_cols, width), jnp.float32),
        ],
        "place_attn",
    )


def place_proj(index, pieces, total, extra):
    blocks, rows, width = pieces[0].shape
    here = blocks // 2
    last = total - (2 * blocks - 1) * rows

    def body(index, *refs):
        sources, result, others = refs[:8], refs[8], refs[9]
        for number, source in enumerate(sources):
            mine, peer, half = number // 4, number // 2 % 2, number % 2
            own = index[mine]
            slot = index[2] if mine == 0 else 1 - index[2]
            group = index[3] if peer == 0 else 1 - index[3]
            quarter = pl.program_id(0) ^ (own // here)
            first = quarter % 2 * here
            for column in range(4):

                @pl.when((quarter // 2 == half) & (slot * 2 + group == column))
                def _(source=source, column=column, own=own, first=first):
                    columns = slice(column * width, (column + 1) * width)
                    for k in range(here):
                        value = source[first + (k ^ (own % here))].astype(jnp.float32)
                        result[k * rows : (k + 1) * rows, columns] = value

                    @pl.when(pl.program_id(0) == 3)
                    def _():
                        others[:, columns] = value[last : last + extra]

    whole = pl.BlockSpec((blocks, rows, width), lambda b, i: (0, 0, 0))
    return pl.pallas_call(
        body,
        grid_spec=pltpu.PrefetchScalarGridSpec(
            num_scalar_prefetch=1,
            grid=(4,),
            in_specs=[whole] * 8,
            out_specs=[
                pl.BlockSpec((here * rows, 4 * width), lambda b, i: (b, 0)),
                pl.BlockSpec((extra, 4 * width), lambda b, i: (0, 0)),
            ],
        ),
        out_shape=[
            jax.ShapeDtypeStruct((total, 4 * width), jnp.float32),
            jax.ShapeDtypeStruct((extra, 4 * width), jnp.float32),
        ],
        cost_estimate=pl.CostEstimate(
            flops=0, bytes_accessed=48 * blocks * rows * width, transcendentals=0
        ),
        compiler_params=pltpu.CompilerParams(vmem_limit_bytes=26 << 20),
        name="place_proj",
    )(index, *pieces)


def rms_forward(values, gain):
    scale = lax.rsqrt(jnp.mean(values * values, axis=-1, keepdims=True) + EPSILON)
    return (values * scale * gain, scale)


def rms_backward(values, scale, gain, grad_normed):
    unit = values * scale
    grad_unit = grad_normed * gain
    grad_values = scale * (grad_unit - unit * jnp.mean(grad_unit * unit, axis=-1, keepdims=True))
    return (grad_values, jnp.sum(grad_normed * unit, axis=0))


def block_scores(
    queries, key_rows, segments, padding, query_start, row_start, query_count, seq_len
):
    query_block = lax.dynamic_slice_in_dim(queries, query_start, query_count, 0)
    scores = jnp.einsum("qhd,khd->hqk", query_block, key_rows, preferred_element_type=jnp.float32)
    query_segment = lax.dynamic_slice_in_dim(segments, query_start, query_count, 0)
    query_place = query_start + jnp.arange(query_count)
    key_place = row_start + jnp.arange(seq_len)
    allowed = (query_segment[:, None] == segments[None, :]) & (
        (padding[None, :] == 1) | (query_place[:, None] == key_place[None, :])
    )
    return (jnp.where(allowed[None], scores, MASKED), query_block, key_rows)


def attention_forward(queries, key_rows, value_rows, segments, padding, seq_len, query_count):
    group_tokens = queries.shape[0]
    per_seq = seq_len // query_count

    def one_block(number):
        query_start = number * query_count
        row_start = number // per_seq * seq_len
        scores, _, _ = block_scores(
            queries, key_rows, segments, padding, query_start, row_start, query_count, seq_len
        )
        top = jnp.max(scores, axis=-1, keepdims=True)
        expo = jnp.exp(scores - top)
        weight_sum = jnp.sum(expo, axis=-1, keepdims=True)
        probs = (expo / weight_sum).astype(jnp.bfloat16)
        mixed = jnp.einsum("hqk,khd->qhd", probs, value_rows, preferred_element_type=jnp.float32)
        return (mixed.astype(jnp.bfloat16), (top + jnp.log(weight_sum))[:, :, 0])

    mixed, log_sums = lax.map(one_block, jnp.arange(group_tokens // query_count))
    return (mixed.reshape(group_tokens, -1), log_sums)


def attention_backward(
    queries, key_rows, value_rows, segments, padding, log_sums, grad_mixed, query_count, between
):
    tokens, heads_here, head_size = queries.shape

    def one_block(carry, item, between=lambda value: value):
        grad_keys, grad_values = carry
        start, log_sum = item
        scores, query_block, key_block = block_scores(
            queries, key_rows, segments, padding, start, 0, query_count, tokens
        )
        grad_block = lax.dynamic_slice_in_dim(grad_mixed, start, query_count, 0)
        probs = jnp.exp(scores - log_sum[:, :, None])
        grad_probs = jnp.einsum(
            "qhd,khd->hqk", grad_block, value_rows, preferred_element_type=jnp.float32
        )
        mean = between(jnp.sum(grad_probs * probs, axis=-1, keepdims=True))
        grad_scores = (probs * (grad_probs - mean)).astype(jnp.bfloat16)
        grad_query = jnp.einsum(
            "hqk,khd->qhd", grad_scores, key_block, preferred_element_type=jnp.float32
        )
        key_part = jnp.einsum(
            "hqk,qhd->khd", grad_scores, query_block, preferred_element_type=jnp.float32
        )
        value_part = jnp.einsum(
            "hqk,qhd->khd",
            probs.astype(jnp.bfloat16),
            grad_block,
            preferred_element_type=jnp.float32,
        )
        return ((grad_keys + key_part, grad_values + value_part), grad_query)

    zero_grads = jnp.zeros((tokens, heads_here, head_size), jnp.float32)
    starts = query_count * jnp.arange(tokens // query_count)
    if tokens == query_count:
        (grad_keys, grad_values), grad_queries = one_block(
            (zero_grads, zero_grads), (0, log_sums[0]), between
        )
    else:
        (grad_keys, grad_values), grad_queries = lax.scan(
            one_block, (zero_grads, zero_grads), (starts, log_sums)
        )
    return (grad_queries.reshape(tokens, heads_here, head_size), grad_keys, grad_values)


def local(
    features,
    segment_ids,
    padding_mask,
    w_proj,
    proj_bias,
    gain_attn,
    w_qkv,
    w_out,
    gain_ffn,
    w_gate_up,
    w_down,
    cotangent,
):
    local_tokens = features.shape[0]
    model_width = w_proj.shape[1]
    attn_cols = w_qkv.shape[2]
    heads_here = attn_cols // HEAD_DIM
    group_tokens = local_tokens * lax.axis_size("heads")
    query_count = min(512, group_tokens)
    ff_here = w_gate_up.shape[2]
    core = lax.axis_index("rows") % 2
    steps = plane_steps()
    count = len(steps)
    blocks = 1 << count
    rows_index = lax.axis_index("rows")
    places = [block_place(steps, rows_index ^ other) for other in range(2)]
    index = jnp.stack(places + [core, lax.axis_index("heads")]).astype(jnp.int32)
    fast = lax.axis_size("heads") == 2 and blocks == 8 and attn_cols % 256 == 0 and ff_here % 128 == 0
    w_heads = jnp.transpose(w_qkv, (1, 0, 2))
    gate_flat = w_gate_up.reshape(model_width, 2 * ff_here)
    lifted = jnp.dot(features, w_proj, preferred_element_type=jnp.float32) + proj_bias
    normed, scale_attn = rms_forward(lifted, gain_attn)
    gathered = gather_group(normed.astype(jnp.bfloat16))
    segments = gather_group(segment_ids)
    padding = gather_group(padding_mask)
    gathered, cot_here = tie_sums(gathered, cotangent)
    grad_gathered = gather_group(cot_here)
    queries, key_rows, value_rows = (
        jnp.dot(gathered, w_heads[i], preferred_element_type=jnp.float32)
        .astype(jnp.bfloat16)
        .reshape(group_tokens, heads_here, HEAD_DIM)
        for i in range(3)
    )
    mixed, log_sums = attention_forward(
        queries, key_rows, value_rows, segments, padding, group_tokens, query_count
    )
    mixed, grad_gathered = tie_sums(mixed, grad_gathered)
    middle = lifted + scatter_group(
        jnp.dot(mixed, w_out, preferred_element_type=jnp.float32).astype(jnp.bfloat16)
    )
    normed_ffn, scale_ffn = rms_forward(middle, gain_ffn)
    gathered_ffn = gather_group(normed_ffn.astype(jnp.bfloat16))
    pair_normed = with_pair(gathered)
    pair_mixed = columns_to_pair(mixed)
    pair_cot = mixed_columns_to_pair(grad_gathered, blocks // 2)
    pair_features = with_pair(features)
    gathered_ffn, gate_flat, pair_normed, pair_mixed, pair_cot, pair_features = tie_sums(
        gathered_ffn, gate_flat, pair_normed, pair_mixed, pair_cot, pair_features
    )
    gate_up = jnp.dot(gathered_ffn, gate_flat, preferred_element_type=jnp.float32)
    activ, gelu_pull = jax.vjp(gelu_tanh, gate_up[:, :ff_here])
    up_part = gate_up[:, ff_here:]
    hidden = (activ * up_part).astype(jnp.bfloat16)
    grad_hidden = contract(grad_gathered, w_down, 1, 1)
    grad_gate = gelu_pull(grad_hidden * up_part)[0].astype(jnp.bfloat16)
    grad_up = (grad_hidden * activ).astype(jnp.bfloat16)
    grad_pre = jnp.concatenate([grad_gate, grad_up], axis=1)
    given, own = to_owners(lambda part: contract(part, gate_flat, 1, 1), grad_pre)
    pre_other = core_swap(jnp.where(core == 0, grad_up, grad_gate))
    pair_hidden = with_pair(hidden)
    pair_ffn = with_pair(gathered_ffn)
    pair_pre = jnp.concatenate([jnp.where(core == 0, grad_gate, grad_up), pre_other], axis=0)
    down_part = contract(pair_cot, pair_hidden, 0, 0)
    down = Summing(steps, down_part.astype(jnp.bfloat16).reshape(blocks, -1, ff_here))
    down.step()
    width = model_width // 2
    place = side(steps[0])
    gate_send, gate_keep = (
        contract(lax.dynamic_slice_in_dim(pair_ffn, which * width, width, 1), pair_pre, 0, 0)
        .astype(jnp.bfloat16)
        .reshape(blocks // 2, -1, ff_here)
        for which in (1 - place, place)
    )
    gate = Summing(steps, gate_keep, gate_send)
    gate.step()
    given, own, gate_send, gate_keep = tie_sums(down, given, own, gate_send, gate_keep)
    down.step()
    grad_normed_ffn = own + given.astype(jnp.float32)
    grad_ffn_norm, grad_gain_ffn = rms_backward(middle, scale_ffn, gain_ffn, grad_normed_ffn)
    grad_middle = cotangent.astype(jnp.float32) + grad_ffn_norm
    grad_mid_b = grad_middle.astype(jnp.bfloat16)
    grad_attn_in = gather_group(grad_mid_b)
    (grad_attn_in,) = tie_sums(gate, down, grad_attn_in)
    gate.step()
    down.step()
    (grad_attn_in,) = behind((gate, down), grad_attn_in)
    grad_mixed = contract(grad_attn_in, w_out, 1, 1).astype(jnp.bfloat16)
    pair_mid = []

    def between(value):
        (value,) = tie_sums(gate, down, value)
        gate.step()
        down.step()
        value, group_mid = behind((gate, down), value, grad_attn_in)
        pair_mid.append(with_pair(group_mid))
        return value

    grad_queries, grad_keys, grad_values = attention_backward(
        queries,
        key_rows,
        value_rows,
        segments,
        padding,
        log_sums,
        grad_mixed.reshape(group_tokens, heads_here, HEAD_DIM),
        query_count,
        between,
    )
    pair_mid = pair_mid[0] if pair_mid else with_pair(grad_attn_in)
    grad_heads = [
        part.astype(jnp.bfloat16).reshape(group_tokens, attn_cols)
        for part in (grad_queries, grad_keys, grad_values)
    ]
    grad_heads = tie_sums(*grad_heads)
    grad_all = jnp.stack(grad_heads, axis=1)

    def to_normed(part):
        return sum(contract(part[:, i], w_heads[i], 1, 1) for i in range(3))

    given, own = to_owners(to_normed, grad_all)
    width = attn_cols // 2
    mine, theirs = (
        jnp.concatenate(
            [lax.dynamic_slice_in_dim(part, which * width, width, 1) for part in grad_heads],
            axis=1,
        )
        for which in (core, 1 - core)
    )
    pair_heads = jnp.concatenate([mine, core_swap(theirs)], axis=0)
    attn_part = jnp.concatenate(
        [
            contract(pair_heads, pair_normed, 0, 0).astype(jnp.bfloat16),
            contract(pair_mixed, pair_mid, 0, 0).astype(jnp.bfloat16),
        ],
        axis=0,
    )
    attn = Summing(steps, attn_part.reshape(blocks, -1, attn_part.shape[1]))
    own = attn.step(own)
    (own,) = tie_sums(gate, own)
    own = gate.step(own)
    grad_normed = own + given.astype(jnp.float32)
    grad_attn_norm, grad_gain_attn = rms_backward(lifted, scale_attn, gain_attn, grad_normed)
    grad_lifted = grad_middle + grad_attn_norm
    grad_lift_b = grad_lifted.astype(jnp.bfloat16)
    sums = jnp.stack([jnp.sum(grad_lifted, axis=0), grad_gain_attn, grad_gain_ffn])
    sums = jnp.pad(sums, ((0, 16 - sums.shape[0]), (0, 0)))
    half = model_width // 2
    mine, theirs = (
        lax.dynamic_slice_in_dim(sums, which * half, half, 1) for which in (core, 1 - core)
    )
    sums = (mine + core_swap(theirs)).astype(jnp.bfloat16)
    sums = jnp.pad(sums, ((0, 16 * blocks - sums.shape[0]), (0, 0)))
    proj_part = contract(pair_features, columns_to_pair(grad_lift_b), 0, 0).astype(jnp.bfloat16)
    proj_part = jnp.concatenate([proj_part, sums], axis=0)
    proj = over_peers(steps, proj_part.reshape(blocks, -1, proj_part.shape[1]))
    proj.step()
    sent = advance(down, proj.sent)
    sent = advance(attn, sent)
    sent = advance(gate, sent)
    hidden, grad_lift_b = lax.optimization_barrier((sent, hidden, grad_lift_b))[1:]
    layer_out = jnp.dot(hidden, w_down, preferred_element_type=jnp.float32).astype(jnp.bfloat16)
    layer_out = scatter_group(layer_out)
    grad_features = contract(grad_lift_b, w_proj, 1, 1)
    sent = advance(proj, grad_features)
    while down.done < 2 * count:
        sent = advance(down, sent)
    while attn.done < count:
        sent = advance(attn, sent)
    sent = advance(gate, sent)
    while proj.done < count:
        sent = advance(proj, sent)
    sent = advance(attn, sent)
    layer_out, sent = lax.optimization_barrier((layer_out, sent))
    layer_out = middle + layer_out
    down.update(lax.optimization_barrier((down.last(), sent, layer_out))[0])
    while down.done < 2 * count:
        down.step()
    down.cores()
    if fast:
        grad_down = place_down(index, down)
        sent = grad_down
    sent = advance(proj, sent)
    sent = advance(attn, sent)
    gate.update(lax.optimization_barrier((gate.last(), sent))[0])
    while gate.done < 2 * count:
        gate.step()
    gate.cores()
    if fast:
        grad_gate_up = place_gate_up(index, gate)
        sent = grad_gate_up
    sent = advance(proj, sent)
    while proj.done < 2 * count - 1:
        sent = advance(proj, sent)
    near = [peer_swap(proj.pieces[0])] if fast else []
    while attn.done < 2 * count:
        sent = advance(attn, sent)
    last, near = lax.optimization_barrier((proj.last(), near))
    proj.update(last)
    near += [peer_swap(proj.pieces[1])] if fast else []
    sent = advance(proj, sent)
    low, high = proj.pieces
    attn.update(lax.optimization_barrier((attn.last(), sent))[0])
    attn.cores()
    attn.others, near = lax.optimization_barrier((attn.others, near))
    if fast:
        pieces = [low, high, jnp.concatenate(near, axis=0), peer_swap(high)]
        grad_qkv, grad_out = place_attn(index, attn, attn_cols)
        grad_qkv, pieces[3] = lax.optimization_barrier((grad_qkv, pieces[3]))
        pieces += [core_swap(piece) for piece in pieces]
        grad_qkv = jnp.transpose(grad_qkv, (1, 0, 2))
        grad_proj, sums = place_proj(index, pieces, w_proj.shape[0], 16)
    else:
        proj.cores()
        half = attn_cols // 2
        pair = two_cores(gate, places, 1, (model_width, 1, ff_here))
        grad_gate_up = pair.astype(jnp.float32)
        pair = two_cores(down, places, 0).reshape(2, blocks // 2, -1, ff_here)
        grad_down = jnp.moveaxis(pair, 0, 1).reshape(model_width, ff_here).T.astype(jnp.float32)
        pair = two_cores(proj, places, 1)
        pair = pair.reshape(pair.shape[0], 2, 1, -1)
        pair = lax.all_gather(pair, "heads", axis=2, tiled=True).astype(jnp.float32)
        pair = pair.reshape(pair.shape[0], -1)
        grad_proj, sums = pair[: w_proj.shape[0]], pair[w_proj.shape[0] :]
        pair = two_cores(attn, places, 0).reshape(2, 4, half, model_width)
        pair = jnp.moveaxis(pair, 0, 1).reshape(4, attn_cols, model_width).astype(jnp.float32)
        grad_qkv, grad_out = jnp.transpose(pair[:3], (2, 0, 1)), pair[3]
    return (
        layer_out.astype(jnp.bfloat16),
        grad_features,
        grad_proj,
        sums[0],
        sums[1],
        grad_qkv,
        grad_out,
        sums[2],
        grad_gate_up,
        grad_down,
    )


def solution(mesh):
    in_specs = (
        P(("rows", "heads"), None),
        P(("rows", "heads")),
        P(("rows", "heads")),
        P(),
        P(),
        P(),
        P(None, None, "heads"),
        P("heads", None),
        P(),
        P(None, None, "heads"),
        P("heads", None),
        P(("rows", "heads"), None),
    )
    out_specs = (
        P(("rows", "heads"), None),
        P(("rows", "heads"), None),
        P(),
        P(),
        P(),
        P(None, None, "heads"),
        P("heads", None),
        P(),
        P(None, None, "heads"),
        P("heads", None),
    )
    return jax.shard_map(local, mesh=mesh, in_specs=in_specs, out_specs=out_specs, check_vma=False)
```

```python
import jax
import jax.numpy as jnp
from jax import lax
from jax.experimental import pallas as pl
from jax.experimental.pallas import tpu as pltpu
from jax.sharding import PartitionSpec as P

HEAD_DIM = 64


EPSILON = 1e-06
MASKED = -1000000000.0


def gelu_tanh(values):
    return jax.nn.gelu(values, approximate=True)


def contract(left, right, left_dim, right_dim):
    return lax.dot_general(
        left, right, (((left_dim,), (right_dim,)), ((), ())), preferred_element_type=jnp.float32
    )


def swap_rows(value, masks):
    count = lax.axis_size("rows")
    return lax.ppermute(value, "rows", [(r, r ^ masks[r % 2]) for r in range(count)])


def core_swap(value):
    return swap_rows(value, (1, 1))


def peer_swap(value):
    return lax.ppermute(value, "heads", [(0, 1), (1, 0)])


def gather_group(value):
    if lax.axis_size("heads") == 2:
        return jnp.concatenate([value, peer_swap(value)], axis=0)
    return lax.all_gather(value, "heads", axis=0, tiled=True)


def scatter_group(value):
    if lax.axis_size("heads") == 2:
        mine = value.shape[0] // 2
        return value[:mine].astype(jnp.float32) + peer_swap(value[mine:]).astype(jnp.float32)
    return lax.psum_scatter(value, "heads", scatter_dimension=0, tiled=True).astype(jnp.float32)


def to_owners(product, left):
    if lax.axis_size("heads") == 2:
        mine = left.shape[0] // 2
        given = peer_swap(product(left[mine:]).astype(jnp.bfloat16))
        return (given, product(left[:mine]))
    given = lax.psum_scatter(
        product(left).astype(jnp.bfloat16), "heads", scatter_dimension=0, tiled=True
    )
    return (given, jnp.zeros((), jnp.float32))


def columns_to_group(value):
    size = lax.axis_size("heads")
    if size == 2:
        width = value.shape[1] // 2
        place = lax.axis_index("heads")
        mine = lax.dynamic_slice_in_dim(value, place * width, width, 1)
        theirs = lax.dynamic_slice_in_dim(value, (1 - place) * width, width, 1)
        return jnp.concatenate([mine, peer_swap(theirs)], axis=0)
    return lax.all_to_all(value, "heads", 1, 0, tiled=True)


def columns_to_pair(value, axis=1):
    width = value.shape[axis] // 2
    core = lax.axis_index("rows") % 2
    mine = lax.dynamic_slice_in_dim(value, core * width, width, axis)
    theirs = lax.dynamic_slice_in_dim(value, (1 - core) * width, width, axis)
    return jnp.concatenate([mine, core_swap(theirs)], axis=0)


def mixed_columns_to_pair(value, pieces):
    width = value.shape[1] // (2 * pieces)
    core = lax.axis_index("rows") % 2
    mine, theirs = (
        jnp.concatenate(
            [
                lax.dynamic_slice_in_dim(value, (2 * k + which) * width, width, 1)
                for k in range(pieces)
            ],
            axis=1,
        )
        for which in (core, 1 - core)
    )
    return jnp.concatenate([mine, core_swap(theirs)], axis=0)


def with_pair(value):
    return jnp.concatenate([value, core_swap(value)], axis=0)


def plane_steps(same=False):
    bits = (lax.axis_size("rows") // 2).bit_length() - 1
    low = bits // 2

    def line(first, count):
        return [
            ((1 << first, (first,) if count == 1 else (first, first + 1)))
        ] if count == 1 else [
            (1 << first, (first, first + 1)),
            (3 << first, (first + 1,)),
        ]

    near = line(1, low)
    far = line(1 + low, bits - low)

    def weave(one, two):
        one, two, order = list(one), list(two), []
        while one or two:
            if one:
                order.append(one.pop(0))
            if two:
                order.append(two.pop(0))
        return order

    first = weave(near, far)
    return list(zip(first, first if same else weave(far, near)))


def side(step, index=None):
    index = lax.axis_index("rows") if index is None else index

    def parity(places):
        total = jnp.zeros((), jnp.int32)
        for place in places:
            total = total ^ ((index >> place) & 1)
        return total

    return jnp.where(index % 2 == 0, parity(step[0][1]), parity(step[1][1]))


def block_place(steps, index):
    place = jnp.zeros((), jnp.int32)
    for step in steps:
        place = place * 2 + side(step, index)
    return place


class Summing:
    def __init__(self, steps, value, send=None):
        self.steps, self.done = steps, 0
        self.sides = [side(step) for step in steps]
        self.size = value.shape[0] if send is None else 2 * value.shape[0]
        self.terms, self.send = [(value, jnp.zeros((), jnp.int32))], send
        self.pieces, self.others, self.sent = [], [], None

    def last(self):
        return self.pieces[-1] if self.pieces else self.terms[-1][0]

    def update(self, value):
        if self.pieces:
            self.pieces = self.pieces[:-1] + [value]
        else:
            self.terms = self.terms[:-1] + [(value, self.terms[-1][1])]

    def masks(self, number):
        step = self.steps[number]
        return (step[0][0], step[1][0])

    def part(self, offset, size):
        total = sum(
            lax.dynamic_slice_in_dim(term, base + offset, size, 0).astype(jnp.float32)
            for term, base in self.terms
        )
        return total.astype(jnp.bfloat16)

    def prepare(self):
        count = len(self.steps)
        if self.done < count:
            place, half = self.sides[self.done], self.size // 2
            if self.send is None:
                self.sent = self.part((1 - place) * half, half)
                self.terms = [(term, base + place * half) for term, base in self.terms]
            else:
                self.sent, self.send = self.send, None
            self.size = half
        else:
            if self.done == count:
                self.pieces, self.terms = [self.part(0, self.size)], []
            else:
                self.pieces = [jnp.concatenate(self.pieces, axis=0)]
            self.sent = self.pieces[0]

    def issue(self):
        count = len(self.steps)
        if self.done < count:
            got = swap_rows(self.sent, self.masks(self.done))
            self.terms = self.terms + [(got, jnp.zeros((), jnp.int32))]
        else:
            self.pieces = [self.sent, swap_rows(self.sent, self.masks(2 * count - 1 - self.done))]
        self.done += 1

    def step(self, *values):
        self.prepare()
        if values:
            self.sent, values = lax.optimization_barrier((self.sent, values))
        self.issue()
        return values if len(values) != 1 else values[0]

    def cores(self):
        self.others = [core_swap(piece) for piece in self.pieces]


def over_peers(steps, value):
    size = lax.axis_size("heads")
    width = value.shape[2] // size
    if size != 2:
        value = lax.psum_scatter(value, "heads", scatter_dimension=2, tiled=True)
        return Summing(steps, value)
    mine, theirs = (
        lax.dynamic_slice_in_dim(value, which * width, width, 2)
        for which in (lax.axis_index("heads"), 1 - lax.axis_index("heads"))
    )
    half = value.shape[0] // 2
    place = side(steps[0])

    def cut(part, which):
        return lax.dynamic_slice_in_dim(part, which * half, half, 0)

    got_send = peer_swap(cut(theirs, 1 - place))
    send = cut(mine, 1 - place).astype(jnp.float32) + got_send.astype(jnp.float32)
    got_keep = peer_swap(cut(theirs, place))
    total = Summing(steps, cut(mine, place), send.astype(jnp.bfloat16))
    total.terms.append((got_keep, jnp.zeros((), jnp.int32)))
    return total


def tie_sums(*sums_and_others):
    sums = [item for item in sums_and_others if isinstance(item, Summing)]
    others = [item for item in sums_and_others if not isinstance(item, Summing)]
    values, others = lax.optimization_barrier(([item.last() for item in sums], others))
    for item, value in zip(sums, values):
        item.update(value)
    return others


def advance(item, *earlier):
    item.update(lax.optimization_barrier((item.last(), earlier))[0])
    item.step()
    return item.sent


def ordered(pieces, place):
    value = jnp.concatenate(pieces, axis=0)
    return jnp.concatenate(
        [
            lax.dynamic_slice_in_dim(value, place ^ block, 1, 0)
            for block in range(value.shape[0])
        ],
        axis=0,
    ).reshape(-1, value.shape[2])


def two_cores(sums, places, axis, reshape=None):
    mine, theirs = ordered(sums.pieces, places[0]), ordered(sums.others, places[1])
    if reshape is not None:
        mine, theirs = (value.reshape(reshape) for value in (mine, theirs))
    return jnp.where(
        lax.axis_index("rows") % 2 == 0,
        jnp.concatenate([mine, theirs], axis=axis),
        jnp.concatenate([theirs, mine], axis=axis),
    )


def place_blocks(kernel, index, sums, out_specs, out_shape, name):
    pieces = sums.pieces + sums.others
    blocks, rows, width = pieces[0].shape
    here = blocks // 2

    def body(index, *refs):
        sources, results = refs[:4], refs[4:]
        for number, source in enumerate(sources):
            own = index[number // 2]
            slot = index[2] if number < 2 else 1 - index[2]
            quarter = pl.program_id(0) ^ (own // here)
            inside = quarter // 2 == number % 2
            first = quarter % 2 * here
            for core in range(2):

                @pl.when(inside & (slot == core))
                def _(source=source, core=core, own=own, first=first):
                    parts = [source[first + (k ^ (own % here))] for k in range(here)]
                    kernel(parts, core, *results)

    whole = pl.BlockSpec((blocks, rows, width), lambda b, i: (0, 0, 0))
    return pl.pallas_call(
        body,
        grid_spec=pltpu.PrefetchScalarGridSpec(
            num_scalar_prefetch=1, grid=(4,), in_specs=[whole] * 4, out_specs=out_specs
        ),
        out_shape=out_shape,
        cost_estimate=pl.CostEstimate(
            flops=0, bytes_accessed=24 * blocks * rows * width, transcendentals=0
        ),
        compiler_params=pltpu.CompilerParams(vmem_limit_bytes=26 << 20),
        name=name,
    )(index, *pieces)


def place_gate_up(index, sums):
    blocks, rows, width = sums.pieces[0].shape

    def kernel(parts, core, result):
        for k, part in enumerate(parts):
            result[k * rows : (k + 1) * rows, core, :] = part.astype(jnp.float32)

    return place_blocks(
        kernel,
        index,
        sums,
        pl.BlockSpec((blocks // 2 * rows, 2, width), lambda b, i: (b, 0, 0)),
        jax.ShapeDtypeStruct((2 * blocks * rows, 2, width), jnp.float32),
        "place_gate_up",
    )


def place_down(index, sums):
    blocks, rows, width = sums.pieces[0].shape
    columns = blocks // 2 * rows

    def kernel(parts, core, result):
        value = jnp.concatenate(parts, axis=0).astype(jnp.float32)
        result[:, core * columns : (core + 1) * columns] = value.T

    return place_blocks(
        kernel,
        index,
        sums,
        pl.BlockSpec((width, 2 * columns), lambda b, i: (0, b)),
        jax.ShapeDtypeStruct((width, 8 * columns), jnp.float32),
        "place_down",
    )


def place_attn(index, sums, attn_cols):
    blocks, rows, width = sums.pieces[0].shape
    part = attn_cols // 2

    def kernel(parts, core, result, out):
        value = jnp.concatenate(parts, axis=0).astype(jnp.float32)
        place = slice(core * part, (core + 1) * part)

        @pl.when(pl.program_id(0) < 3)
        def _():
            result[0, :, place] = value.T

        @pl.when(pl.program_id(0) == 3)
        def _():
            out[place, :] = value

    return place_blocks(
        kernel,
        index,
        sums,
        [
            pl.BlockSpec((1, width, attn_cols), lambda b, i: (jnp.minimum(b, 2), 0, 0)),
            pl.BlockSpec((attn_cols, width), lambda b, i: (0, 0)),
        ],
        [
            jax.ShapeDtypeStruct((3, width, attn_cols), jnp.float32),
            jax.ShapeDtypeStruct((attn_cols, width), jnp.float32),
        ],
        "place_attn",
    )


def place_proj(index, pieces, total, extra):
    blocks, rows, width = pieces[0].shape
    here = blocks // 2
    last = total - (2 * blocks - 1) * rows

    def body(index, *refs):
        sources, result, others = refs[:8], refs[8], refs[9]
        for number, source in enumerate(sources):
            mine, peer, half = number // 4, number // 2 % 2, number % 2
            own = index[mine]
            slot = index[2] if mine == 0 else 1 - index[2]
            group = index[3] if peer == 0 else 1 - index[3]
            quarter = pl.program_id(0) ^ (own // here)
            first = quarter % 2 * here
            for column in range(4):

                @pl.when((quarter // 2 == half) & (slot * 2 + group == column))
                def _(source=source, column=column, own=own, first=first):
                    columns = slice(column * width, (column + 1) * width)
                    for k in range(here):
                        value = source[first + (k ^ (own % here))].astype(jnp.float32)
                        result[k * rows : (k + 1) * rows, columns] = value

                    @pl.when(pl.program_id(0) == 3)
                    def _():
                        others[:, columns] = value[last : last + extra]

    whole = pl.BlockSpec((blocks, rows, width), lambda b, i: (0, 0, 0))
    return pl.pallas_call(
        body,
        grid_spec=pltpu.PrefetchScalarGridSpec(
            num_scalar_prefetch=1,
            grid=(4,),
            in_specs=[whole] * 8,
            out_specs=[
                pl.BlockSpec((here * rows, 4 * width), lambda b, i: (b, 0)),
                pl.BlockSpec((extra, 4 * width), lambda b, i: (0, 0)),
            ],
        ),
        out_shape=[
            jax.ShapeDtypeStruct((total, 4 * width), jnp.float32),
            jax.ShapeDtypeStruct((extra, 4 * width), jnp.float32),
        ],
        cost_estimate=pl.CostEstimate(
            flops=0, bytes_accessed=48 * blocks * rows * width, transcendentals=0
        ),
        compiler_params=pltpu.CompilerParams(vmem_limit_bytes=26 << 20),
        name="place_proj",
    )(index, *pieces)


def rms_forward(values, gain):
    scale = lax.rsqrt(jnp.mean(values * values, axis=-1, keepdims=True) + EPSILON)
    return (values * scale * gain, scale)


def rms_backward(values, scale, gain, grad_normed):
    unit = values * scale
    grad_unit = grad_normed * gain
    grad_values = scale * (grad_unit - unit * jnp.mean(grad_unit * unit, axis=-1, keepdims=True))
    return (grad_values, jnp.sum(grad_normed * unit, axis=0))


def block_scores(
    queries, key_rows, segments, padding, query_start, row_start, query_count, seq_len
):
    query_block = lax.dynamic_slice_in_dim(queries, query_start, query_count, 0)
    scores = jnp.einsum("qhd,khd->hqk", query_block, key_rows, preferred_element_type=jnp.float32)
    query_segment = lax.dynamic_slice_in_dim(segments, query_start, query_count, 0)
    query_place = query_start + jnp.arange(query_count)
    key_place = row_start + jnp.arange(seq_len)
    allowed = (query_segment[:, None] == segments[None, :]) & (
        (padding[None, :] == 1) | (query_place[:, None] == key_place[None, :])
    )
    return (jnp.where(allowed[None], scores, MASKED), query_block, key_rows)


def attention_forward(queries, key_rows, value_rows, segments, padding, seq_len, query_count):
    group_tokens = queries.shape[0]
    per_seq = seq_len // query_count

    def one_block(number):
        query_start = number * query_count
        row_start = number // per_seq * seq_len
        scores, _, _ = block_scores(
            queries, key_rows, segments, padding, query_start, row_start, query_count, seq_len
        )
        top = jnp.max(scores, axis=-1, keepdims=True)
        expo = jnp.exp(scores - top)
        weight_sum = jnp.sum(expo, axis=-1, keepdims=True)
        probs = (expo / weight_sum).astype(jnp.bfloat16)
        mixed = jnp.einsum("hqk,khd->qhd", probs, value_rows, preferred_element_type=jnp.float32)
        return (mixed.astype(jnp.bfloat16), (top + jnp.log(weight_sum))[:, :, 0])

    mixed, log_sums = lax.map(one_block, jnp.arange(group_tokens // query_count))
    return (mixed.reshape(group_tokens, -1), log_sums)


def attention_backward(
    queries, key_rows, value_rows, segments, padding, log_sums, grad_mixed, query_count, between
):
    tokens, heads_here, head_size = queries.shape

    def one_block(carry, item, between=lambda value: value):
        grad_keys, grad_values = carry
        start, log_sum = item
        scores, query_block, key_block = block_scores(
            queries, key_rows, segments, padding, start, 0, query_count, tokens
        )
        grad_block = lax.dynamic_slice_in_dim(grad_mixed, start, query_count, 0)
        probs = jnp.exp(scores - log_sum[:, :, None])
        grad_probs = jnp.einsum(
            "qhd,khd->hqk", grad_block, value_rows, preferred_element_type=jnp.float32
        )
        mean = between(jnp.sum(grad_probs * probs, axis=-1, keepdims=True))
        grad_scores = (probs * (grad_probs - mean)).astype(jnp.bfloat16)
        grad_query = jnp.einsum(
            "hqk,khd->qhd", grad_scores, key_block, preferred_element_type=jnp.float32
        )
        key_part = jnp.einsum(
            "hqk,qhd->khd", grad_scores, query_block, preferred_element_type=jnp.float32
        )
        value_part = jnp.einsum(
            "hqk,qhd->khd",
            probs.astype(jnp.bfloat16),
            grad_block,
            preferred_element_type=jnp.float32,
        )
        return ((grad_keys + key_part, grad_values + value_part), grad_query)

    zero_grads = jnp.zeros((tokens, heads_here, head_size), jnp.float32)
    starts = query_count * jnp.arange(tokens // query_count)
    if tokens == query_count:
        (grad_keys, grad_values), grad_queries = one_block(
            (zero_grads, zero_grads), (0, log_sums[0]), between
        )
    else:
        (grad_keys, grad_values), grad_queries = lax.scan(
            one_block, (zero_grads, zero_grads), (starts, log_sums)
        )
    return (grad_queries.reshape(tokens, heads_here, head_size), grad_keys, grad_values)


def local(
    features,
    segment_ids,
    padding_mask,
    w_proj,
    proj_bias,
    gain_attn,
    w_qkv,
    w_out,
    gain_ffn,
    w_gate_up,
    w_down,
    cotangent,
):
    local_tokens = features.shape[0]
    model_width = w_proj.shape[1]
    attn_cols = w_qkv.shape[2]
    heads_here = attn_cols // HEAD_DIM
    group_tokens = local_tokens * lax.axis_size("heads")
    query_count = min(512, group_tokens)
    ff_here = w_gate_up.shape[2]
    core = lax.axis_index("rows") % 2
    steps = plane_steps()
    count = len(steps)
    blocks = 1 << count
    rows_index = lax.axis_index("rows")
    places = [block_place(steps, rows_index ^ other) for other in range(2)]
    index = jnp.stack(places + [core, lax.axis_index("heads")]).astype(jnp.int32)
    fast = lax.axis_size("heads") == 2 and blocks == 8 and attn_cols % 256 == 0 and ff_here % 128 == 0
    w_heads = jnp.transpose(w_qkv, (1, 0, 2))
    gate_flat = w_gate_up.reshape(model_width, 2 * ff_here)
    lifted = jnp.dot(features, w_proj, preferred_element_type=jnp.float32) + proj_bias
    normed, scale_attn = rms_forward(lifted, gain_attn)
    gathered = gather_group(normed.astype(jnp.bfloat16))
    segments = gather_group(segment_ids)
    padding = gather_group(padding_mask)
    gathered, cot_here = tie_sums(gathered, cotangent)
    grad_gathered = gather_group(cot_here)
    queries, key_rows, value_rows = (
        jnp.dot(gathered, w_heads[i], preferred_element_type=jnp.float32)
        .astype(jnp.bfloat16)
        .reshape(group_tokens, heads_here, HEAD_DIM)
        for i in range(3)
    )
    mixed, log_sums = attention_forward(
        queries, key_rows, value_rows, segments, padding, group_tokens, query_count
    )
    mixed, grad_gathered = tie_sums(mixed, grad_gathered)
    middle = lifted + scatter_group(
        jnp.dot(mixed, w_out, preferred_element_type=jnp.float32).astype(jnp.bfloat16)
    )
    normed_ffn, scale_ffn = rms_forward(middle, gain_ffn)
    gathered_ffn = gather_group(normed_ffn.astype(jnp.bfloat16))
    pair_normed = with_pair(gathered)
    pair_mixed = columns_to_pair(mixed)
    pair_cot = mixed_columns_to_pair(grad_gathered, blocks // 2)
    features_more = jnp.concatenate(
        [
            jnp.pad(features, ((0, 0), (0, 16 * blocks))),
            jnp.eye(16, w_proj.shape[0] + 16 * blocks, w_proj.shape[0], dtype=features.dtype),
        ],
        axis=0,
    )
    pair_features = with_pair(features_more)
    gathered_ffn, gate_flat, pair_normed, pair_mixed, pair_cot, pair_features = tie_sums(
        gathered_ffn, gate_flat, pair_normed, pair_mixed, pair_cot, pair_features
    )
    gate_up = jnp.dot(gathered_ffn, gate_flat, preferred_element_type=jnp.float32)
    activ, gelu_pull = jax.vjp(gelu_tanh, gate_up[:, :ff_here])
    up_part = gate_up[:, ff_here:]
    hidden = (activ * up_part).astype(jnp.bfloat16)
    grad_hidden = contract(grad_gathered, w_down, 1, 1)
    grad_gate = gelu_pull(grad_hidden * up_part)[0].astype(jnp.bfloat16)
    grad_up = (grad_hidden * activ).astype(jnp.bfloat16)
    grad_pre = jnp.concatenate([grad_gate, grad_up], axis=1)
    given, own = to_owners(lambda part: contract(part, gate_flat, 1, 1), grad_pre)
    pre_other = core_swap(jnp.where(core == 0, grad_up, grad_gate))
    pair_hidden = with_pair(hidden)
    pair_ffn = with_pair(gathered_ffn)
    pair_pre = jnp.concatenate([jnp.where(core == 0, grad_gate, grad_up), pre_other], axis=0)
    down_part = contract(pair_cot, pair_hidden, 0, 0)
    down = Summing(steps, down_part.astype(jnp.bfloat16).reshape(blocks, -1, ff_here))
    down.step()
    width = model_width // 2
    place = side(steps[0])
    gate_send, gate_keep = (
        contract(lax.dynamic_slice_in_dim(pair_ffn, which * width, width, 1), pair_pre, 0, 0)
        .astype(jnp.bfloat16)
        .reshape(blocks // 2, -1, ff_here)
        for which in (1 - place, place)
    )
    gate = Summing(steps, gate_keep, gate_send)
    gate.step()
    given, own, gate_send, gate_keep = tie_sums(down, given, own, gate_send, gate_keep)
    down.step()
    grad_normed_ffn = own + given.astype(jnp.float32)
    grad_ffn_norm, grad_gain_ffn = rms_backward(middle, scale_ffn, gain_ffn, grad_normed_ffn)
    grad_middle = cotangent.astype(jnp.float32) + grad_ffn_norm
    grad_mid_b = grad_middle.astype(jnp.bfloat16)
    grad_attn_in = gather_group(grad_mid_b)
    (grad_attn_in,) = tie_sums(gate, down, grad_attn_in)
    gate.step()
    down.step()
    grad_mixed = contract(grad_attn_in, w_out, 1, 1).astype(jnp.bfloat16)
    pair_mid = []

    def between(value):
        (value,) = tie_sums(gate, down, value)
        gate.step()
        down.step()
        pair_mid.append(with_pair(grad_attn_in))
        return value

    grad_queries, grad_keys, grad_values = attention_backward(
        queries,
        key_rows,
        value_rows,
        segments,
        padding,
        log_sums,
        grad_mixed.reshape(group_tokens, heads_here, HEAD_DIM),
        query_count,
        between,
    )
    pair_mid = pair_mid[0] if pair_mid else with_pair(grad_attn_in)
    grad_heads = [
        part.astype(jnp.bfloat16).reshape(group_tokens, attn_cols)
        for part in (grad_queries, grad_keys, grad_values)
    ]
    grad_heads = tie_sums(*grad_heads)
    grad_all = jnp.stack(grad_heads, axis=1)

    def to_normed(part):
        return sum(contract(part[:, i], w_heads[i], 1, 1) for i in range(3))

    given, own = to_owners(to_normed, grad_all)
    width = attn_cols // 2
    mine, theirs = (
        jnp.concatenate(
            [lax.dynamic_slice_in_dim(part, which * width, width, 1) for part in grad_heads],
            axis=1,
        )
        for which in (core, 1 - core)
    )
    pair_heads = jnp.concatenate([mine, core_swap(theirs)], axis=0)
    attn_part = jnp.concatenate(
        [
            contract(pair_heads, pair_normed, 0, 0).astype(jnp.bfloat16),
            contract(pair_mixed, pair_mid, 0, 0).astype(jnp.bfloat16),
        ],
        axis=0,
    )
    attn = Summing(steps, attn_part.reshape(blocks, -1, attn_part.shape[1]))
    own = attn.step(own)
    (own,) = tie_sums(gate, own)
    own = gate.step(own)
    grad_normed = own + given.astype(jnp.float32)
    grad_attn_norm, grad_gain_attn = rms_backward(lifted, scale_attn, gain_attn, grad_normed)
    grad_lifted = grad_middle + grad_attn_norm
    grad_lift_b = grad_lifted.astype(jnp.bfloat16)
    sums = jnp.stack([jnp.sum(grad_lifted, axis=0), grad_gain_attn, grad_gain_ffn])
    sums = jnp.pad(sums, ((0, 16 - sums.shape[0]), (0, 0))).astype(jnp.bfloat16)
    lift_more = jnp.concatenate([grad_lift_b, sums], axis=0)
    proj_part = contract(pair_features, columns_to_pair(lift_more), 0, 0).astype(jnp.bfloat16)
    proj = over_peers(steps, proj_part.reshape(blocks, -1, proj_part.shape[1]))
    proj.step()
    sent = advance(down, proj.sent)
    sent = advance(attn, sent)
    sent = advance(gate, sent)
    hidden, grad_lift_b = lax.optimization_barrier((sent, hidden, grad_lift_b))[1:]
    layer_out = jnp.dot(hidden, w_down, preferred_element_type=jnp.float32).astype(jnp.bfloat16)
    layer_out = scatter_group(layer_out)
    grad_features = contract(grad_lift_b, w_proj, 1, 1)
    sent = advance(proj, grad_features)
    while down.done < 2 * count:
        sent = advance(down, sent)
    while attn.done < count:
        sent = advance(attn, sent)
    sent = advance(gate, sent)
    while proj.done < count:
        sent = advance(proj, sent)
    sent = advance(attn, sent)
    layer_out, sent = lax.optimization_barrier((layer_out, sent))
    layer_out = middle + layer_out
    down.update(lax.optimization_barrier((down.last(), sent, layer_out))[0])
    while down.done < 2 * count:
        down.step()
    down.cores()
    if fast:
        grad_down = place_down(index, down)
        sent = grad_down
    sent = advance(proj, sent)
    sent = advance(attn, sent)
    gate.update(lax.optimization_barrier((gate.last(), sent))[0])
    while gate.done < 2 * count:
        gate.step()
    gate.cores()
    if fast:
        grad_gate_up = place_gate_up(index, gate)
        sent = grad_gate_up
    sent = advance(proj, sent)
    while proj.done < 2 * count - 1:
        sent = advance(proj, sent)
    near = [peer_swap(proj.pieces[0])] if fast else []
    while attn.done < 2 * count:
        sent = advance(attn, sent)
    last, near = lax.optimization_barrier((proj.last(), near))
    proj.update(last)
    near += [peer_swap(proj.pieces[1])] if fast else []
    sent = advance(proj, sent)
    low, high = proj.pieces
    attn.update(lax.optimization_barrier((attn.last(), sent))[0])
    attn.cores()
    attn.others, near = lax.optimization_barrier((attn.others, near))
    if fast:
        pieces = [low, high, jnp.concatenate(near, axis=0), peer_swap(high)]
        grad_qkv, grad_out = place_attn(index, attn, attn_cols)
        grad_qkv, pieces[3] = lax.optimization_barrier((grad_qkv, pieces[3]))
        pieces += [core_swap(piece) for piece in pieces]
        grad_qkv = jnp.transpose(grad_qkv, (1, 0, 2))
        grad_proj, sums = place_proj(index, pieces, w_proj.shape[0], 16)
    else:
        proj.cores()
        half = attn_cols // 2
        pair = two_cores(gate, places, 1, (model_width, 1, ff_here))
        grad_gate_up = pair.astype(jnp.float32)
        pair = two_cores(down, places, 0).reshape(2, blocks // 2, -1, ff_here)
        grad_down = jnp.moveaxis(pair, 0, 1).reshape(model_width, ff_here).T.astype(jnp.float32)
        pair = two_cores(proj, places, 1)
        pair = pair.reshape(pair.shape[0], 2, 1, -1)
        pair = lax.all_gather(pair, "heads", axis=2, tiled=True).astype(jnp.float32)
        pair = pair.reshape(pair.shape[0], -1)
        grad_proj, sums = pair[: w_proj.shape[0]], pair[w_proj.shape[0] :]
        pair = two_cores(attn, places, 0).reshape(2, 4, half, model_width)
        pair = jnp.moveaxis(pair, 0, 1).reshape(4, attn_cols, model_width).astype(jnp.float32)
        grad_qkv, grad_out = jnp.transpose(pair[:3], (2, 0, 1)), pair[3]
    return (
        layer_out.astype(jnp.bfloat16),
        grad_features,
        grad_proj,
        sums[0],
        sums[1],
        grad_qkv,
        grad_out,
        sums[2],
        grad_gate_up,
        grad_down,
    )


def solution(mesh):
    in_specs = (
        P(("rows", "heads"), None),
        P(("rows", "heads")),
        P(("rows", "heads")),
        P(),
        P(),
        P(),
        P(None, None, "heads"),
        P("heads", None),
        P(),
        P(None, None, "heads"),
        P("heads", None),
        P(("rows", "heads"), None),
    )
    out_specs = (
        P(("rows", "heads"), None),
        P(("rows", "heads"), None),
        P(),
        P(),
        P(),
        P(None, None, "heads"),
        P("heads", None),
        P(),
        P(None, None, "heads"),
        P("heads", None),
    )
    return jax.shard_map(local, mesh=mesh, in_specs=in_specs, out_specs=out_specs, check_vma=False)
```

```python
import jax
import jax.numpy as jnp
from jax import lax
from jax.experimental import pallas as pl
from jax.experimental.pallas import tpu as pltpu
from jax.sharding import PartitionSpec as P

HEAD_DIM = 64


EPSILON = 1e-06
MASKED = -1000000000.0


def gelu_tanh(values):
    return jax.nn.gelu(values, approximate=True)


def contract(left, right, left_dim, right_dim):
    return lax.dot_general(
        left, right, (((left_dim,), (right_dim,)), ((), ())), preferred_element_type=jnp.float32
    )


def swap_rows(value, masks):
    count = lax.axis_size("rows")
    return lax.ppermute(value, "rows", [(r, r ^ masks[r % 2]) for r in range(count)])


def core_swap(value):
    return swap_rows(value, (1, 1))


def peer_swap(value):
    return lax.ppermute(value, "heads", [(0, 1), (1, 0)])


def gather_group(value):
    if lax.axis_size("heads") == 2:
        return jnp.concatenate([value, peer_swap(value)], axis=0)
    return lax.all_gather(value, "heads", axis=0, tiled=True)


def scatter_group(value):
    if lax.axis_size("heads") == 2:
        mine = value.shape[0] // 2
        return value[:mine].astype(jnp.float32) + peer_swap(value[mine:]).astype(jnp.float32)
    return lax.psum_scatter(value, "heads", scatter_dimension=0, tiled=True).astype(jnp.float32)


def to_owners(product, left):
    if lax.axis_size("heads") == 2:
        mine = left.shape[0] // 2
        given = peer_swap(product(left[mine:]).astype(jnp.bfloat16))
        return (given, product(left[:mine]))
    given = lax.psum_scatter(
        product(left).astype(jnp.bfloat16), "heads", scatter_dimension=0, tiled=True
    )
    return (given, jnp.zeros((), jnp.float32))


def columns_to_group(value):
    size = lax.axis_size("heads")
    if size == 2:
        width = value.shape[1] // 2
        place = lax.axis_index("heads")
        mine = lax.dynamic_slice_in_dim(value, place * width, width, 1)
        theirs = lax.dynamic_slice_in_dim(value, (1 - place) * width, width, 1)
        return jnp.concatenate([mine, peer_swap(theirs)], axis=0)
    return lax.all_to_all(value, "heads", 1, 0, tiled=True)


def columns_to_pair(value, axis=1):
    width = value.shape[axis] // 2
    core = lax.axis_index("rows") % 2
    mine = lax.dynamic_slice_in_dim(value, core * width, width, axis)
    theirs = lax.dynamic_slice_in_dim(value, (1 - core) * width, width, axis)
    return jnp.concatenate([mine, core_swap(theirs)], axis=0)


def mixed_columns_to_pair(value, pieces):
    width = value.shape[1] // (2 * pieces)
    core = lax.axis_index("rows") % 2
    mine, theirs = (
        jnp.concatenate(
            [
                lax.dynamic_slice_in_dim(value, (2 * k + which) * width, width, 1)
                for k in range(pieces)
            ],
            axis=1,
        )
        for which in (core, 1 - core)
    )
    return jnp.concatenate([mine, core_swap(theirs)], axis=0)


def with_pair(value):
    return jnp.concatenate([value, core_swap(value)], axis=0)


def plane_steps(same=False):
    bits = (lax.axis_size("rows") // 2).bit_length() - 1
    low = bits // 2

    def line(first, count):
        return [
            ((1 << first, (first,) if count == 1 else (first, first + 1)))
        ] if count == 1 else [
            (1 << first, (first, first + 1)),
            (3 << first, (first + 1,)),
        ]

    near = line(1, low)
    far = line(1 + low, bits - low)

    def weave(one, two):
        one, two, order = list(one), list(two), []
        while one or two:
            if one:
                order.append(one.pop(0))
            if two:
                order.append(two.pop(0))
        return order

    first = weave(near, far)
    return list(zip(first, first if same else weave(far, near)))


def side(step, index=None):
    index = lax.axis_index("rows") if index is None else index

    def parity(places):
        total = jnp.zeros((), jnp.int32)
        for place in places:
            total = total ^ ((index >> place) & 1)
        return total

    return jnp.where(index % 2 == 0, parity(step[0][1]), parity(step[1][1]))


def block_place(steps, index):
    place = jnp.zeros((), jnp.int32)
    for step in steps:
        place = place * 2 + side(step, index)
    return place


class Summing:
    def __init__(self, steps, value, send=None):
        self.steps, self.done = steps, 0
        self.sides = [side(step) for step in steps]
        self.size = value.shape[0] if send is None else 2 * value.shape[0]
        self.terms, self.send = [(value, jnp.zeros((), jnp.int32))], send
        self.pieces, self.others, self.sent = [], [], None

    def last(self):
        return self.pieces[-1] if self.pieces else self.terms[-1][0]

    def update(self, value):
        if self.pieces:
            self.pieces = self.pieces[:-1] + [value]
        else:
            self.terms = self.terms[:-1] + [(value, self.terms[-1][1])]

    def masks(self, number):
        step = self.steps[number]
        return (step[0][0], step[1][0])

    def part(self, offset, size):
        total = sum(
            lax.dynamic_slice_in_dim(term, base + offset, size, 0).astype(jnp.float32)
            for term, base in self.terms
        )
        return total.astype(jnp.bfloat16)

    def prepare(self):
        count = len(self.steps)
        if self.done < count:
            place, half = self.sides[self.done], self.size // 2
            if self.send is None:
                self.sent = self.part((1 - place) * half, half)
                self.terms = [(term, base + place * half) for term, base in self.terms]
            else:
                self.sent, self.send = self.send, None
            self.size = half
        else:
            if self.done == count:
                self.pieces, self.terms = [self.part(0, self.size)], []
            else:
                self.pieces = [jnp.concatenate(self.pieces, axis=0)]
            self.sent = self.pieces[0]

    def issue(self):
        count = len(self.steps)
        if self.done < count:
            got = swap_rows(self.sent, self.masks(self.done))
            self.terms = self.terms + [(got, jnp.zeros((), jnp.int32))]
        else:
            self.pieces = [self.sent, swap_rows(self.sent, self.masks(2 * count - 1 - self.done))]
        self.done += 1

    def step(self, *values):
        self.prepare()
        if values:
            self.sent, values = lax.optimization_barrier((self.sent, values))
        self.issue()
        return values if len(values) != 1 else values[0]

    def cores(self):
        self.others = [core_swap(piece) for piece in self.pieces]


def over_peers(steps, value):
    size = lax.axis_size("heads")
    width = value.shape[2] // size
    if size != 2:
        value = lax.psum_scatter(value, "heads", scatter_dimension=2, tiled=True)
        return Summing(steps, value)
    mine, theirs = (
        lax.dynamic_slice_in_dim(value, which * width, width, 2)
        for which in (lax.axis_index("heads"), 1 - lax.axis_index("heads"))
    )
    half = value.shape[0] // 2
    place = side(steps[0])

    def cut(part, which):
        return lax.dynamic_slice_in_dim(part, which * half, half, 0)

    got_send = peer_swap(cut(theirs, 1 - place))
    send = cut(mine, 1 - place).astype(jnp.float32) + got_send.astype(jnp.float32)
    got_keep = peer_swap(cut(theirs, place))
    total = Summing(steps, cut(mine, place), send.astype(jnp.bfloat16))
    total.terms.append((got_keep, jnp.zeros((), jnp.int32)))
    return total


def tie_sums(*sums_and_others):
    sums = [item for item in sums_and_others if isinstance(item, Summing)]
    others = [item for item in sums_and_others if not isinstance(item, Summing)]
    values, others = lax.optimization_barrier(([item.last() for item in sums], others))
    for item, value in zip(sums, values):
        item.update(value)
    return others


def advance(item, *earlier):
    item.update(lax.optimization_barrier((item.last(), earlier))[0])
    item.step()
    return item.sent


def ordered(pieces, place):
    value = jnp.concatenate(pieces, axis=0)
    return jnp.concatenate(
        [
            lax.dynamic_slice_in_dim(value, place ^ block, 1, 0)
            for block in range(value.shape[0])
        ],
        axis=0,
    ).reshape(-1, value.shape[2])


def two_cores(sums, places, axis, reshape=None):
    mine, theirs = ordered(sums.pieces, places[0]), ordered(sums.others, places[1])
    if reshape is not None:
        mine, theirs = (value.reshape(reshape) for value in (mine, theirs))
    return jnp.where(
        lax.axis_index("rows") % 2 == 0,
        jnp.concatenate([mine, theirs], axis=axis),
        jnp.concatenate([theirs, mine], axis=axis),
    )


def place_blocks(kernel, index, sums, out_specs, out_shape, name):
    pieces = sums.pieces + sums.others
    blocks, rows, width = pieces[0].shape
    here = blocks // 2

    def body(index, *refs):
        sources, results = refs[:4], refs[4:]
        for number, source in enumerate(sources):
            own = index[number // 2]
            slot = index[2] if number < 2 else 1 - index[2]
            quarter = pl.program_id(0) ^ (own // here)
            inside = quarter // 2 == number % 2
            first = quarter % 2 * here
            for core in range(2):

                @pl.when(inside & (slot == core))
                def _(source=source, core=core, own=own, first=first):
                    parts = [source[first + (k ^ (own % here))] for k in range(here)]
                    kernel(parts, core, *results)

    whole = pl.BlockSpec((blocks, rows, width), lambda b, i: (0, 0, 0))
    return pl.pallas_call(
        body,
        grid_spec=pltpu.PrefetchScalarGridSpec(
            num_scalar_prefetch=1, grid=(4,), in_specs=[whole] * 4, out_specs=out_specs
        ),
        out_shape=out_shape,
        cost_estimate=pl.CostEstimate(
            flops=0, bytes_accessed=24 * blocks * rows * width, transcendentals=0
        ),
        compiler_params=pltpu.CompilerParams(vmem_limit_bytes=26 << 20),
        name=name,
    )(index, *pieces)


def place_gate_up(index, sums):
    blocks, rows, width = sums.pieces[0].shape

    def kernel(parts, core, result):
        for k, part in enumerate(parts):
            result[k * rows : (k + 1) * rows, core, :] = part.astype(jnp.float32)

    return place_blocks(
        kernel,
        index,
        sums,
        pl.BlockSpec((blocks // 2 * rows, 2, width), lambda b, i: (b, 0, 0)),
        jax.ShapeDtypeStruct((2 * blocks * rows, 2, width), jnp.float32),
        "place_gate_up",
    )


def place_down(index, sums):
    blocks, rows, width = sums.pieces[0].shape
    columns = blocks // 2 * rows

    def kernel(parts, core, result):
        value = jnp.concatenate(parts, axis=0).astype(jnp.float32)
        result[:, core * columns : (core + 1) * columns] = value.T

    return place_blocks(
        kernel,
        index,
        sums,
        pl.BlockSpec((width, 2 * columns), lambda b, i: (0, b)),
        jax.ShapeDtypeStruct((width, 8 * columns), jnp.float32),
        "place_down",
    )


def place_attn(index, sums, attn_cols):
    blocks, rows, width = sums.pieces[0].shape
    part = attn_cols // 2

    def kernel(parts, core, result, out):
        value = jnp.concatenate(parts, axis=0).astype(jnp.float32)
        place = slice(core * part, (core + 1) * part)

        @pl.when(pl.program_id(0) < 3)
        def _():
            result[0, :, place] = value.T

        @pl.when(pl.program_id(0) == 3)
        def _():
            out[place, :] = value

    return place_blocks(
        kernel,
        index,
        sums,
        [
            pl.BlockSpec((1, width, attn_cols), lambda b, i: (jnp.minimum(b, 2), 0, 0)),
            pl.BlockSpec((attn_cols, width), lambda b, i: (0, 0)),
        ],
        [
            jax.ShapeDtypeStruct((3, width, attn_cols), jnp.float32),
            jax.ShapeDtypeStruct((attn_cols, width), jnp.float32),
        ],
        "place_attn",
    )


def place_proj(index, pieces, total, extra):
    blocks, rows, width = pieces[0].shape
    here = blocks // 2
    last = total - (2 * blocks - 1) * rows

    def body(index, *refs):
        sources, result, others = refs[:8], refs[8], refs[9]
        for number, source in enumerate(sources):
            mine, peer, half = number // 4, number // 2 % 2, number % 2
            own = index[mine]
            slot = index[2] if mine == 0 else 1 - index[2]
            group = index[3] if peer == 0 else 1 - index[3]
            quarter = pl.program_id(0) ^ (own // here)
            first = quarter % 2 * here
            for column in range(4):

                @pl.when((quarter // 2 == half) & (slot * 2 + group == column))
                def _(source=source, column=column, own=own, first=first):
                    columns = slice(column * width, (column + 1) * width)
                    for k in range(here):
                        value = source[first + (k ^ (own % here))].astype(jnp.float32)
                        result[k * rows : (k + 1) * rows, columns] = value

                    @pl.when(pl.program_id(0) == 3)
                    def _():
                        others[:, columns] = value[last : last + extra]

    whole = pl.BlockSpec((blocks, rows, width), lambda b, i: (0, 0, 0))
    return pl.pallas_call(
        body,
        grid_spec=pltpu.PrefetchScalarGridSpec(
            num_scalar_prefetch=1,
            grid=(4,),
            in_specs=[whole] * 8,
            out_specs=[
                pl.BlockSpec((here * rows, 4 * width), lambda b, i: (b, 0)),
                pl.BlockSpec((extra, 4 * width), lambda b, i: (0, 0)),
            ],
        ),
        out_shape=[
            jax.ShapeDtypeStruct((total, 4 * width), jnp.float32),
            jax.ShapeDtypeStruct((extra, 4 * width), jnp.float32),
        ],
        cost_estimate=pl.CostEstimate(
            flops=0, bytes_accessed=48 * blocks * rows * width, transcendentals=0
        ),
        compiler_params=pltpu.CompilerParams(vmem_limit_bytes=26 << 20),
        name="place_proj",
    )(index, *pieces)


def rms_forward(values, gain):
    scale = lax.rsqrt(jnp.mean(values * values, axis=-1, keepdims=True) + EPSILON)
    return (values * scale * gain, scale)


def rms_backward(values, scale, gain, grad_normed):
    unit = values * scale
    grad_unit = grad_normed * gain
    grad_values = scale * (grad_unit - unit * jnp.mean(grad_unit * unit, axis=-1, keepdims=True))
    return (grad_values, jnp.sum(grad_normed * unit, axis=0))


def block_scores(
    queries, key_rows, segments, padding, query_start, row_start, query_count, seq_len
):
    query_block = lax.dynamic_slice_in_dim(queries, query_start, query_count, 0)
    scores = jnp.einsum("qhd,khd->hqk", query_block, key_rows, preferred_element_type=jnp.float32)
    query_segment = lax.dynamic_slice_in_dim(segments, query_start, query_count, 0)
    query_place = query_start + jnp.arange(query_count)
    key_place = row_start + jnp.arange(seq_len)
    allowed = (query_segment[:, None] == segments[None, :]) & (
        (padding[None, :] == 1) | (query_place[:, None] == key_place[None, :])
    )
    return (jnp.where(allowed[None], scores, MASKED), query_block, key_rows)


def attention_forward(queries, key_rows, value_rows, segments, padding, seq_len, query_count):
    group_tokens = queries.shape[0]
    per_seq = seq_len // query_count

    def one_block(number):
        query_start = number * query_count
        row_start = number // per_seq * seq_len
        scores, _, _ = block_scores(
            queries, key_rows, segments, padding, query_start, row_start, query_count, seq_len
        )
        top = jnp.max(scores, axis=-1, keepdims=True)
        expo = jnp.exp(scores - top)
        weight_sum = jnp.sum(expo, axis=-1, keepdims=True)
        probs = (expo / weight_sum).astype(jnp.bfloat16)
        mixed = jnp.einsum("hqk,khd->qhd", probs, value_rows, preferred_element_type=jnp.float32)
        return (mixed.astype(jnp.bfloat16), (top + jnp.log(weight_sum))[:, :, 0])

    mixed, log_sums = lax.map(one_block, jnp.arange(group_tokens // query_count))
    return (mixed.reshape(group_tokens, -1), log_sums)


def attention_backward(
    queries, key_rows, value_rows, segments, padding, log_sums, grad_mixed, query_count, between
):
    tokens, heads_here, head_size = queries.shape

    def one_block(carry, item, between=lambda value: value):
        grad_keys, grad_values = carry
        start, log_sum = item
        scores, query_block, key_block = block_scores(
            queries, key_rows, segments, padding, start, 0, query_count, tokens
        )
        grad_block = lax.dynamic_slice_in_dim(grad_mixed, start, query_count, 0)
        probs = jnp.exp(scores - log_sum[:, :, None])
        grad_probs = jnp.einsum(
            "qhd,khd->hqk", grad_block, value_rows, preferred_element_type=jnp.float32
        )
        mean = between(jnp.sum(grad_probs * probs, axis=-1, keepdims=True))
        grad_scores = (probs * (grad_probs - mean)).astype(jnp.bfloat16)
        grad_query = jnp.einsum(
            "hqk,khd->qhd", grad_scores, key_block, preferred_element_type=jnp.float32
        )
        key_part = jnp.einsum(
            "hqk,qhd->khd", grad_scores, query_block, preferred_element_type=jnp.float32
        )
        value_part = jnp.einsum(
            "hqk,qhd->khd",
            probs.astype(jnp.bfloat16),
            grad_block,
            preferred_element_type=jnp.float32,
        )
        return ((grad_keys + key_part, grad_values + value_part), grad_query)

    zero_grads = jnp.zeros((tokens, heads_here, head_size), jnp.float32)
    starts = query_count * jnp.arange(tokens // query_count)
    if tokens == query_count:
        (grad_keys, grad_values), grad_queries = one_block(
            (zero_grads, zero_grads), (0, log_sums[0]), between
        )
    else:
        (grad_keys, grad_values), grad_queries = lax.scan(
            one_block, (zero_grads, zero_grads), (starts, log_sums)
        )
    return (grad_queries.reshape(tokens, heads_here, head_size), grad_keys, grad_values)


def local(
    features,
    segment_ids,
    padding_mask,
    w_proj,
    proj_bias,
    gain_attn,
    w_qkv,
    w_out,
    gain_ffn,
    w_gate_up,
    w_down,
    cotangent,
):
    local_tokens = features.shape[0]
    model_width = w_proj.shape[1]
    attn_cols = w_qkv.shape[2]
    heads_here = attn_cols // HEAD_DIM
    group_tokens = local_tokens * lax.axis_size("heads")
    query_count = min(512, group_tokens)
    ff_here = w_gate_up.shape[2]
    core = lax.axis_index("rows") % 2
    steps = plane_steps()
    count = len(steps)
    blocks = 1 << count
    rows_index = lax.axis_index("rows")
    places = [block_place(steps, rows_index ^ other) for other in range(2)]
    index = jnp.stack(places + [core, lax.axis_index("heads")]).astype(jnp.int32)
    fast = lax.axis_size("heads") == 2 and blocks == 8 and attn_cols % 256 == 0 and ff_here % 128 == 0
    w_heads = jnp.transpose(w_qkv, (1, 0, 2))
    gate_flat = w_gate_up.reshape(model_width, 2 * ff_here)
    lifted = jnp.dot(features, w_proj, preferred_element_type=jnp.float32) + proj_bias
    normed, scale_attn = rms_forward(lifted, gain_attn)
    gathered = gather_group(normed.astype(jnp.bfloat16))
    both = gather_group(2 * segment_ids + padding_mask)
    segments, padding = both >> 1, both & 1
    gathered, cot_here = tie_sums(gathered, cotangent)
    grad_gathered = gather_group(cot_here)
    queries, key_rows, value_rows = (
        jnp.dot(gathered, w_heads[i], preferred_element_type=jnp.float32)
        .astype(jnp.bfloat16)
        .reshape(group_tokens, heads_here, HEAD_DIM)
        for i in range(3)
    )
    mixed, log_sums = attention_forward(
        queries, key_rows, value_rows, segments, padding, group_tokens, query_count
    )
    mixed, grad_gathered = tie_sums(mixed, grad_gathered)
    given, own = to_owners(
        lambda part: jnp.dot(part, w_out, preferred_element_type=jnp.float32), mixed
    )
    middle = lifted + own + given.astype(jnp.float32)
    normed_ffn, scale_ffn = rms_forward(middle, gain_ffn)
    gathered_ffn = gather_group(normed_ffn.astype(jnp.bfloat16))
    pair_normed = with_pair(gathered)
    pair_mixed = columns_to_pair(mixed)
    pair_cot = mixed_columns_to_pair(grad_gathered, blocks // 2)
    features_more = jnp.concatenate(
        [
            jnp.pad(features, ((0, 0), (0, 16 * blocks))),
            jnp.eye(16, w_proj.shape[0] + 16 * blocks, w_proj.shape[0], dtype=features.dtype),
        ],
        axis=0,
    )
    pair_features = with_pair(features_more)
    gathered_ffn, gate_flat, pair_normed, pair_mixed, pair_cot, pair_features = tie_sums(
        gathered_ffn, gate_flat, pair_normed, pair_mixed, pair_cot, pair_features
    )
    gate_up = jnp.dot(gathered_ffn, gate_flat, preferred_element_type=jnp.float32)
    activ, gelu_pull = jax.vjp(gelu_tanh, gate_up[:, :ff_here])
    up_part = gate_up[:, ff_here:]
    hidden = (activ * up_part).astype(jnp.bfloat16)
    grad_hidden = contract(grad_gathered, w_down, 1, 1)
    grad_gate = gelu_pull(grad_hidden * up_part)[0].astype(jnp.bfloat16)
    grad_up = (grad_hidden * activ).astype(jnp.bfloat16)
    grad_pre = jnp.concatenate([grad_gate, grad_up], axis=1)
    given, own = to_owners(lambda part: contract(part, gate_flat, 1, 1), grad_pre)
    pre_other = core_swap(jnp.where(core == 0, grad_up, grad_gate))
    pair_hidden = with_pair(hidden)
    pair_ffn = with_pair(gathered_ffn)
    pair_pre = jnp.concatenate([jnp.where(core == 0, grad_gate, grad_up), pre_other], axis=0)
    down_part = contract(pair_cot, pair_hidden, 0, 0)
    down = Summing(steps, down_part.astype(jnp.bfloat16).reshape(blocks, -1, ff_here))
    down.step()
    width = model_width // 2
    place = side(steps[0])
    gate_send, gate_keep = (
        contract(lax.dynamic_slice_in_dim(pair_ffn, which * width, width, 1), pair_pre, 0, 0)
        .astype(jnp.bfloat16)
        .reshape(blocks // 2, -1, ff_here)
        for which in (1 - place, place)
    )
    gate = Summing(steps, gate_keep, gate_send)
    gate.step()
    given, own, gate_send, gate_keep = tie_sums(down, given, own, gate_send, gate_keep)
    down.step()
    grad_normed_ffn = own + given.astype(jnp.float32)
    grad_ffn_norm, grad_gain_ffn = rms_backward(middle, scale_ffn, gain_ffn, grad_normed_ffn)
    grad_middle = cotangent.astype(jnp.float32) + grad_ffn_norm
    grad_mid_b = grad_middle.astype(jnp.bfloat16)
    grad_attn_in = gather_group(grad_mid_b)
    (grad_attn_in,) = tie_sums(gate, down, grad_attn_in)
    gate.step()
    down.step()
    grad_mixed = contract(grad_attn_in, w_out, 1, 1).astype(jnp.bfloat16)
    pair_mid = []

    def between(value):
        (value,) = tie_sums(gate, down, value)
        gate.step()
        down.step()
        pair_mid.append(with_pair(grad_attn_in))
        return value

    grad_queries, grad_keys, grad_values = attention_backward(
        queries,
        key_rows,
        value_rows,
        segments,
        padding,
        log_sums,
        grad_mixed.reshape(group_tokens, heads_here, HEAD_DIM),
        query_count,
        between,
    )
    pair_mid = pair_mid[0] if pair_mid else with_pair(grad_attn_in)
    grad_heads = [
        part.astype(jnp.bfloat16).reshape(group_tokens, attn_cols)
        for part in (grad_queries, grad_keys, grad_values)
    ]
    grad_heads = tie_sums(*grad_heads)
    grad_all = jnp.stack(grad_heads, axis=1)

    def to_normed(part):
        return sum(contract(part[:, i], w_heads[i], 1, 1) for i in range(3))

    given, own = to_owners(to_normed, grad_all)
    width = attn_cols // 2
    mine, theirs = (
        jnp.concatenate(
            [lax.dynamic_slice_in_dim(part, which * width, width, 1) for part in grad_heads],
            axis=1,
        )
        for which in (core, 1 - core)
    )
    pair_heads = jnp.concatenate([mine, core_swap(theirs)], axis=0)
    attn_part = jnp.concatenate(
        [
            contract(pair_heads, pair_normed, 0, 0).astype(jnp.bfloat16),
            contract(pair_mixed, pair_mid, 0, 0).astype(jnp.bfloat16),
        ],
        axis=0,
    )
    attn = Summing(steps, attn_part.reshape(blocks, -1, attn_part.shape[1]))
    own = attn.step(own)
    (own,) = tie_sums(gate, own)
    own = gate.step(own)
    grad_normed = own + given.astype(jnp.float32)
    grad_attn_norm, grad_gain_attn = rms_backward(lifted, scale_attn, gain_attn, grad_normed)
    grad_lifted = grad_middle + grad_attn_norm
    grad_lift_b = grad_lifted.astype(jnp.bfloat16)
    sums = jnp.stack([jnp.sum(grad_lifted, axis=0), grad_gain_attn, grad_gain_ffn])
    sums = jnp.pad(sums, ((0, 16 - sums.shape[0]), (0, 0))).astype(jnp.bfloat16)
    lift_more = jnp.concatenate([grad_lift_b, sums], axis=0)
    proj_part = contract(pair_features, columns_to_pair(lift_more), 0, 0).astype(jnp.bfloat16)
    proj = over_peers(steps, proj_part.reshape(blocks, -1, proj_part.shape[1]))
    proj.step()
    sent = advance(down, proj.sent)
    sent = advance(attn, sent)
    sent = advance(gate, sent)
    hidden, grad_lift_b = lax.optimization_barrier((sent, hidden, grad_lift_b))[1:]
    layer_out = jnp.dot(hidden, w_down, preferred_element_type=jnp.float32).astype(jnp.bfloat16)
    layer_out = scatter_group(layer_out)
    grad_features = contract(grad_lift_b, w_proj, 1, 1)
    sent = advance(proj, grad_features)
    while down.done < 2 * count:
        sent = advance(down, sent)
    while attn.done < count:
        sent = advance(attn, sent)
    sent = advance(gate, sent)
    while proj.done < count:
        sent = advance(proj, sent)
    sent = advance(attn, sent)
    layer_out, sent = lax.optimization_barrier((layer_out, sent))
    layer_out = middle + layer_out
    down.update(lax.optimization_barrier((down.last(), sent, layer_out))[0])
    while down.done < 2 * count:
        down.step()
    down.cores()
    if fast:
        grad_down = place_down(index, down)
        sent = grad_down
    sent = advance(proj, sent)
    sent = advance(attn, sent)
    gate.update(lax.optimization_barrier((gate.last(), sent))[0])
    while gate.done < 2 * count:
        gate.step()
    gate.cores()
    if fast:
        grad_gate_up = place_gate_up(index, gate)
        sent = grad_gate_up
    sent = advance(proj, sent)
    while proj.done < 2 * count - 1:
        sent = advance(proj, sent)
    near = [peer_swap(proj.pieces[0])] if fast else []
    while attn.done < 2 * count:
        sent = advance(attn, sent)
    last, near = lax.optimization_barrier((proj.last(), near))
    proj.update(last)
    near += [peer_swap(proj.pieces[1])] if fast else []
    sent = advance(proj, sent)
    low, high = proj.pieces
    attn.update(lax.optimization_barrier((attn.last(), sent))[0])
    attn.cores()
    attn.others, near = lax.optimization_barrier((attn.others, near))
    if fast:
        pieces = [low, high, jnp.concatenate(near, axis=0), peer_swap(high)]
        grad_qkv, grad_out = place_attn(index, attn, attn_cols)
        grad_qkv, pieces[3] = lax.optimization_barrier((grad_qkv, pieces[3]))
        pieces += [core_swap(piece) for piece in pieces]
        grad_qkv = jnp.transpose(grad_qkv, (1, 0, 2))
        grad_proj, sums = place_proj(index, pieces, w_proj.shape[0], 16)
    else:
        proj.cores()
        half = attn_cols // 2
        pair = two_cores(gate, places, 1, (model_width, 1, ff_here))
        grad_gate_up = pair.astype(jnp.float32)
        pair = two_cores(down, places, 0).reshape(2, blocks // 2, -1, ff_here)
        grad_down = jnp.moveaxis(pair, 0, 1).reshape(model_width, ff_here).T.astype(jnp.float32)
        pair = two_cores(proj, places, 1)
        pair = pair.reshape(pair.shape[0], 2, 1, -1)
        pair = lax.all_gather(pair, "heads", axis=2, tiled=True).astype(jnp.float32)
        pair = pair.reshape(pair.shape[0], -1)
        grad_proj, sums = pair[: w_proj.shape[0]], pair[w_proj.shape[0] :]
        pair = two_cores(attn, places, 0).reshape(2, 4, half, model_width)
        pair = jnp.moveaxis(pair, 0, 1).reshape(4, attn_cols, model_width).astype(jnp.float32)
        grad_qkv, grad_out = jnp.transpose(pair[:3], (2, 0, 1)), pair[3]
    return (
        layer_out.astype(jnp.bfloat16),
        grad_features,
        grad_proj,
        sums[0],
        sums[1],
        grad_qkv,
        grad_out,
        sums[2],
        grad_gate_up,
        grad_down,
    )


def solution(mesh):
    in_specs = (
        P(("rows", "heads"), None),
        P(("rows", "heads")),
        P(("rows", "heads")),
        P(),
        P(),
        P(),
        P(None, None, "heads"),
        P("heads", None),
        P(),
        P(None, None, "heads"),
        P("heads", None),
        P(("rows", "heads"), None),
    )
    out_specs = (
        P(("rows", "heads"), None),
        P(("rows", "heads"), None),
        P(),
        P(),
        P(),
        P(None, None, "heads"),
        P("heads", None),
        P(),
        P(None, None, "heads"),
        P("heads", None),
    )
    return jax.shard_map(local, mesh=mesh, in_specs=in_specs, out_specs=out_specs, check_vma=False)
```

```python
import jax
import jax.numpy as jnp
from jax import lax
from jax.experimental import pallas as pl
from jax.experimental.pallas import tpu as pltpu
from jax.sharding import PartitionSpec as P

HEAD_DIM = 64


EPSILON = 1e-06
MASKED = -1000000000.0


def gelu_tanh(values):
    return jax.nn.gelu(values, approximate=True)


def contract(left, right, left_dim, right_dim):
    return lax.dot_general(
        left, right, (((left_dim,), (right_dim,)), ((), ())), preferred_element_type=jnp.float32
    )


def swap_rows(value, masks):
    count = lax.axis_size("rows")
    return lax.ppermute(value, "rows", [(r, r ^ masks[r % 2]) for r in range(count)])


def core_swap(value):
    return swap_rows(value, (1, 1))


def peer_swap(value):
    return lax.ppermute(value, "heads", [(0, 1), (1, 0)])


def gather_group(value):
    if lax.axis_size("heads") == 2:
        return jnp.concatenate([value, peer_swap(value)], axis=0)
    return lax.all_gather(value, "heads", axis=0, tiled=True)


def scatter_group(value):
    if lax.axis_size("heads") == 2:
        mine = value.shape[0] // 2
        return value[:mine].astype(jnp.float32) + peer_swap(value[mine:]).astype(jnp.float32)
    return lax.psum_scatter(value, "heads", scatter_dimension=0, tiled=True).astype(jnp.float32)


def to_owners(product, left):
    if lax.axis_size("heads") == 2:
        mine = left.shape[0] // 2
        given = peer_swap(product(left[mine:]).astype(jnp.bfloat16))
        return (given, product(left[:mine]))
    given = lax.psum_scatter(
        product(left).astype(jnp.bfloat16), "heads", scatter_dimension=0, tiled=True
    )
    return (given, jnp.zeros((), jnp.float32))


def columns_to_group(value):
    size = lax.axis_size("heads")
    if size == 2:
        width = value.shape[1] // 2
        place = lax.axis_index("heads")
        mine = lax.dynamic_slice_in_dim(value, place * width, width, 1)
        theirs = lax.dynamic_slice_in_dim(value, (1 - place) * width, width, 1)
        return jnp.concatenate([mine, peer_swap(theirs)], axis=0)
    return lax.all_to_all(value, "heads", 1, 0, tiled=True)


def columns_to_pair(value, axis=1):
    width = value.shape[axis] // 2
    core = lax.axis_index("rows") % 2
    mine = lax.dynamic_slice_in_dim(value, core * width, width, axis)
    theirs = lax.dynamic_slice_in_dim(value, (1 - core) * width, width, axis)
    return jnp.concatenate([mine, core_swap(theirs)], axis=0)


def mixed_columns_to_pair(value, pieces):
    width = value.shape[1] // (2 * pieces)
    core = lax.axis_index("rows") % 2
    mine, theirs = (
        jnp.concatenate(
            [
                lax.dynamic_slice_in_dim(value, (2 * k + which) * width, width, 1)
                for k in range(pieces)
            ],
            axis=1,
        )
        for which in (core, 1 - core)
    )
    return jnp.concatenate([mine, core_swap(theirs)], axis=0)


def with_pair(value):
    return jnp.concatenate([value, core_swap(value)], axis=0)


def plane_steps(same=False):
    bits = (lax.axis_size("rows") // 2).bit_length() - 1
    low = bits // 2

    def line(first, count):
        return [
            ((1 << first, (first,) if count == 1 else (first, first + 1)))
        ] if count == 1 else [
            (1 << first, (first, first + 1)),
            (3 << first, (first + 1,)),
        ]

    near = line(1, low)
    far = line(1 + low, bits - low)

    def weave(one, two):
        one, two, order = list(one), list(two), []
        while one or two:
            if one:
                order.append(one.pop(0))
            if two:
                order.append(two.pop(0))
        return order

    first = weave(near, far)
    return list(zip(first, first if same else weave(far, near)))


def side(step, index=None):
    index = lax.axis_index("rows") if index is None else index

    def parity(places):
        total = jnp.zeros((), jnp.int32)
        for place in places:
            total = total ^ ((index >> place) & 1)
        return total

    return jnp.where(index % 2 == 0, parity(step[0][1]), parity(step[1][1]))


def block_place(steps, index):
    place = jnp.zeros((), jnp.int32)
    for step in steps:
        place = place * 2 + side(step, index)
    return place


class Summing:
    def __init__(self, steps, value, send=None):
        self.steps, self.done = steps, 0
        self.sides = [side(step) for step in steps]
        self.size = value.shape[0] if send is None else 2 * value.shape[0]
        self.terms, self.send = [(value, jnp.zeros((), jnp.int32))], send
        self.pieces, self.others, self.sent = [], [], None

    def last(self):
        return self.pieces[-1] if self.pieces else self.terms[-1][0]

    def update(self, value):
        if self.pieces:
            self.pieces = self.pieces[:-1] + [value]
        else:
            self.terms = self.terms[:-1] + [(value, self.terms[-1][1])]

    def masks(self, number):
        step = self.steps[number]
        return (step[0][0], step[1][0])

    def part(self, offset, size):
        total = sum(
            lax.dynamic_slice_in_dim(term, base + offset, size, 0).astype(jnp.float32)
            for term, base in self.terms
        )
        return total.astype(jnp.bfloat16)

    def prepare(self):
        count = len(self.steps)
        if self.done < count:
            place, half = self.sides[self.done], self.size // 2
            if self.send is None:
                self.sent = self.part((1 - place) * half, half)
                self.terms = [(term, base + place * half) for term, base in self.terms]
            else:
                self.sent, self.send = self.send, None
            self.size = half
        else:
            if self.done == count:
                self.pieces, self.terms = [self.part(0, self.size)], []
            else:
                self.pieces = [jnp.concatenate(self.pieces, axis=0)]
            self.sent = self.pieces[0]

    def issue(self):
        count = len(self.steps)
        if self.done < count:
            got = swap_rows(self.sent, self.masks(self.done))
            self.terms = self.terms + [(got, jnp.zeros((), jnp.int32))]
        else:
            self.pieces = [self.sent, swap_rows(self.sent, self.masks(2 * count - 1 - self.done))]
        self.done += 1

    def step(self, *values):
        self.prepare()
        if values:
            self.sent, values = lax.optimization_barrier((self.sent, values))
        self.issue()
        return values if len(values) != 1 else values[0]

    def cores(self):
        self.others = [core_swap(piece) for piece in self.pieces]


def over_peers(steps, value):
    size = lax.axis_size("heads")
    width = value.shape[2] // size
    if size != 2:
        value = lax.psum_scatter(value, "heads", scatter_dimension=2, tiled=True)
        return Summing(steps, value)
    mine, theirs = (
        lax.dynamic_slice_in_dim(value, which * width, width, 2)
        for which in (lax.axis_index("heads"), 1 - lax.axis_index("heads"))
    )
    half = value.shape[0] // 2
    place = side(steps[0])

    def cut(part, which):
        return lax.dynamic_slice_in_dim(part, which * half, half, 0)

    got_send = peer_swap(cut(theirs, 1 - place))
    send = cut(mine, 1 - place).astype(jnp.float32) + got_send.astype(jnp.float32)
    got_keep = peer_swap(cut(theirs, place))
    total = Summing(steps, cut(mine, place), send.astype(jnp.bfloat16))
    total.terms.append((got_keep, jnp.zeros((), jnp.int32)))
    return total


def tie_sums(*sums_and_others):
    sums = [item for item in sums_and_others if isinstance(item, Summing)]
    others = [item for item in sums_and_others if not isinstance(item, Summing)]
    values, others = lax.optimization_barrier(([item.last() for item in sums], others))
    for item, value in zip(sums, values):
        item.update(value)
    return others


def advance(item, *earlier):
    item.update(lax.optimization_barrier((item.last(), earlier))[0])
    item.step()
    return item.sent


def ordered(pieces, place):
    value = jnp.concatenate(pieces, axis=0)
    return jnp.concatenate(
        [
            lax.dynamic_slice_in_dim(value, place ^ block, 1, 0)
            for block in range(value.shape[0])
        ],
        axis=0,
    ).reshape(-1, value.shape[2])


def two_cores(sums, places, axis, reshape=None):
    mine, theirs = ordered(sums.pieces, places[0]), ordered(sums.others, places[1])
    if reshape is not None:
        mine, theirs = (value.reshape(reshape) for value in (mine, theirs))
    return jnp.where(
        lax.axis_index("rows") % 2 == 0,
        jnp.concatenate([mine, theirs], axis=axis),
        jnp.concatenate([theirs, mine], axis=axis),
    )


def place_blocks(kernel, index, sums, out_specs, out_shape, name):
    pieces = sums.pieces + sums.others
    blocks, rows, width = pieces[0].shape
    here = blocks // 2

    def body(index, *refs):
        sources, results = refs[:4], refs[4:]
        for number, source in enumerate(sources):
            own = index[number // 2]
            slot = index[2] if number < 2 else 1 - index[2]
            quarter = pl.program_id(0) ^ (own // here)
            inside = quarter // 2 == number % 2
            first = quarter % 2 * here
            for core in range(2):

                @pl.when(inside & (slot == core))
                def _(source=source, core=core, own=own, first=first):
                    parts = [source[first + (k ^ (own % here))] for k in range(here)]
                    kernel(parts, core, *results)

    whole = pl.BlockSpec((blocks, rows, width), lambda b, i: (0, 0, 0))
    return pl.pallas_call(
        body,
        grid_spec=pltpu.PrefetchScalarGridSpec(
            num_scalar_prefetch=1, grid=(4,), in_specs=[whole] * 4, out_specs=out_specs
        ),
        out_shape=out_shape,
        cost_estimate=pl.CostEstimate(
            flops=0, bytes_accessed=24 * blocks * rows * width, transcendentals=0
        ),
        compiler_params=pltpu.CompilerParams(vmem_limit_bytes=26 << 20),
        name=name,
    )(index, *pieces)


def place_gate_up(index, sums):
    blocks, rows, width = sums.pieces[0].shape

    def kernel(parts, core, result):
        for k, part in enumerate(parts):
            result[k * rows : (k + 1) * rows, core, :] = part.astype(jnp.float32)

    return place_blocks(
        kernel,
        index,
        sums,
        pl.BlockSpec((blocks // 2 * rows, 2, width), lambda b, i: (b, 0, 0)),
        jax.ShapeDtypeStruct((2 * blocks * rows, 2, width), jnp.float32),
        "place_gate_up",
    )


def place_down(index, sums):
    blocks, rows, width = sums.pieces[0].shape
    columns = blocks // 2 * rows

    def kernel(parts, core, result):
        value = jnp.concatenate(parts, axis=0).astype(jnp.float32)
        result[:, core * columns : (core + 1) * columns] = value.T

    return place_blocks(
        kernel,
        index,
        sums,
        pl.BlockSpec((width, 2 * columns), lambda b, i: (0, b)),
        jax.ShapeDtypeStruct((width, 8 * columns), jnp.float32),
        "place_down",
    )


def place_attn(index, sums, attn_cols):
    blocks, rows, width = sums.pieces[0].shape
    part = attn_cols // 2

    def kernel(parts, core, result, out):
        value = jnp.concatenate(parts, axis=0).astype(jnp.float32)
        place = slice(core * part, (core + 1) * part)

        @pl.when(pl.program_id(0) < 3)
        def _():
            result[0, :, place] = value.T

        @pl.when(pl.program_id(0) == 3)
        def _():
            out[place, :] = value

    return place_blocks(
        kernel,
        index,
        sums,
        [
            pl.BlockSpec((1, width, attn_cols), lambda b, i: (jnp.minimum(b, 2), 0, 0)),
            pl.BlockSpec((attn_cols, width), lambda b, i: (0, 0)),
        ],
        [
            jax.ShapeDtypeStruct((3, width, attn_cols), jnp.float32),
            jax.ShapeDtypeStruct((attn_cols, width), jnp.float32),
        ],
        "place_attn",
    )


def place_proj(index, pieces, total, extra):
    blocks, rows, width = pieces[0].shape
    here = blocks // 2
    last = total - (2 * blocks - 1) * rows

    def body(index, *refs):
        sources, result, others = refs[:8], refs[8], refs[9]
        for number, source in enumerate(sources):
            mine, peer, half = number // 4, number // 2 % 2, number % 2
            own = index[mine]
            slot = index[2] if mine == 0 else 1 - index[2]
            group = index[3] if peer == 0 else 1 - index[3]
            quarter = pl.program_id(0) ^ (own // here)
            first = quarter % 2 * here
            for column in range(4):

                @pl.when((quarter // 2 == half) & (slot * 2 + group == column))
                def _(source=source, column=column, own=own, first=first):
                    columns = slice(column * width, (column + 1) * width)
                    for k in range(here):
                        value = source[first + (k ^ (own % here))].astype(jnp.float32)
                        result[k * rows : (k + 1) * rows, columns] = value

                    @pl.when(pl.program_id(0) == 3)
                    def _():
                        others[:, columns] = value[last : last + extra]

    whole = pl.BlockSpec((blocks, rows, width), lambda b, i: (0, 0, 0))
    return pl.pallas_call(
        body,
        grid_spec=pltpu.PrefetchScalarGridSpec(
            num_scalar_prefetch=1,
            grid=(4,),
            in_specs=[whole] * 8,
            out_specs=[
                pl.BlockSpec((here * rows, 4 * width), lambda b, i: (b, 0)),
                pl.BlockSpec((extra, 4 * width), lambda b, i: (0, 0)),
            ],
        ),
        out_shape=[
            jax.ShapeDtypeStruct((total, 4 * width), jnp.float32),
            jax.ShapeDtypeStruct((extra, 4 * width), jnp.float32),
        ],
        cost_estimate=pl.CostEstimate(
            flops=0, bytes_accessed=48 * blocks * rows * width, transcendentals=0
        ),
        compiler_params=pltpu.CompilerParams(vmem_limit_bytes=26 << 20),
        name="place_proj",
    )(index, *pieces)


def rms_forward(values, gain):
    scale = lax.rsqrt(jnp.mean(values * values, axis=-1, keepdims=True) + EPSILON)
    return (values * scale * gain, scale)


def rms_backward(values, scale, gain, grad_normed):
    unit = values * scale
    grad_unit = grad_normed * gain
    grad_values = scale * (grad_unit - unit * jnp.mean(grad_unit * unit, axis=-1, keepdims=True))
    return (grad_values, jnp.sum(grad_normed * unit, axis=0))


def block_scores(
    queries, key_rows, segments, padding, query_start, row_start, query_count, seq_len
):
    query_block = lax.dynamic_slice_in_dim(queries, query_start, query_count, 0)
    scores = jnp.einsum("qhd,khd->hqk", query_block, key_rows, preferred_element_type=jnp.float32)
    query_segment = lax.dynamic_slice_in_dim(segments, query_start, query_count, 0)
    query_place = query_start + jnp.arange(query_count)
    key_place = row_start + jnp.arange(seq_len)
    allowed = (query_segment[:, None] == segments[None, :]) & (
        (padding[None, :] == 1) | (query_place[:, None] == key_place[None, :])
    )
    return (jnp.where(allowed[None], scores, MASKED), query_block, key_rows)


def attention_forward(queries, key_rows, value_rows, segments, padding, seq_len, query_count):
    group_tokens = queries.shape[0]
    per_seq = seq_len // query_count

    def one_block(number):
        query_start = number * query_count
        row_start = number // per_seq * seq_len
        scores, _, _ = block_scores(
            queries, key_rows, segments, padding, query_start, row_start, query_count, seq_len
        )
        top = jnp.max(scores, axis=-1, keepdims=True)
        expo = jnp.exp(scores - top)
        weight_sum = jnp.sum(expo, axis=-1, keepdims=True)
        probs = (expo / weight_sum).astype(jnp.bfloat16)
        mixed = jnp.einsum("hqk,khd->qhd", probs, value_rows, preferred_element_type=jnp.float32)
        return (mixed.astype(jnp.bfloat16), (top + jnp.log(weight_sum))[:, :, 0])

    mixed, log_sums = lax.map(one_block, jnp.arange(group_tokens // query_count))
    return (mixed.reshape(group_tokens, -1), log_sums)


def attention_backward(
    queries, key_rows, value_rows, segments, padding, log_sums, grad_mixed, query_count, between
):
    tokens, heads_here, head_size = queries.shape

    def one_block(carry, item, between=lambda value: value):
        grad_keys, grad_values = carry
        start, log_sum = item
        scores, query_block, key_block = block_scores(
            queries, key_rows, segments, padding, start, 0, query_count, tokens
        )
        grad_block = lax.dynamic_slice_in_dim(grad_mixed, start, query_count, 0)
        probs = jnp.exp(scores - log_sum[:, :, None])
        grad_probs = jnp.einsum(
            "qhd,khd->hqk", grad_block, value_rows, preferred_element_type=jnp.float32
        )
        mean = between(jnp.sum(grad_probs * probs, axis=-1, keepdims=True))
        grad_scores = (probs * (grad_probs - mean)).astype(jnp.bfloat16)
        grad_query = jnp.einsum(
            "hqk,khd->qhd", grad_scores, key_block, preferred_element_type=jnp.float32
        )
        key_part = jnp.einsum(
            "hqk,qhd->khd", grad_scores, query_block, preferred_element_type=jnp.float32
        )
        value_part = jnp.einsum(
            "hqk,qhd->khd",
            probs.astype(jnp.bfloat16),
            grad_block,
            preferred_element_type=jnp.float32,
        )
        return ((grad_keys + key_part, grad_values + value_part), grad_query)

    zero_grads = jnp.zeros((tokens, heads_here, head_size), jnp.float32)
    starts = query_count * jnp.arange(tokens // query_count)
    if tokens == query_count:
        (grad_keys, grad_values), grad_queries = one_block(
            (zero_grads, zero_grads), (0, log_sums[0]), between
        )
    else:
        (grad_keys, grad_values), grad_queries = lax.scan(
            one_block, (zero_grads, zero_grads), (starts, log_sums)
        )
    return (grad_queries.reshape(tokens, heads_here, head_size), grad_keys, grad_values)


def local(
    features,
    segment_ids,
    padding_mask,
    w_proj,
    proj_bias,
    gain_attn,
    w_qkv,
    w_out,
    gain_ffn,
    w_gate_up,
    w_down,
    cotangent,
):
    local_tokens = features.shape[0]
    model_width = w_proj.shape[1]
    attn_cols = w_qkv.shape[2]
    heads_here = attn_cols // HEAD_DIM
    group_tokens = local_tokens * lax.axis_size("heads")
    query_count = min(512, group_tokens)
    ff_here = w_gate_up.shape[2]
    core = lax.axis_index("rows") % 2
    steps = plane_steps()
    count = len(steps)
    blocks = 1 << count
    rows_index = lax.axis_index("rows")
    places = [block_place(steps, rows_index ^ other) for other in range(2)]
    index = jnp.stack(places + [core, lax.axis_index("heads")]).astype(jnp.int32)
    fast = lax.axis_size("heads") == 2 and blocks == 8 and attn_cols % 256 == 0 and ff_here % 128 == 0
    w_heads = jnp.transpose(w_qkv, (1, 0, 2))
    gate_flat = w_gate_up.reshape(model_width, 2 * ff_here)
    lifted = jnp.dot(features, w_proj, preferred_element_type=jnp.float32) + proj_bias
    normed, scale_attn = rms_forward(lifted, gain_attn)
    gathered = gather_group(normed.astype(jnp.bfloat16))
    both = gather_group(2 * segment_ids + padding_mask)
    segments, padding = both >> 1, both & 1
    gathered, cot_here = tie_sums(gathered, cotangent)
    grad_gathered = gather_group(cot_here)
    queries, key_rows, value_rows = (
        jnp.dot(gathered, w_heads[i], preferred_element_type=jnp.float32)
        .astype(jnp.bfloat16)
        .reshape(group_tokens, heads_here, HEAD_DIM)
        for i in range(3)
    )
    mixed, log_sums = attention_forward(
        queries, key_rows, value_rows, segments, padding, group_tokens, query_count
    )
    mixed, grad_gathered = tie_sums(mixed, grad_gathered)
    given, own = to_owners(
        lambda part: jnp.dot(part, w_out, preferred_element_type=jnp.float32), mixed
    )
    middle = lifted + own + given.astype(jnp.float32)
    normed_ffn, scale_ffn = rms_forward(middle, gain_ffn)
    gathered_ffn = gather_group(normed_ffn.astype(jnp.bfloat16))
    pair_normed = with_pair(gathered)
    pair_mixed = columns_to_pair(mixed)
    pair_cot = mixed_columns_to_pair(grad_gathered, blocks // 2)
    features_more = jnp.concatenate(
        [
            jnp.pad(features, ((0, 0), (0, 16 * blocks))),
            jnp.eye(16, w_proj.shape[0] + 16 * blocks, w_proj.shape[0], dtype=features.dtype),
        ],
        axis=0,
    )
    pair_features = with_pair(features_more)
    gathered_ffn, gate_flat, pair_normed, pair_mixed, pair_cot, pair_features = tie_sums(
        gathered_ffn, gate_flat, pair_normed, pair_mixed, pair_cot, pair_features
    )
    gate_up = jnp.dot(gathered_ffn, gate_flat, preferred_element_type=jnp.float32)
    activ, gelu_pull = jax.vjp(gelu_tanh, gate_up[:, :ff_here])
    up_part = gate_up[:, ff_here:]
    hidden = (activ * up_part).astype(jnp.bfloat16)
    grad_hidden = contract(grad_gathered, w_down, 1, 1)
    grad_gate = gelu_pull(grad_hidden * up_part)[0].astype(jnp.bfloat16)
    grad_up = (grad_hidden * activ).astype(jnp.bfloat16)
    grad_pre = jnp.concatenate([grad_gate, grad_up], axis=1)
    given, own = to_owners(lambda part: contract(part, gate_flat, 1, 1), grad_pre)
    pre_other = core_swap(jnp.where(core == 0, grad_up, grad_gate))
    pair_hidden = with_pair(hidden)
    pair_ffn = with_pair(gathered_ffn)
    pair_pre = jnp.concatenate([jnp.where(core == 0, grad_gate, grad_up), pre_other], axis=0)
    down_part = contract(pair_cot, pair_hidden, 0, 0)
    down = Summing(steps, down_part.astype(jnp.bfloat16).reshape(blocks, -1, ff_here))
    down.step()
    width = model_width // 2
    place = side(steps[0])
    gate_send, gate_keep = (
        contract(lax.dynamic_slice_in_dim(pair_ffn, which * width, width, 1), pair_pre, 0, 0)
        .astype(jnp.bfloat16)
        .reshape(blocks // 2, -1, ff_here)
        for which in (1 - place, place)
    )
    gate = Summing(steps, gate_keep, gate_send)
    gate.step()
    given, own, gate_send, gate_keep = tie_sums(down, given, own, gate_send, gate_keep)
    down.step()
    grad_normed_ffn = own + given.astype(jnp.float32)
    grad_ffn_norm, grad_gain_ffn = rms_backward(middle, scale_ffn, gain_ffn, grad_normed_ffn)
    grad_middle = cotangent.astype(jnp.float32) + grad_ffn_norm
    grad_mid_b = grad_middle.astype(jnp.bfloat16)
    grad_attn_in = gather_group(grad_mid_b)
    (grad_attn_in,) = tie_sums(gate, down, grad_attn_in)
    gate.step()
    down.step()
    grad_mixed = contract(grad_attn_in, w_out, 1, 1).astype(jnp.bfloat16)
    pair_mid = []

    def between(value):
        (value,) = tie_sums(gate, down, value)
        gate.step()
        down.step()
        pair_mid.append(with_pair(grad_attn_in))
        return value

    grad_queries, grad_keys, grad_values = attention_backward(
        queries,
        key_rows,
        value_rows,
        segments,
        padding,
        log_sums,
        grad_mixed.reshape(group_tokens, heads_here, HEAD_DIM),
        query_count,
        between,
    )
    pair_mid = pair_mid[0] if pair_mid else with_pair(grad_attn_in)
    grad_heads = [
        part.astype(jnp.bfloat16).reshape(group_tokens, attn_cols)
        for part in (grad_queries, grad_keys, grad_values)
    ]
    grad_heads = tie_sums(*grad_heads)
    grad_all = jnp.stack(grad_heads, axis=1)

    def to_normed(part):
        return sum(contract(part[:, i], w_heads[i], 1, 1) for i in range(3))

    given, own = to_owners(to_normed, grad_all)
    width = attn_cols // 2
    mine, theirs = (
        jnp.concatenate(
            [lax.dynamic_slice_in_dim(part, which * width, width, 1) for part in grad_heads],
            axis=1,
        )
        for which in (core, 1 - core)
    )
    pair_heads = jnp.concatenate([mine, core_swap(theirs)], axis=0)
    attn_part = jnp.concatenate(
        [
            contract(pair_heads, pair_normed, 0, 0).astype(jnp.bfloat16),
            contract(pair_mixed, pair_mid, 0, 0).astype(jnp.bfloat16),
        ],
        axis=0,
    )
    attn = Summing(steps, attn_part.reshape(blocks, -1, attn_part.shape[1]))
    own = attn.step(own)
    (own,) = tie_sums(gate, own)
    own = gate.step(own)
    grad_normed = own + given.astype(jnp.float32)
    grad_attn_norm, grad_gain_attn = rms_backward(lifted, scale_attn, gain_attn, grad_normed)
    grad_lifted = grad_middle + grad_attn_norm
    grad_lift_b = grad_lifted.astype(jnp.bfloat16)
    sums = jnp.stack([jnp.sum(grad_lifted, axis=0), grad_gain_attn, grad_gain_ffn])
    sums = jnp.pad(sums, ((0, 16 - sums.shape[0]), (0, 0))).astype(jnp.bfloat16)
    lift_more = jnp.concatenate([grad_lift_b, sums], axis=0)
    proj_part = contract(pair_features, columns_to_pair(lift_more), 0, 0).astype(jnp.bfloat16)
    proj = over_peers(steps, proj_part.reshape(blocks, -1, proj_part.shape[1]))
    proj.step()
    sent = advance(down, proj.sent)
    sent = advance(attn, sent)
    sent = advance(gate, sent)
    hidden, grad_lift_b = lax.optimization_barrier((sent, hidden, grad_lift_b))[1:]
    layer_out, own = to_owners(
        lambda part: jnp.dot(part, w_down, preferred_element_type=jnp.float32), hidden
    )
    layer_out = own + layer_out.astype(jnp.float32)
    grad_features = contract(grad_lift_b, w_proj, 1, 1)
    sent = advance(proj, grad_features)
    while down.done < 2 * count:
        sent = advance(down, sent)
    while attn.done < count:
        sent = advance(attn, sent)
    sent = advance(gate, sent)
    while proj.done < count:
        sent = advance(proj, sent)
    sent = advance(attn, sent)
    layer_out, sent = lax.optimization_barrier((layer_out, sent))
    layer_out = middle + layer_out
    down.update(lax.optimization_barrier((down.last(), sent, layer_out))[0])
    while down.done < 2 * count:
        down.step()
    down.cores()
    if fast:
        grad_down = place_down(index, down)
        sent = grad_down
    sent = advance(proj, sent)
    sent = advance(attn, sent)
    gate.update(lax.optimization_barrier((gate.last(), sent))[0])
    while gate.done < 2 * count:
        gate.step()
    gate.cores()
    if fast:
        grad_gate_up = place_gate_up(index, gate)
        sent = grad_gate_up
    sent = advance(proj, sent)
    while proj.done < 2 * count - 1:
        sent = advance(proj, sent)
    near = [peer_swap(proj.pieces[0])] if fast else []
    while attn.done < 2 * count:
        sent = advance(attn, sent)
    last, near = lax.optimization_barrier((proj.last(), near))
    proj.update(last)
    near += [peer_swap(proj.pieces[1])] if fast else []
    sent = advance(proj, sent)
    low, high = proj.pieces
    attn.update(lax.optimization_barrier((attn.last(), sent))[0])
    attn.cores()
    attn.others, near = lax.optimization_barrier((attn.others, near))
    if fast:
        pieces = [low, high, jnp.concatenate(near, axis=0), peer_swap(high)]
        grad_qkv, grad_out = place_attn(index, attn, attn_cols)
        grad_qkv, pieces[3] = lax.optimization_barrier((grad_qkv, pieces[3]))
        pieces += [core_swap(piece) for piece in pieces]
        grad_qkv = jnp.transpose(grad_qkv, (1, 0, 2))
        grad_proj, sums = place_proj(index, pieces, w_proj.shape[0], 16)
    else:
        proj.cores()
        half = attn_cols // 2
        pair = two_cores(gate, places, 1, (model_width, 1, ff_here))
        grad_gate_up = pair.astype(jnp.float32)
        pair = two_cores(down, places, 0).reshape(2, blocks // 2, -1, ff_here)
        grad_down = jnp.moveaxis(pair, 0, 1).reshape(model_width, ff_here).T.astype(jnp.float32)
        pair = two_cores(proj, places, 1)
        pair = pair.reshape(pair.shape[0], 2, 1, -1)
        pair = lax.all_gather(pair, "heads", axis=2, tiled=True).astype(jnp.float32)
        pair = pair.reshape(pair.shape[0], -1)
        grad_proj, sums = pair[: w_proj.shape[0]], pair[w_proj.shape[0] :]
        pair = two_cores(attn, places, 0).reshape(2, 4, half, model_width)
        pair = jnp.moveaxis(pair, 0, 1).reshape(4, attn_cols, model_width).astype(jnp.float32)
        grad_qkv, grad_out = jnp.transpose(pair[:3], (2, 0, 1)), pair[3]
    return (
        layer_out.astype(jnp.bfloat16),
        grad_features,
        grad_proj,
        sums[0],
        sums[1],
        grad_qkv,
        grad_out,
        sums[2],
        grad_gate_up,
        grad_down,
    )


def solution(mesh):
    in_specs = (
        P(("rows", "heads"), None),
        P(("rows", "heads")),
        P(("rows", "heads")),
        P(),
        P(),
        P(),
        P(None, None, "heads"),
        P("heads", None),
        P(),
        P(None, None, "heads"),
        P("heads", None),
        P(("rows", "heads"), None),
    )
    out_specs = (
        P(("rows", "heads"), None),
        P(("rows", "heads"), None),
        P(),
        P(),
        P(),
        P(None, None, "heads"),
        P("heads", None),
        P(),
        P(None, None, "heads"),
        P("heads", None),
    )
    return jax.shard_map(local, mesh=mesh, in_specs=in_specs, out_specs=out_specs, check_vma=False)
```
